512 devices in a mesh: seq: 64 (over x, z), tensor: 8 (over y, core).
Axes of the slice: x: 4, y: 4, z: 16, core: 2. Of those that a mesh axis runs over, the one named last changes fastest.
Arguments:
- layer_entry_vectors: bfloat16 [1024, 4, 2048], P('seq'), may hold values from -6 to 6
- tally_of_tokens: int32 [1024], P('seq'), may hold values from 1 to 4, as said below
- prior_slot_lookup: int32 [1024], P('seq'), may hold values from 0 to 1023, as said below
- memory_matrices: float32 [1024, 32, 4096], P('seq', 'tensor'), may hold values from -6 to 6
- previous_standardized_entries: float32 [1024, 2048], P('seq'), may hold values from -6 to 6
- entry_standardize_scale: float32 [2048], replicated, may hold values from 0.1 to 1.9
- blend_coefficients: float32 [4, 2048], replicated, may hold values from 0 to 1
- acceptance_projection_matrix: bfloat16 [2048, 2048], P(None, 'tensor'), may hold values from -0.125 to 0.125
- lookup_projection_matrix: bfloat16 [2048, 2048], P(None, 'tensor'), may hold values from -0.125 to 0.125
- payload_projection_matrix: bfloat16 [2048, 2048], P(None, 'tensor'), may hold values from -0.125 to 0.125
- forget_map_left_matrix: bfloat16 [2048, 64], P('tensor'), may hold values from -0.125 to 0.125
- forget_map_right_matrix: bfloat16 [64, 2048], P(None, 'tensor'), may hold values from -0.75 to 0.75
- feature_forget_logloglevel: float32 [2048], P('tensor'), may hold values from -6 to 1
- present_token_boost: float32 [2048], P('tensor'), may hold values from -3 to 3
- team_standardize_scale: float32 [2048], P('tensor'), may hold values from 0.1 to 1.9
- final_projection_matrix: bfloat16 [2048, 2048], P('tensor'), may hold values from -0.125 to 0.125
Outputs:
- mixed: bfloat16 [1024, 4, 2048], P('seq')
- new_states: float32 [1024, 32, 4096], P('seq', 'tensor')
- new_shifts: float32 [1024, 2048], P('seq')
The draws below stay inside these ranges and needn't reach their ends.
Inputs may be any that keep to these rules, and one draw needn't show every extreme that they name: `tally_of_tokens`: valid tokens of a request, at least one; some request has all 4, some has one. `prior_slot_lookup`: each former slot appears once. The 16 new slots of one index of seq take exactly one former slot of the index before it along seq, exactly one of the index after it (cyclically), and the rest from their own former slots.
All inputs are finite; a program needn't handle non-finite values.
Results may differ from the reference program's by a relative error of at most 0.015.
Values may be sent and summed in bfloat16 or wider, within the bound.
No kernel may reach another device: no remote copies, remote signals or barrier semaphores. Data moves between devices by JAX's collectives and lax.ppermute only.
A program may use at most 64 MiB of HBM per device.

```python
import jax
import jax.numpy as jnp
from jax import lax

EMBEDDING_DIM = 2048
TEAM_DIMENSION = 64
DECAY_RANK = 64
STEPS = 4
REQ_DEV = 16
ATTENTION_TEAMS = 32
REQUESTS = 1024


def draw_tally_of_tokens(key, part):
    levels = jax.random.randint(key, (REQUESTS,), 0, 16)
    result = 1 + (levels >= 8).astype(jnp.int32) + (levels >= 12).astype(jnp.int32) + (levels >= 14).astype(jnp.int32)
    first = jax.random.randint(jax.random.fold_in(key, 1), (), 0, REQUESTS)
    second = jnp.mod(first + 1 + jax.random.randint(jax.random.fold_in(key, 2), (), 0, REQUESTS - 1), REQUESTS)
    result = result.at[first].set(STEPS)
    result = result.at[second].set(1)
    return result.astype(jnp.int32)


def draw_prior_slot_lookup(key, part):
    groups = REQUESTS // REQ_DEV
    key_old = jax.random.fold_in(key, 11)
    key_new = jax.random.fold_in(key, 12)
    old_order = jax.vmap(lambda one: jax.random.permutation(one, REQ_DEV))(jax.random.split(key_old, groups)).astype(jnp.int32)
    new_order = jax.vmap(lambda one: jax.random.permutation(one, REQ_DEV))(jax.random.split(key_new, groups)).astype(jnp.int32)
    device = jnp.arange(groups, dtype=jnp.int32)
    to_before = old_order[:, 0]
    to_after = old_order[:, 1]
    from_before = jnp.roll(device, 1) * REQ_DEV + jnp.roll(to_after, 1)
    from_after = jnp.roll(device, -1) * REQ_DEV + jnp.roll(to_before, -1)
    kept = device[:, None] * REQ_DEV + old_order[:, 2:]
    listed = jnp.concatenate([from_before[:, None], from_after[:, None], kept], axis=1)
    placed = jnp.take_along_axis(listed, new_order, axis=1)
    return placed.reshape(REQUESTS).astype(jnp.int32)


def level_of(stream_key, dims, shards, low, largest):
    factor_of, own = 1.0, jax.random.fold_in(stream_key, 6)
    for axis_at, blocks in shards:
        draws = jnp.exp(jax.random.uniform(jax.random.fold_in(own, axis_at), (blocks,), jnp.float32, low / len(shards), largest / len(shards)))
        factor_of = factor_of * jnp.repeat(draws, dims[axis_at] // blocks).reshape([-1 if axis == axis_at else 1 for axis in range(len(dims))])
    return factor_of


def bell_draw(own_key, shape, scale, limit, pieces=(), held_as=jnp.bfloat16):
    level = level_of(own_key, shape, pieces, -0.22, 0.18) if pieces else 1.0
    values = jax.random.normal(own_key, shape, jnp.float32) * scale * level
    return jnp.minimum(jnp.maximum(values, -limit), limit).astype(held_as)


def setup_inputs(seed: int = 0) -> dict:
    seeds = jax.random.split(jax.random.key(seed), 17)
    layer_entry_vectors = bell_draw(seeds[0], (REQUESTS, STEPS, EMBEDDING_DIM), 1.0, 6.0, ((0, 64),))
    tally_of_tokens = draw_tally_of_tokens(jax.random.fold_in(seeds[16], 71), 0)
    prior_slot_lookup = draw_prior_slot_lookup(jax.random.fold_in(seeds[16], 71), 0)
    memory_matrices = bell_draw(seeds[3], (REQUESTS, ATTENTION_TEAMS, TEAM_DIMENSION * TEAM_DIMENSION), 1.0, 6.0, ((0, 64), (1, 8)), jnp.float32)
    previous_standardized_entries = bell_draw(seeds[4], (REQUESTS, EMBEDDING_DIM), 1.0, 6.0, ((0, 64),), jnp.float32)
    entry_standardize_scale = jnp.clip(1.0 + 0.18 * jax.random.normal(seeds[5], (EMBEDDING_DIM,), jnp.float32), 0.1, 1.9)
    blend_coefficients = jnp.clip(jax.random.uniform(seeds[6], (4, EMBEDDING_DIM), jnp.float32, 0.0, 1.0), 0.0, 1.0)
    acceptance_projection_matrix = bell_draw(seeds[7], (EMBEDDING_DIM, EMBEDDING_DIM), EMBEDDING_DIM ** -0.5, 0.125, ((1, 8),))
    lookup_projection_matrix = bell_draw(seeds[8], (EMBEDDING_DIM, EMBEDDING_DIM), EMBEDDING_DIM ** -0.5, 0.125, ((1, 8),))
    payload_projection_matrix = bell_draw(seeds[9], (EMBEDDING_DIM, EMBEDDING_DIM), EMBEDDING_DIM ** -0.5, 0.125, ((1, 8),))
    forget_map_left_matrix = bell_draw(seeds[10], (EMBEDDING_DIM, DECAY_RANK), EMBEDDING_DIM ** -0.5, 0.125, ((0, 8),))
    forget_map_right_matrix = bell_draw(seeds[11], (DECAY_RANK, EMBEDDING_DIM), DECAY_RANK ** -0.5, 0.75, ((1, 8),))
    feature_forget_logloglevel = jnp.clip(-6.0 + 7.0 * jax.random.uniform(seeds[12], (EMBEDDING_DIM,), jnp.float32) ** level_of(seeds[12], (EMBEDDING_DIM,), ((0, 8),), -0.2, 0.2), -6.0, 1.0)
    present_token_boost = bell_draw(seeds[13], (EMBEDDING_DIM,), 0.5, 3.0, ((0, 8),), jnp.float32)
    team_standardize_scale = jnp.clip(1.0 + 0.18 * jax.random.normal(seeds[14], (EMBEDDING_DIM,), jnp.float32), 0.1, 1.9)
    final_projection_matrix = bell_draw(seeds[15], (EMBEDDING_DIM, EMBEDDING_DIM), EMBEDDING_DIM ** -0.5, 0.125, ((0, 8),))
    return dict(layer_entry_vectors=layer_entry_vectors, tally_of_tokens=tally_of_tokens, prior_slot_lookup=prior_slot_lookup, memory_matrices=memory_matrices, previous_standardized_entries=previous_standardized_entries, entry_standardize_scale=entry_standardize_scale, blend_coefficients=blend_coefficients, acceptance_projection_matrix=acceptance_projection_matrix, lookup_projection_matrix=lookup_projection_matrix, payload_projection_matrix=payload_projection_matrix, forget_map_left_matrix=forget_map_left_matrix, forget_map_right_matrix=forget_map_right_matrix, feature_forget_logloglevel=feature_forget_logloglevel, present_token_boost=present_token_boost, team_standardize_scale=team_standardize_scale, final_projection_matrix=final_projection_matrix)


EPS = 1e-05

def layer_norm(values, gain):
    center = values - lax.optimization_barrier(jnp.mean(values, axis=-1, keepdims=True))
    spread = lax.optimization_barrier(jnp.mean(center * center, axis=-1, keepdims=True))
    return center * lax.rsqrt(spread + EPS) * gain

def reference(layer_entry_vectors, tally_of_tokens, prior_slot_lookup, memory_matrices, previous_standardized_entries, entry_standardize_scale, blend_coefficients, acceptance_projection_matrix, lookup_projection_matrix, payload_projection_matrix, forget_map_left_matrix, forget_map_right_matrix, feature_forget_logloglevel, present_token_boost, team_standardize_scale, final_projection_matrix):
    total = layer_entry_vectors.shape[0]
    moved = jnp.take(memory_matrices, prior_slot_lookup, axis=0)
    shift_in = jnp.take(previous_standardized_entries, prior_slot_lookup, axis=0)
    inputs = layer_entry_vectors.astype(jnp.float32)
    normed = layer_norm(inputs, entry_standardize_scale)
    before = jnp.concatenate([shift_in[:, None, :], normed[:, :-1]], axis=1)
    change = before - normed

    def shifted_mix_rows(which):
        return (normed + change * blend_coefficients[which]).astype(jnp.bfloat16).reshape(total * STEPS, EMBEDDING_DIM)

    def project(which, weight):
        return jnp.dot(shifted_mix_rows(which), weight, preferred_element_type=jnp.float32).reshape(total, STEPS, ATTENTION_TEAMS, TEAM_DIMENSION)
    recept = project(0, acceptance_projection_matrix)
    keys = project(1, lookup_projection_matrix)
    values = project(2, payload_projection_matrix)
    prenorm_output = jnp.dot(shifted_mix_rows(3), forget_map_left_matrix, preferred_element_type=jnp.float32)
    decay_lowrank = jnp.tanh(prenorm_output).astype(jnp.bfloat16)
    decay_factor = jnp.exp(-jnp.exp(feature_forget_logloglevel + jnp.dot(decay_lowrank, forget_map_right_matrix, preferred_element_type=jnp.float32)))
    decay_factor = decay_factor.reshape(total, STEPS, ATTENTION_TEAMS, TEAM_DIMENSION)
    team_boost_vectors = present_token_boost.reshape(ATTENTION_TEAMS, TEAM_DIMENSION)
    state = moved.reshape(total, ATTENTION_TEAMS, TEAM_DIMENSION, TEAM_DIMENSION)
    outputs = []
    for step in range(STEPS):
        valid = (tally_of_tokens > step)[:, None, None, None]
        current_receptance = recept[:, step]
        current_key = keys[:, step]
        current_value = values[:, step]
        state_readout = jnp.einsum('rhi,rhij->rhj', current_receptance, state, precision=lax.Precision.HIGHEST)
        state_readout = state_readout + lax.optimization_barrier(jnp.sum(current_receptance * team_boost_vectors * current_key, axis=-1, keepdims=True)) * current_value
        outputs.append(state_readout)
        updated = decay_factor[:, step][..., None] * state + current_key[..., None] * current_value[..., None, :]
        state = jnp.where(valid, updated, state)
    heads_out = jnp.stack(outputs, axis=1)
    center = heads_out - lax.optimization_barrier(jnp.mean(heads_out, axis=-1, keepdims=True))
    spread = lax.optimization_barrier(jnp.mean(center * center, axis=-1, keepdims=True))
    normal_out = (center * lax.rsqrt(spread + EPS)).reshape(total, STEPS, EMBEDDING_DIM) * team_standardize_scale
    normal_out = normal_out.astype(jnp.bfloat16).reshape(total * STEPS, EMBEDDING_DIM)
    proj = jnp.dot(normal_out, final_projection_matrix, preferred_element_type=jnp.float32).reshape(total, STEPS, EMBEDDING_DIM)
    positions = jnp.arange(STEPS).astype(jnp.int32)
    valid_slots = tally_of_tokens[:, None] > positions[None, :]
    mixed = jnp.where(valid_slots[..., None], inputs + proj, 0.0).astype(jnp.bfloat16)
    last_slot = (positions[None, :] == tally_of_tokens[:, None] - 1)[..., None]
    new_shifts = lax.optimization_barrier(jnp.sum(jnp.where(last_slot, normed, 0.0), axis=1))
    return (mixed, state.reshape(total, ATTENTION_TEAMS, TEAM_DIMENSION * TEAM_DIMENSION), new_shifts)
```

```python
import functools

import jax
import jax.numpy as jnp
from jax import lax
from jax.experimental import pallas as pl
from jax.experimental.pallas import tpu as pltpu
from jax.sharding import PartitionSpec as P

EPS = 1e-05
F32 = jnp.float32
BF16 = jnp.bfloat16
HEAD = 64
SLOTS = 16
STEPS = 4
WIDTH = 2048
HEADS = 4
LOCAL = HEADS * HEAD
TILES = WIDTH // 128
ROWS = SLOTS * STEPS
STATE_ROWS = HEADS * HEAD * HEAD // 128
PIECE = STATE_ROWS + TILES
PACK_ROWS = 2 * PIECE + 8


def vmem(count):
    return [pl.BlockSpec(memory_space=pltpu.VMEM)] * count


def smem(count):
    return [pl.BlockSpec(memory_space=pltpu.SMEM)] * count


def dot(a, b):
    return jnp.dot(a, b, preferred_element_type=F32)


def dot_rows(a, b):
    return lax.dot_general(a, b, (((0,), (0,)), ((), ())), preferred_element_type=F32)


def split(a):
    hi = a.astype(BF16)
    return hi, (a - hi.astype(F32)).astype(BF16)


def dot_split(a, b):
    hi, lo = split(a)
    return dot(hi, b) + dot(lo, b)


def iota(shape, dim):
    return lax.broadcasted_iota(jnp.int32, shape, dim)


def column_of(tally_ref, shape):
    rows = iota(shape, 0)
    out = jnp.zeros(shape, jnp.int32)
    for q in range(SLOTS):
        out = jnp.where(rows == q, tally_ref[q], out)
    return out


def row_of(ref):
    return jnp.concatenate([ref[i : i + 1, :] for i in range(ref.shape[0])], axis=1)


def pack_kernel(where_ref, lookup_ref, mem_ref, prev_ref, out_ref):
    first = where_ref[0] * SLOTS
    kept = jnp.int32(0)
    for q in range(SLOTS):
        at = lookup_ref[q] - first
        own = (at >= 0) & (at < SLOTS)
        kept = kept | jnp.where(own, jnp.int32(1) << jnp.where(own, at, 0), 0)
    low, high = jnp.int32(0), jnp.int32(0)
    for s in range(SLOTS):
        high = jnp.where((kept >> s) & 1 == 0, s, high)
        low = jnp.where((kept >> (SLOTS - 1 - s)) & 1 == 0, SLOTS - 1 - s, low)
    for n, slot in enumerate((low, high)):
        base = n * PIECE
        out_ref[base : base + STATE_ROWS, :] = mem_ref[pl.ds(slot * STATE_ROWS, STATE_ROWS), :]
        row = prev_ref[pl.ds(slot, 1), :]
        for c in range(TILES):
            out_ref[base + STATE_ROWS + c : base + STATE_ROWS + c + 1, :] = row[:, c * 128 : (c + 1) * 128]
    ids = jnp.where(iota((8, 128), 0) == 0, first + low, first + high)
    out_ref[2 * PIECE : 2 * PIECE + 8, :] = ids.astype(F32)


def pick(recv_ref, wanted, start, count):
    is_low = recv_ref[2 * PIECE : 2 * PIECE + 1, :] == wanted.astype(F32)
    return jnp.where(is_low, recv_ref[start : start + count, :], recv_ref[PIECE + start : PIECE + start + count, :])


def sources(where_ref, lookup_ref, q):
    wanted = lookup_ref[q]
    owner = wanted // SLOTS
    own = owner == where_ref[0]
    before = owner == where_ref[1]
    at = jnp.where(own, wanted - where_ref[0] * SLOTS, 0)
    return wanted, own, before, at


def project_kernel(
    where_ref, lookup_ref, tally_ref, x_ref, prev_ref, from_before, from_after, gain_ref, blend_ref, wr_ref, wk_ref, wv_ref,
    r_ref, k_ref, v_ref, mixed_ref, last_ref, x32, shift,
):
    x32[...] = x_ref[...].astype(F32)
    gain = row_of(gain_ref)
    normed = []
    for t in range(STEPS):
        row = jnp.concatenate([x32[pl.ds(c * STEPS + t, SLOTS, stride=STEPS * TILES), :] for c in range(TILES)], axis=1)
        center = row - jnp.mean(row, axis=-1, keepdims=True)
        spread = jnp.mean(center * center, axis=-1, keepdims=True)
        normed.append(center * lax.rsqrt(spread + EPS) * gain)
    tally = column_of(tally_ref, (SLOTS, 128))[:, :1]
    last = normed[0]
    for t in range(1, STEPS):
        last = jnp.where(tally == t + 1, normed[t], last)
    last_ref[...] = last
    for q in range(SLOTS):
        wanted, own, before, at = sources(where_ref, lookup_ref, q)

        @pl.when(own)
        def _():
            shift[q : q + 1, :] = prev_ref[pl.ds(at, 1), :]

        @pl.when(jnp.logical_not(own))
        def _():
            rows = jnp.where(
                before, pick(from_before, wanted, STATE_ROWS, TILES), pick(from_after, wanted, STATE_ROWS, TILES)
            )
            for c in range(TILES):
                shift[q : q + 1, c * 128 : (c + 1) * 128] = rows[c : c + 1, :]

    xn = jnp.concatenate(normed, axis=0)
    change = jnp.concatenate([shift[...]] + normed[:-1], axis=0) - xn

    def mix(which):
        return (xn + change * blend_ref[which : which + 1, :]).astype(BF16)

    r_ref[...] = dot(mix(0), wr_ref[...])
    k_ref[...] = dot(mix(1), wk_ref[...])
    v_ref[...] = dot(mix(2), wv_ref[...])
    mixed_ref[...] = mix(3)


def step_kernel(
    where_ref, lookup_ref, tally_ref, mixed_ref, left_ref, right_ref, base_ref, boost_ref, gain_ref, r_ref, k_ref, v_ref,
    mem_ref, from_before, from_after, final_ref,
    part_ref, new_ref, state, reads, keys, vals, decays, heads, part,
):
    for q in range(SLOTS):
        wanted, own, before, at = sources(where_ref, lookup_ref, q)
        here = slice(q * STATE_ROWS, (q + 1) * STATE_ROWS)

        @pl.when(own)
        def _():
            state[here, :] = mem_ref[pl.ds(at * STATE_ROWS, STATE_ROWS), :]

        @pl.when(jnp.logical_not(own) & before)
        def _():
            state[here, :] = pick(from_before, wanted, 0, STATE_ROWS)

        @pl.when(jnp.logical_not(own) & jnp.logical_not(before))
        def _():
            state[here, :] = pick(from_after, wanted, 0, STATE_ROWS)

    pre = jnp.zeros((ROWS, left_ref.shape[1]), F32)
    chunk = left_ref.shape[2]
    for n in range(left_ref.shape[0]):
        pre = pre + lax.dot_general(
            mixed_ref[:, n * chunk : (n + 1) * chunk], left_ref[n], (((1,), (1,)), ((), ())), preferred_element_type=F32
        )
    lora = jnp.tanh(pre).astype(BF16)
    decay = jnp.exp(-jnp.exp(row_of(base_ref) + dot(lora, right_ref[...])))
    tally = column_of(tally_ref, (SLOTS, 128))[:, :1]
    cut = lambda a, t: a[t * SLOTS : (t + 1) * SLOTS, :]
    r = [cut(r_ref[...], t) for t in range(STEPS)]
    k = [cut(k_ref[...], t) for t in range(STEPS)]
    v = [cut(v_ref[...], t) for t in range(STEPS)]
    d = [jnp.where(tally > t, cut(decay, t), 1.0) for t in range(STEPS)]
    kept = [jnp.where(tally > t, k[t], 0.0) for t in range(STEPS)]
    boost = row_of(boost_ref)

    run, reach = r[0] * 0.0 + 1.0, []
    for t in range(STEPS):
        reach.append(r[t] * run)
        run = run * d[t]
    tail, coefs = None, [None] * STEPS
    for t in reversed(range(STEPS)):
        coefs[t] = kept[t] if tail is None else kept[t] * tail
        tail = d[t] if tail is None else tail * d[t]
    pairs, terms = [], []
    for t in range(STEPS):
        pairs.append((t, t))
        terms.append(r[t] * boost * k[t])
        weight = r[t]
        for s in reversed(range(t)):
            pairs.append((t, s))
            terms.append(weight * kept[s])
            weight = weight * d[s]
    row256, col256 = iota((LOCAL, LOCAL), 0), iota((LOCAL, LOCAL), 1)
    same_head = (row256 // HEAD == col256 // HEAD).astype(BF16)
    sums = dot_split(jnp.concatenate(terms, axis=0), same_head)
    within = [None] * STEPS
    for n, (t, s) in enumerate(pairs):
        term = cut(sums, n) * v[s]
        within[t] = term if within[t] is None else within[t] + term

    source = (col256 % HEADS) * HEAD + ((col256 // HEADS) % (HEAD // 2)) * 2 + col256 // 128
    reorder = (row256 == source).astype(BF16)
    moved = dot_split(jnp.concatenate(reach + coefs + [run], axis=0), reorder)
    rowd, cold = iota((LOCAL, HEADS * 128), 0), iota((LOCAL, HEADS * 128), 1)
    double = (rowd == (cold // 128) * HEAD + cold % HEAD).astype(BF16)
    doubled = dot(v_ref[...].astype(BF16), double)

    lane = iota((SLOTS, 128), 1)
    for h in range(HEADS):
        head_lane = lane % HEADS == h
        for p in range(2):
            half = lane // HEAD == p
            for t in range(STEPS):
                at = pl.ds(t * 8 + p * HEADS + h, SLOTS, stride=STEPS * 8)
                cols = slice(p * 128, (p + 1) * 128)
                reads[at, :] = jnp.where(head_lane, cut(moved, t)[:, cols], 0.0)
                keys[at, :] = jnp.where(head_lane, cut(moved, STEPS + t)[:, cols], 0.0)
                vals[at, :] = jnp.where(half, cut(doubled, t)[:, h * 128 : (h + 1) * 128], 0.0)
            whole = jnp.where(head_lane, cut(moved, 2 * STEPS)[:, cols], 0.0)
            high = whole.astype(BF16).astype(F32)
            decays[pl.ds(p * HEADS + h, SLOTS, stride=16), :] = high
            decays[pl.ds(8 + p * HEADS + h, SLOTS, stride=16), :] = whole - high
    ones = ((iota((16, 128), 0) // HEADS) % 2 == iota((16, 128), 1) // HEAD).astype(BF16)
    for q in range(SLOTS):
        here = slice(q * STATE_ROWS, (q + 1) * STATE_ROWS)
        rows = slice(q * STEPS * 8, (q + 1) * STEPS * 8)
        now = state[here, :]
        heads[rows, :] = dot(reads[rows, :].astype(BF16), now.astype(BF16))
        fade = dot_rows(decays[q * 16 : (q + 1) * 16, :].astype(BF16), ones)
        grown = dot_rows(keys[rows, :].astype(BF16), vals[rows, :].astype(BF16))
        new_ref[here, :] = fade * now + grown

    outs = []
    left_half = lane < HEAD
    for t in range(STEPS):
        def read(p, h):
            return heads[pl.ds(t * 8 + p * HEADS + h, SLOTS, stride=STEPS * 8), :]

        cols = []
        for h in range(0, HEADS, 2):
            a, b, c, e = read(0, h), read(1, h), read(0, h + 1), read(1, h + 1)
            cols.append(jnp.where(left_half, a, e) + pltpu.roll(jnp.where(left_half, c, b), HEAD, 1))
        outs.append(jnp.concatenate(cols, axis=1) + within[t])
    y = jnp.concatenate(outs, axis=0)
    center = y - dot_split(y, same_head) * (1.0 / HEAD)
    spread = dot_split(center * center, same_head) * (1.0 / HEAD)
    g = (center * lax.rsqrt(spread + EPS) * row_of(gain_ref)).astype(BF16)
    proj = dot(g, final_ref[...])
    for t in range(STEPS):
        for c in range(TILES):
            part[pl.ds(c * STEPS + t, SLOTS, stride=STEPS * TILES), :] = cut(proj, t)[:, c * 128 : (c + 1) * 128]
    part_ref[...] = part[...].astype(BF16)


def finish_kernel(tally_ref, x_ref, proj_ref, out_ref):
    step = iota((STEPS * TILES, 128), 0) % STEPS
    for q in range(SLOTS):
        here = slice(q * STEPS * TILES, (q + 1) * STEPS * TILES)
        total = x_ref[here, :].astype(F32) + proj_ref[here, :].astype(F32)
        out_ref[here, :] = jnp.where(step < tally_ref[q], total, 0.0).astype(BF16)


def cost(flops, bytes_accessed):
    return pl.CostEstimate(flops=flops, bytes_accessed=bytes_accessed, transcendentals=0)


def tiles_view(a):
    lead, mid, width = a.shape
    return a.reshape(lead, mid, width // 128, 128).transpose(0, 2, 1, 3).reshape(lead * width // 128 * mid, 128)


def tiles_back(a, lead, mid, width):
    return a.reshape(lead, width // 128, mid, 128).transpose(0, 2, 1, 3).reshape(lead, mid, width)


def shards(
    layer_entry_vectors,
    tally_of_tokens,
    prior_slot_lookup,
    memory_matrices,
    previous_standardized_entries,
    entry_standardize_scale,
    blend_coefficients,
    acceptance_projection_matrix,
    lookup_projection_matrix,
    payload_projection_matrix,
    forget_map_left_matrix,
    forget_map_right_matrix,
    feature_forget_logloglevel,
    present_token_boost,
    team_standardize_scale,
    final_projection_matrix,
):
    rings = lax.axis_size("seq")
    teams = lax.axis_size("tensor")
    device = lax.axis_index("seq")
    where = jnp.stack([device, (device + rings - 1) % rings]).astype(jnp.int32)
    x = tiles_view(layer_entry_vectors)
    mem = tiles_view(memory_matrices)
    params = pltpu.CompilerParams(vmem_limit_bytes=24 << 20)

    left_t = forget_map_left_matrix.T
    left = lax.all_to_all(jnp.broadcast_to(left_t[None], (teams,) + left_t.shape), "tensor", 0, 0)

    packed = pl.pallas_call(
        pack_kernel,
        out_shape=jax.ShapeDtypeStruct((PACK_ROWS, 128), F32),
        in_specs=smem(2) + vmem(2),
        out_specs=vmem(1)[0],
        compiler_params=params,
        cost_estimate=cost(0, 1 << 20),
        name="pack",
    )(where, prior_slot_lookup, mem, previous_standardized_entries)
    from_before = lax.ppermute(packed, "seq", [(i, (i + 1) % rings) for i in range(rings)])
    from_after = lax.ppermute(packed, "seq", [((i + 1) % rings, i) for i in range(rings)])

    r, k, v, mixed3, new_shifts = pl.pallas_call(
        project_kernel,
        out_shape=[jax.ShapeDtypeStruct((ROWS, LOCAL), F32)] * 3
        + [jax.ShapeDtypeStruct((ROWS, WIDTH), BF16), jax.ShapeDtypeStruct((SLOTS, WIDTH), F32)],
        in_specs=smem(3) + vmem(9),
        out_specs=vmem(5),
        scratch_shapes=[pltpu.VMEM((ROWS * TILES, 128), F32), pltpu.VMEM((SLOTS, WIDTH), F32)],
        compiler_params=params,
        cost_estimate=cost(6 * ROWS * WIDTH * LOCAL, 4 << 20),
        name="project",
    )(
        where, prior_slot_lookup, tally_of_tokens, x, previous_standardized_entries, from_before, from_after,
        entry_standardize_scale.reshape(TILES, 128), blend_coefficients,
        acceptance_projection_matrix, lookup_projection_matrix, payload_projection_matrix,
    )

    part, new_states = pl.pallas_call(
        step_kernel,
        out_shape=[
            jax.ShapeDtypeStruct((ROWS * TILES, 128), BF16),
            jax.ShapeDtypeStruct((SLOTS * STATE_ROWS, 128), F32),
        ],
        in_specs=smem(3) + vmem(13),
        out_specs=vmem(2),
        scratch_shapes=[
            pltpu.VMEM((SLOTS * STATE_ROWS, 128), F32),
            pltpu.VMEM((SLOTS * STEPS * 8, 128), F32),
            pltpu.VMEM((SLOTS * STEPS * 8, 128), F32),
            pltpu.VMEM((SLOTS * STEPS * 8, 128), F32),
            pltpu.VMEM((SLOTS * 16, 128), F32),
            pltpu.VMEM((SLOTS * STEPS * 8, 128), F32),
            pltpu.VMEM((ROWS * TILES, 128), F32),
        ],
        compiler_params=params,
        cost_estimate=cost(2 * ROWS * WIDTH * LOCAL, 4 << 20),
        name="step",
    )(
        where, prior_slot_lookup, tally_of_tokens, mixed3, left, forget_map_right_matrix,
        feature_forget_logloglevel.reshape(2, 128), present_token_boost.reshape(2, 128),
        team_standardize_scale.reshape(2, 128), r, k, v, mem, from_before, from_after, final_projection_matrix,
    )

    pairs = [[2 * i, 2 * i + 1] for i in range(teams // 2)]
    chips = [[2 * i + c for i in range(teams // 2)] for c in range(2)]
    half = ROWS * TILES // 2
    both = lax.all_gather(part, "tensor", axis_index_groups=pairs, tiled=False)
    core = lax.axis_index("tensor") % 2
    mine = lax.dynamic_slice_in_dim(both, core * half, half, 1).astype(F32).sum(0).astype(BF16)
    spread = lax.all_to_all(
        jnp.broadcast_to(mine[None], (teams // 2,) + mine.shape), "tensor", 0, 0, axis_index_groups=chips
    )
    total = spread.astype(F32).sum(0).astype(BF16)
    proj = lax.all_gather(total, "tensor", axis_index_groups=pairs, tiled=True)

    mixed = pl.pallas_call(
        finish_kernel,
        out_shape=jax.ShapeDtypeStruct((ROWS * TILES, 128), BF16),
        in_specs=smem(1) + vmem(2),
        out_specs=vmem(1)[0],
        compiler_params=params,
        cost_estimate=cost(0, 1 << 19),
        name="finish",
    )(tally_of_tokens, x, proj)
    return (
        tiles_back(mixed, SLOTS, STEPS, WIDTH),
        tiles_back(new_states, SLOTS, HEADS, HEAD * HEAD),
        new_shifts,
    )


def solution(mesh):
    in_specs = (
        P("seq", None, None),
        P("seq"),
        P("seq"),
        P("seq", "tensor", None),
        P("seq", None),
        P(),
        P(),
        P(None, "tensor"),
        P(None, "tensor"),
        P(None, "tensor"),
        P("tensor", None),
        P(None, "tensor"),
        P("tensor"),
        P("tensor"),
        P("tensor"),
        P("tensor", None),
    )
    out_specs = (P("seq", None, None), P("seq", "tensor", None), P("seq", None))
    return jax.shard_map(shards, mesh=mesh, in_specs=in_specs, out_specs=out_specs, check_vma=False)
```

```python
import functools

import jax
import jax.numpy as jnp
from jax import lax
from jax.experimental import pallas as pl
from jax.experimental.pallas import tpu as pltpu
from jax.sharding import PartitionSpec as P

EPS = 1e-05
F32 = jnp.float32
BF16 = jnp.bfloat16
HEAD = 64
SLOTS = 16
STEPS = 4
WIDTH = 2048
HEADS = 4
LOCAL = HEADS * HEAD
TILES = WIDTH // 128
ROWS = SLOTS * STEPS
STATE_ROWS = HEADS * HEAD * HEAD // 128
PIECE = STATE_ROWS + TILES
PACK_ROWS = 2 * PIECE + 8
TALLY, OWNER = SLOTS, 2 * SLOTS


def spec(space, count):
    return [pl.BlockSpec(memory_space=space)] * count


def dot(a, b):
    return jnp.dot(a, b, preferred_element_type=F32)


def dot_rows(a, b):
    return lax.dot_general(a, b, (((0,), (0,)), ((), ())), preferred_element_type=F32)


def split(a):
    hi = a.astype(BF16)
    return hi, (a - hi.astype(F32)).astype(BF16)


def dot_split(a, b):
    hi, lo = split(a)
    return dot(hi, b) + dot(lo, b)


def iota(shape, dim):
    return lax.broadcasted_iota(jnp.int32, shape, dim)


def column_of(meta_ref, shape):
    rows = iota(shape, 0)
    out = jnp.zeros(shape, jnp.int32)
    for q in range(SLOTS):
        out = jnp.where(rows == q, meta_ref[TALLY + q], out)
    return out


def row_of(ref):
    return jnp.concatenate([ref[i : i + 1, :] for i in range(ref.shape[0])], axis=1)


def start(copies):
    for copy in copies:
        copy.start()


def pack_kernel(meta_ref, mem_ref, prev_ref, left_ref, out_ref, left_out, prev, row_tile, sems):
    first = meta_ref[OWNER] * SLOTS
    load = pltpu.make_async_copy(prev_ref, prev, sems.at[0])
    load.start()
    spread = [
        pltpu.make_async_copy(left_ref, left_out.at[n], sems.at[8 + n]) for n in range(left_out.shape[0])
    ]
    start(spread)
    kept = jnp.int32(0)
    for q in range(SLOTS):
        at = meta_ref[q] - first
        own = (at >= 0) & (at < SLOTS)
        kept = kept | jnp.where(own, jnp.int32(1) << jnp.where(own, at, 0), 0)
    low, high = jnp.int32(0), jnp.int32(0)
    for s in range(SLOTS):
        high = jnp.where((kept >> s) & 1 == 0, s, high)
        low = jnp.where((kept >> (SLOTS - 1 - s)) & 1 == 0, SLOTS - 1 - s, low)
    moves = [
        pltpu.make_async_copy(
            mem_ref.at[pl.ds(pl.multiple_of(slot * STATE_ROWS, STATE_ROWS), STATE_ROWS), :],
            out_ref.at[pl.ds(n * PIECE, STATE_ROWS), :],
            sems.at[1 + n],
        )
        for n, slot in enumerate((low, high))
    ]
    start(moves)
    row_tile[2 * TILES :, :] = jnp.where(iota((8, 128), 0) == 0, first + low, first + high).astype(F32)
    load.wait()
    for n, slot in enumerate((low, high)):
        row = prev[pl.ds(slot, 1), :]
        for c in range(TILES):
            row_tile[n * TILES + c : n * TILES + c + 1, :] = row[:, c * 128 : (c + 1) * 128]
    rows = [
        pltpu.make_async_copy(
            row_tile.at[pl.ds(0, TILES), :], out_ref.at[pl.ds(STATE_ROWS, TILES), :], sems.at[3]
        ),
        pltpu.make_async_copy(
            row_tile.at[pl.ds(TILES, TILES + 8), :], out_ref.at[pl.ds(PIECE + STATE_ROWS, TILES + 8), :], sems.at[4]
        ),
    ]
    start(rows)
    for copy in moves + rows + spread:
        copy.wait()


def pick(recv_ref, wanted, begin, count):
    is_low = recv_ref[2 * PIECE : 2 * PIECE + 1, :] == wanted.astype(F32)
    return jnp.where(is_low, recv_ref[begin : begin + count, :], recv_ref[PIECE + begin : PIECE + begin + count, :])


def sources(meta_ref, q):
    wanted = meta_ref[q]
    owner = wanted // SLOTS
    own = owner == meta_ref[OWNER]
    before = owner == meta_ref[OWNER + 1]
    at = jnp.where(own, wanted - meta_ref[OWNER] * SLOTS, 0)
    return wanted, own, before, at


def main_kernel(*refs):
    meta_ref, mem_hbm = refs[:2]
    hbm = refs[2:17]
    part_ref, new_hbm, last_ref = refs[17:20]
    bufs = refs[20:35]
    x32, shift, state, reads, keys, vals, decays, heads, part, mixed_ref, fresh, sems, state_sems, new_sems = refs[35:]
    loads = [pltpu.make_async_copy(src, dst, sems.at[n]) for n, (src, dst) in enumerate(zip(hbm, bufs))]
    start(loads)
    state_loads = []
    for q in range(SLOTS):
        at = sources(meta_ref, q)[3]
        state_loads.append(
            pltpu.make_async_copy(
                mem_hbm.at[pl.ds(pl.multiple_of(at * STATE_ROWS, STATE_ROWS), STATE_ROWS), :],
                state.at[pl.ds(q * STATE_ROWS, STATE_ROWS), :],
                state_sems.at[q],
            )
        )
    start(state_loads)
    (
        x_ref, gain_ref, prev_ref, from_before, from_after, blend_ref, wr_ref, wk_ref, wv_ref,
        left_ref, right_ref, base_ref, boost_ref, team_ref, final_ref,
    ) = bufs
    arrive = lambda *which: [loads[n].wait() for n in which]

    arrive(0, 1)
    x32[...] = x_ref[...].astype(F32)
    gain = row_of(gain_ref)
    normed = []
    for t in range(STEPS):
        row = jnp.concatenate([x32[pl.ds(c * STEPS + t, SLOTS, stride=STEPS * TILES), :] for c in range(TILES)], axis=1)
        center = row - jnp.mean(row, axis=-1, keepdims=True)
        spread = jnp.mean(center * center, axis=-1, keepdims=True)
        normed.append(center * lax.rsqrt(spread + EPS) * gain)
    tally = column_of(meta_ref, (SLOTS, 128))[:, :1]
    last = normed[0]
    for t in range(1, STEPS):
        last = jnp.where(tally == t + 1, normed[t], last)
    last_ref[...] = last
    arrive(2, 3, 4, 5)
    for q in range(SLOTS):
        wanted, own, before, at = sources(meta_ref, q)

        @pl.when(own)
        def _():
            shift[q : q + 1, :] = prev_ref[pl.ds(at, 1), :]

        @pl.when(jnp.logical_not(own))
        def _():
            rows = jnp.where(
                before, pick(from_before, wanted, STATE_ROWS, TILES), pick(from_after, wanted, STATE_ROWS, TILES)
            )
            for c in range(TILES):
                shift[q : q + 1, c * 128 : (c + 1) * 128] = rows[c : c + 1, :]

    xn = jnp.concatenate(normed, axis=0)
    change = jnp.concatenate([shift[...]] + normed[:-1], axis=0) - xn

    def mix(which):
        return (xn + change * blend_ref[which : which + 1, :]).astype(BF16)

    mixed_ref[...] = mix(3)
    arrive(6)
    r_all = dot(mix(0), wr_ref[...])
    arrive(7)
    k_all = dot(mix(1), wk_ref[...])
    arrive(8)
    v_all = dot(mix(2), wv_ref[...])

    arrive(9, 10, 11, 12, 13)
    pre = jnp.zeros((ROWS, left_ref.shape[1]), F32)
    chunk = left_ref.shape[2]
    for n in range(left_ref.shape[0]):
        pre = pre + lax.dot_general(
            mixed_ref[:, n * chunk : (n + 1) * chunk], left_ref[n], (((1,), (1,)), ((), ())), preferred_element_type=F32
        )
    lora = jnp.tanh(pre).astype(BF16)
    decay = jnp.exp(-jnp.exp(row_of(base_ref) + dot(lora, right_ref[...])))
    cut = lambda a, t: a[t * SLOTS : (t + 1) * SLOTS, :]
    r = [cut(r_all, t) for t in range(STEPS)]
    k = [cut(k_all, t) for t in range(STEPS)]
    v = [cut(v_all, t) for t in range(STEPS)]
    d = [jnp.where(tally > t, cut(decay, t), 1.0) for t in range(STEPS)]
    kept = [jnp.where(tally > t, k[t], 0.0) for t in range(STEPS)]
    boost = row_of(boost_ref)

    run, reach = r[0] * 0.0 + 1.0, []
    for t in range(STEPS):
        reach.append(r[t] * run)
        run = run * d[t]
    tail, coefs = None, [None] * STEPS
    for t in reversed(range(STEPS)):
        coefs[t] = kept[t] if tail is None else kept[t] * tail
        tail = d[t] if tail is None else tail * d[t]
    pairs, terms = [], []
    for t in range(STEPS):
        pairs.append((t, t))
        terms.append(r[t] * boost * k[t])
        weight = r[t]
        for s in reversed(range(t)):
            pairs.append((t, s))
            terms.append(weight * kept[s])
            weight = weight * d[s]
    row256, col256 = iota((LOCAL, LOCAL), 0), iota((LOCAL, LOCAL), 1)
    same_head = (row256 // HEAD == col256 // HEAD).astype(BF16)
    sums = dot_split(jnp.concatenate(terms, axis=0), same_head)
    within = [None] * STEPS
    for n, (t, s) in enumerate(pairs):
        term = cut(sums, n) * v[s]
        within[t] = term if within[t] is None else within[t] + term

    source = (col256 % HEADS) * HEAD + ((col256 // HEADS) % (HEAD // 2)) * 2 + col256 // 128
    reorder = (row256 == source).astype(BF16)
    moved = dot_split(jnp.concatenate(reach + coefs + [run], axis=0), reorder)
    rowd, cold = iota((LOCAL, HEADS * 128), 0), iota((LOCAL, HEADS * 128), 1)
    double = (rowd == (cold // 128) * HEAD + cold % HEAD).astype(BF16)
    doubled = dot(v_all.astype(BF16), double)

    lane = iota((SLOTS, 128), 1)
    for h in range(HEADS):
        head_lane = lane % HEADS == h
        for p in range(2):
            half = lane // HEAD == p
            for t in range(STEPS):
                at = pl.ds(t * 8 + p * HEADS + h, SLOTS, stride=STEPS * 8)
                cols = slice(p * 128, (p + 1) * 128)
                reads[at, :] = jnp.where(head_lane, cut(moved, t)[:, cols], 0.0)
                keys[at, :] = jnp.where(head_lane, cut(moved, STEPS + t)[:, cols], 0.0)
                vals[at, :] = jnp.where(half, cut(doubled, t)[:, h * 128 : (h + 1) * 128], 0.0)
            whole = jnp.where(head_lane, cut(moved, 2 * STEPS)[:, cols], 0.0)
            high = whole.astype(BF16).astype(F32)
            decays[pl.ds(p * HEADS + h, SLOTS, stride=16), :] = high
            decays[pl.ds(8 + p * HEADS + h, SLOTS, stride=16), :] = whole - high
    ones = ((iota((16, 128), 0) // HEADS) % 2 == iota((16, 128), 1) // HEAD).astype(BF16)
    news = []
    for q in range(SLOTS):
        state_loads[q].wait()
        wanted, own, before, _ = sources(meta_ref, q)
        here = slice(q * STATE_ROWS, (q + 1) * STATE_ROWS)

        @pl.when(jnp.logical_not(own) & before)
        def _():
            state[here, :] = pick(from_before, wanted, 0, STATE_ROWS)

        @pl.when(jnp.logical_not(own) & jnp.logical_not(before))
        def _():
            state[here, :] = pick(from_after, wanted, 0, STATE_ROWS)

    for q in range(SLOTS):
        here = slice(q * STATE_ROWS, (q + 1) * STATE_ROWS)
        rows = slice(q * STEPS * 8, (q + 1) * STEPS * 8)
        now = state[here, :]
        heads[rows, :] = dot(reads[rows, :].astype(BF16), now.astype(BF16))
        fade = dot_rows(decays[q * 16 : (q + 1) * 16, :].astype(BF16), ones)
        grown = dot_rows(keys[rows, :].astype(BF16), vals[rows, :].astype(BF16))
        fresh[here, :] = fade * now + grown
        news.append(pltpu.make_async_copy(fresh.at[here, :], new_hbm.at[here, :], new_sems.at[q]))
        news[-1].start()

    outs = []
    left_half = lane < HEAD
    for t in range(STEPS):
        def read(p, h):
            return heads[pl.ds(t * 8 + p * HEADS + h, SLOTS, stride=STEPS * 8), :]

        cols = []
        for h in range(0, HEADS, 2):
            a, b, c, e = read(0, h), read(1, h), read(0, h + 1), read(1, h + 1)
            cols.append(jnp.where(left_half, a, e) + pltpu.roll(jnp.where(left_half, c, b), HEAD, 1))
        outs.append(jnp.concatenate(cols, axis=1) + within[t])
    y = jnp.concatenate(outs, axis=0)
    center = y - dot_split(y, same_head) * (1.0 / HEAD)
    spread = dot_split(center * center, same_head) * (1.0 / HEAD)
    g = (center * lax.rsqrt(spread + EPS) * row_of(team_ref)).astype(BF16)
    arrive(14)
    proj = dot(g, final_ref[...])
    for t in range(STEPS):
        for c in range(TILES):
            part[pl.ds(c * STEPS + t, SLOTS, stride=STEPS * TILES), :] = cut(proj, t)[:, c * 128 : (c + 1) * 128]
    part_ref[...] = part[...].astype(BF16)
    for copy in news:
        copy.wait()


def finish_kernel(meta_ref, x_hbm, parts_ref, out_ref, x_ref, sem):
    rows = out_ref.shape[0]
    begin = meta_ref[OWNER + 2] * rows
    load = pltpu.make_async_copy(x_hbm.at[pl.ds(pl.multiple_of(begin, rows), rows), :], x_ref, sem)
    load.start()
    step = iota((STEPS * TILES, 128), 0) % STEPS
    load.wait()
    for q in range(rows // (STEPS * TILES)):
        here = slice(q * STEPS * TILES, (q + 1) * STEPS * TILES)
        total = x_ref[here, :].astype(F32)
        for n in range(parts_ref.shape[0]):
            total = total + parts_ref[n, here, :].astype(F32)
        tally = meta_ref[TALLY + meta_ref[OWNER + 2] * (rows // (STEPS * TILES)) + q]
        out_ref[here, :] = jnp.where(step < tally, total, 0.0).astype(BF16)


def cost(flops, bytes_accessed):
    return pl.CostEstimate(flops=flops, bytes_accessed=bytes_accessed, transcendentals=0)


def tiles_view(a):
    lead, mid, width = a.shape
    return a.reshape(lead, mid, width // 128, 128).transpose(0, 2, 1, 3).reshape(lead * width // 128 * mid, 128)


def tiles_back(a, lead, mid, width):
    return a.reshape(lead, width // 128, mid, 128).transpose(0, 2, 1, 3).reshape(lead, mid, width)


def shards(
    layer_entry_vectors,
    tally_of_tokens,
    prior_slot_lookup,
    memory_matrices,
    previous_standardized_entries,
    entry_standardize_scale,
    blend_coefficients,
    acceptance_projection_matrix,
    lookup_projection_matrix,
    payload_projection_matrix,
    forget_map_left_matrix,
    forget_map_right_matrix,
    feature_forget_logloglevel,
    present_token_boost,
    team_standardize_scale,
    final_projection_matrix,
):
    rings = lax.axis_size("seq")
    teams = lax.axis_size("tensor")
    device = lax.axis_index("seq")
    core = lax.axis_index("tensor") % 2
    meta = jnp.concatenate(
        [prior_slot_lookup, tally_of_tokens, jnp.stack([device, (device + rings - 1) % rings, core]).astype(jnp.int32)]
    )
    x = tiles_view(layer_entry_vectors)
    mem = tiles_view(memory_matrices)
    prev = previous_standardized_entries
    left_t = forget_map_left_matrix.T
    shape, scratch, dma = jax.ShapeDtypeStruct, pltpu.VMEM, pltpu.SemaphoreType.DMA

    packed, left = pl.pallas_call(
        pack_kernel,
        out_shape=[shape((PACK_ROWS, 128), F32), shape((teams,) + left_t.shape, BF16)],
        in_specs=spec(pltpu.SMEM, 1) + spec(pl.ANY, 3),
        out_specs=spec(pl.ANY, 2),
        scratch_shapes=[scratch(prev.shape, F32), scratch((2 * TILES + 8, 128), F32), dma((8 + teams,))],
        cost_estimate=cost(0, 1 << 20),
        compiler_params=pltpu.CompilerParams(vmem_limit_bytes=60 << 20),
        name="pack",
    )(meta, mem, prev, left_t)
    from_before = lax.ppermute(packed, "seq", [(i, (i + 1) % rings) for i in range(rings)])
    from_after = lax.ppermute(packed, "seq", [((i + 1) % rings, i) for i in range(rings)])
    left = lax.all_to_all(left, "tensor", 0, 0)

    operands = [
        x, entry_standardize_scale.reshape(TILES, 128), prev, from_before, from_after, blend_coefficients,
        acceptance_projection_matrix, lookup_projection_matrix, payload_projection_matrix,
        left, forget_map_right_matrix, feature_forget_logloglevel.reshape(2, 128),
        present_token_boost.reshape(2, 128), team_standardize_scale.reshape(2, 128), final_projection_matrix,
    ]
    part, new_states, new_shifts = pl.pallas_call(
        main_kernel,
        out_shape=[
            shape((ROWS * TILES, 128), BF16),
            shape((SLOTS * STATE_ROWS, 128), F32),
            shape((SLOTS, WIDTH), F32),
        ],
        in_specs=spec(pltpu.SMEM, 1) + spec(pl.ANY, 1 + len(operands)),
        out_specs=spec(pltpu.VMEM, 1) + spec(pl.ANY, 1) + spec(pltpu.VMEM, 1),
        scratch_shapes=[scratch(a.shape, a.dtype) for a in operands]
        + [
            scratch((ROWS * TILES, 128), F32),
            scratch((SLOTS, WIDTH), F32),
            scratch((SLOTS * STATE_ROWS, 128), F32),
            scratch((SLOTS * STEPS * 8, 128), F32),
            scratch((SLOTS * STEPS * 8, 128), F32),
            scratch((SLOTS * STEPS * 8, 128), F32),
            scratch((SLOTS * 16, 128), F32),
            scratch((SLOTS * STEPS * 8, 128), F32),
            scratch((ROWS * TILES, 128), F32),
            scratch((ROWS, WIDTH), BF16),
            scratch((SLOTS * STATE_ROWS, 128), F32),
            dma((len(operands),)),
            dma((SLOTS,)),
            dma((SLOTS,)),
        ],
        cost_estimate=cost(8 * ROWS * WIDTH * LOCAL, 8 << 20),
        compiler_params=pltpu.CompilerParams(vmem_limit_bytes=52 << 20),
        name="main",
    )(meta, mem, *operands)

    pairs = [[2 * i, 2 * i + 1] for i in range(teams // 2)]
    chips = [[2 * i + c for i in range(teams // 2)] for c in range(2)]
    half = ROWS * TILES // 2
    both = lax.all_gather(part, "tensor", axis_index_groups=pairs, tiled=False)
    mine = lax.dynamic_slice_in_dim(both, core * half, half, 1).astype(F32).sum(0).astype(BF16)
    spread = lax.all_to_all(
        jnp.broadcast_to(mine[None], (teams // 2,) + mine.shape), "tensor", 0, 0, axis_index_groups=chips
    )
    mixed = pl.pallas_call(
        finish_kernel,
        out_shape=shape((half, 128), BF16),
        in_specs=spec(pltpu.SMEM, 1) + spec(pl.ANY, 1) + spec(pltpu.VMEM, 1),
        out_specs=spec(pltpu.VMEM, 1)[0],
        scratch_shapes=[scratch((half, 128), BF16), dma],
        cost_estimate=cost(0, 1 << 19),
        compiler_params=pltpu.CompilerParams(vmem_limit_bytes=8 << 20),
        name="finish",
    )(meta, x, spread)
    mixed = tiles_back(mixed, SLOTS // 2, STEPS, WIDTH)
    mixed = lax.all_gather(mixed, "tensor", axis_index_groups=pairs, tiled=True)
    return (
        mixed,
        tiles_back(new_states, SLOTS, HEADS, HEAD * HEAD),
        new_shifts,
    )


def solution(mesh):
    in_specs = (
        P("seq", None, None),
        P("seq"),
        P("seq"),
        P("seq", "tensor", None),
        P("seq", None),
        P(),
        P(),
        P(None, "tensor"),
        P(None, "tensor"),
        P(None, "tensor"),
        P("tensor", None),
        P(None, "tensor"),
        P("tensor"),
        P("tensor"),
        P("tensor"),
        P("tensor", None),
    )
    out_specs = (P("seq", None, None), P("seq", "tensor", None), P("seq", None))
    return jax.shard_map(shards, mesh=mesh, in_specs=in_specs, out_specs=out_specs, check_vma=False)
```

```python
import functools

import jax
import jax.numpy as jnp
from jax import lax
from jax.experimental import pallas as pl
from jax.experimental.pallas import tpu as pltpu
from jax.sharding import PartitionSpec as P

EPS = 1e-05
F32 = jnp.float32
BF16 = jnp.bfloat16
HEAD = 64
SLOTS = 16
STEPS = 4
WIDTH = 2048
HEADS = 4
LOCAL = HEADS * HEAD
TILES = WIDTH // 128
ROWS = SLOTS * STEPS
STATE_ROWS = HEADS * HEAD * HEAD // 128
PIECE = STATE_ROWS + TILES
PACK_ROWS = 2 * PIECE + 8
PACK_MIB, MAIN_MIB = 60, 52


def spec(space, count):
    return [pl.BlockSpec(memory_space=space)] * count


def dot(a, b):
    return jnp.dot(a, b, preferred_element_type=F32)


def dot_rows(a, b):
    return lax.dot_general(a, b, (((0,), (0,)), ((), ())), preferred_element_type=F32)


def split(a):
    hi = a.astype(BF16)
    return hi, (a - hi.astype(F32)).astype(BF16)


def dot_split(a, b):
    hi, lo = split(a)
    return dot(hi, b) + dot(lo, b)


def iota(shape, dim):
    return lax.broadcasted_iota(jnp.int32, shape, dim)


def column_of(tally_ref, shape):
    rows = iota(shape, 0)
    out = jnp.zeros(shape, jnp.int32)
    for q in range(SLOTS):
        out = jnp.where(rows == q, tally_ref[q], out)
    return out


def row_of(ref):
    return jnp.concatenate([ref[i : i + 1, :] for i in range(ref.shape[0])], axis=1)


def start(items):
    for copy in items:
        copy.start()


def pack_kernel(where_ref, lookup_hbm, mem_ref, prev_ref, left_ref, out_ref, left_out, lookup_ref, prev, left, tile, sems):
    loads = [
        pltpu.make_async_copy(lookup_hbm, lookup_ref, sems.at[0]),
        pltpu.make_async_copy(prev_ref, prev, sems.at[1]),
        pltpu.make_async_copy(left_ref, left, sems.at[2]),
    ]
    start(loads)
    first = where_ref[0] * SLOTS
    loads[0].wait()
    kept = jnp.int32(0)
    for q in range(SLOTS):
        at = lookup_ref[q] - first
        own = (at >= 0) & (at < SLOTS)
        kept = kept | jnp.where(own, jnp.int32(1) << jnp.where(own, at, 0), 0)
    low, high = jnp.int32(0), jnp.int32(0)
    for s in range(SLOTS):
        high = jnp.where((kept >> s) & 1 == 0, s, high)
        low = jnp.where((kept >> (SLOTS - 1 - s)) & 1 == 0, SLOTS - 1 - s, low)
    moves = [
        pltpu.make_async_copy(
            mem_ref.at[pl.ds(pl.multiple_of(slot * STATE_ROWS, STATE_ROWS), STATE_ROWS), :],
            tile.at[pl.ds(n * PIECE, STATE_ROWS), :],
            sems.at[3 + n],
        )
        for n, slot in enumerate((low, high))
    ]
    start(moves)
    loads[2].wait()
    spread = [pltpu.make_async_copy(left, left_out.at[n], sems.at[8 + n]) for n in range(left_out.shape[0])]
    start(spread)
    tile[2 * PIECE :, :] = jnp.where(iota((8, 128), 0) == 0, first + low, first + high).astype(F32)
    loads[1].wait()
    for n, slot in enumerate((low, high)):
        row = prev[pl.ds(slot, 1), :]
        at = n * PIECE + STATE_ROWS
        for c in range(TILES):
            tile[at + c : at + c + 1, :] = row[:, c * 128 : (c + 1) * 128]
    moves[0].wait()
    moves[1].wait()
    done = pltpu.make_async_copy(tile, out_ref, sems.at[5])
    done.start()
    done.wait()
    for copy in spread:
        copy.wait()


def pick(recv_ref, wanted, begin, count):
    is_low = recv_ref[2 * PIECE : 2 * PIECE + 1, :] == wanted.astype(F32)
    return jnp.where(is_low, recv_ref[begin : begin + count, :], recv_ref[PIECE + begin : PIECE + begin + count, :])


def sources(where_ref, lookup_ref, q):
    wanted = lookup_ref[q]
    owner = wanted // SLOTS
    own = owner == where_ref[0]
    before = owner == where_ref[1]
    at = jnp.where(own, wanted - where_ref[0] * SLOTS, 0)
    return wanted, own, before, at


def copies(sources_, targets, sems):
    return [pltpu.make_async_copy(a, b, sems.at[n]) for n, (a, b) in enumerate(zip(sources_, targets))]


def state_copies(where_ref, lookup_ref, mem_hbm, state, sems):
    out = []
    for q in range(SLOTS):
        at = sources(where_ref, lookup_ref, q)[3]
        out.append(
            pltpu.make_async_copy(
                mem_hbm.at[pl.ds(pl.multiple_of(at * STATE_ROWS, STATE_ROWS), STATE_ROWS), :],
                state.at[pl.ds(q * STATE_ROWS, STATE_ROWS), :],
                sems.at[q],
            )
        )
    return out


def place_received(where_ref, lookup_ref, from_before, from_after, state):
    for q in range(SLOTS):
        wanted, own, before, _ = sources(where_ref, lookup_ref, q)
        here = slice(q * STATE_ROWS, (q + 1) * STATE_ROWS)

        @pl.when(jnp.logical_not(own) & before)
        def _():
            state[here, :] = pick(from_before, wanted, 0, STATE_ROWS)

        @pl.when(jnp.logical_not(own) & jnp.logical_not(before))
        def _():
            state[here, :] = pick(from_after, wanted, 0, STATE_ROWS)


def cut(a, t):
    return a[t * SLOTS : (t + 1) * SLOTS, :]


def project_kernel(where_ref, lookup_ref, tally_ref, *refs):
    count = 9
    hbm, (rkv_ref, mixed_ref, last_ref), bufs = refs[:count], refs[count : count + 3], refs[count + 3 : 2 * count + 3]
    x32, shift, sems = refs[2 * count + 3 :]
    loads = copies(hbm, bufs, sems)
    start(loads)
    x_ref, gain_ref, prev_ref, from_before, from_after, blend_ref = bufs[:6]
    loads[0].wait()
    loads[1].wait()
    x32[...] = x_ref[...].astype(F32)
    gain = row_of(gain_ref)
    normed = []
    for t in range(STEPS):
        row = jnp.concatenate([x32[pl.ds(c * STEPS + t, SLOTS, stride=STEPS * TILES), :] for c in range(TILES)], axis=1)
        center = row - jnp.mean(row, axis=-1, keepdims=True)
        spread = jnp.mean(center * center, axis=-1, keepdims=True)
        normed.append(center * lax.rsqrt(spread + EPS) * gain)
    tally = column_of(tally_ref, (SLOTS, 128))[:, :1]
    last = normed[0]
    for t in range(1, STEPS):
        last = jnp.where(tally == t + 1, normed[t], last)
    last_ref[...] = last
    for n in range(2, 6):
        loads[n].wait()
    for q in range(SLOTS):
        wanted, own, before, at = sources(where_ref, lookup_ref, q)

        @pl.when(own)
        def _():
            shift[q : q + 1, :] = prev_ref[pl.ds(at, 1), :]

        @pl.when(jnp.logical_not(own))
        def _():
            rows = jnp.where(
                before, pick(from_before, wanted, STATE_ROWS, TILES), pick(from_after, wanted, STATE_ROWS, TILES)
            )
            for c in range(TILES):
                shift[q : q + 1, c * 128 : (c + 1) * 128] = rows[c : c + 1, :]

    xn = jnp.concatenate(normed, axis=0)
    change = jnp.concatenate([shift[...]] + normed[:-1], axis=0) - xn

    def mix(which):
        return (xn + change * blend_ref[which : which + 1, :]).astype(BF16)

    mixed_ref[...] = mix(3)
    for n in range(3):
        loads[6 + n].wait()
        rkv_ref[n] = dot(mix(n), bufs[6 + n][...])


def step_kernel(where_ref, lookup_ref, tally_ref, mem_hbm, *refs):
    count = 10
    hbm, (part_ref, moved_ref, doubled_ref) = refs[:count], refs[count : count + 3]
    bufs = refs[count + 3 : 2 * count + 3]
    state, reads, heads, part, sems, state_sems = refs[2 * count + 3 :]
    loads = copies(hbm, bufs, sems)
    start(loads)
    state_loads = state_copies(where_ref, lookup_ref, mem_hbm, state, state_sems)
    start(state_loads)
    (
        mixed_ref, left_ref, right_ref, base_ref, boost_ref, team_ref, rkv_ref, from_before, from_after, final_ref,
    ) = bufs
    for n in range(7):
        loads[n].wait()
    tally = column_of(tally_ref, (SLOTS, 128))[:, :1]
    pre = jnp.zeros((ROWS, left_ref.shape[1]), F32)
    chunk = left_ref.shape[2]
    for n in range(left_ref.shape[0]):
        pre = pre + lax.dot_general(
            mixed_ref[:, n * chunk : (n + 1) * chunk], left_ref[n], (((1,), (1,)), ((), ())), preferred_element_type=F32
        )
    lora = jnp.tanh(pre).astype(BF16)
    decay = jnp.exp(-jnp.exp(row_of(base_ref) + dot(lora, right_ref[...])))
    r = [cut(rkv_ref[0], t) for t in range(STEPS)]
    k = [cut(rkv_ref[1], t) for t in range(STEPS)]
    v = [cut(rkv_ref[2], t) for t in range(STEPS)]
    d = [jnp.where(tally > t, cut(decay, t), 1.0) for t in range(STEPS)]
    kept = [jnp.where(tally > t, k[t], 0.0) for t in range(STEPS)]
    boost = row_of(boost_ref)

    run, reach = r[0] * 0.0 + 1.0, []
    for t in range(STEPS):
        reach.append(r[t] * run)
        run = run * d[t]
    tail, coefs = None, [None] * STEPS
    for t in reversed(range(STEPS)):
        coefs[t] = kept[t] if tail is None else kept[t] * tail
        tail = d[t] if tail is None else tail * d[t]
    pairs, terms = [], []
    for t in range(STEPS):
        pairs.append((t, t))
        terms.append(r[t] * boost * k[t])
        weight = r[t]
        for s in reversed(range(t)):
            pairs.append((t, s))
            terms.append(weight * kept[s])
            weight = weight * d[s]
    row256, col256 = iota((LOCAL, LOCAL), 0), iota((LOCAL, LOCAL), 1)
    same_head = (row256 // HEAD == col256 // HEAD).astype(BF16)
    sums = dot_split(jnp.concatenate(terms, axis=0), same_head)
    within = [None] * STEPS
    for n, (t, s) in enumerate(pairs):
        term = cut(sums, n) * v[s]
        within[t] = term if within[t] is None else within[t] + term

    source = (col256 % HEADS) * HEAD + ((col256 // HEADS) % (HEAD // 2)) * 2 + col256 // 128
    reorder = (row256 == source).astype(BF16)
    moved = dot_split(jnp.concatenate(reach + coefs + [run], axis=0), reorder)
    moved_ref[...] = moved[STEPS * SLOTS :, :]
    rowd, cold = iota((LOCAL, HEADS * 128), 0), iota((LOCAL, HEADS * 128), 1)
    double = (rowd == (cold // 128) * HEAD + cold % HEAD).astype(BF16)
    doubled_ref[...] = dot(rkv_ref[2].astype(BF16), double)

    lane = iota((SLOTS, 128), 1)
    for h in range(HEADS):
        head_lane = lane % HEADS == h
        for p in range(2):
            for t in range(STEPS):
                at = pl.ds(t * 8 + p * HEADS + h, SLOTS, stride=STEPS * 8)
                reads[at, :] = jnp.where(head_lane, cut(moved, t)[:, p * 128 : (p + 1) * 128], 0.0)
    for copy in loads[7:9] + state_loads:
        copy.wait()
    place_received(where_ref, lookup_ref, from_before, from_after, state)
    for q in range(SLOTS):
        rows = slice(q * STEPS * 8, (q + 1) * STEPS * 8)
        now = state[q * STATE_ROWS : (q + 1) * STATE_ROWS, :]
        heads[rows, :] = dot(reads[rows, :].astype(BF16), now.astype(BF16))

    outs = []
    left_half = lane < HEAD
    for t in range(STEPS):
        def read(p, h):
            return heads[pl.ds(t * 8 + p * HEADS + h, SLOTS, stride=STEPS * 8), :]

        cols = []
        for h in range(0, HEADS, 2):
            a, b, c, e = read(0, h), read(1, h), read(0, h + 1), read(1, h + 1)
            cols.append(jnp.where(left_half, a, e) + pltpu.roll(jnp.where(left_half, c, b), HEAD, 1))
        outs.append(jnp.concatenate(cols, axis=1) + within[t])
    y = jnp.concatenate(outs, axis=0)
    center = y - dot_split(y, same_head) * (1.0 / HEAD)
    spread = dot_split(center * center, same_head) * (1.0 / HEAD)
    g = (center * lax.rsqrt(spread + EPS) * row_of(team_ref)).astype(BF16)
    loads[9].wait()
    proj = dot(g, final_ref[...])
    for t in range(STEPS):
        for c in range(TILES):
            part[pl.ds(c * STEPS + t, SLOTS, stride=STEPS * TILES), :] = cut(proj, t)[:, c * 128 : (c + 1) * 128]
    part_ref[...] = part[...].astype(BF16)


def update_kernel(where_ref, lookup_ref, mem_hbm, *refs):
    count = 4
    hbm, new_hbm, bufs = refs[:count], refs[count], refs[count + 1 : 2 * count + 1]
    state, keys, vals, decays, fresh, sems, state_sems, new_sems = refs[2 * count + 1 :]
    loads = copies(hbm, bufs, sems)
    start(loads)
    state_loads = state_copies(where_ref, lookup_ref, mem_hbm, state, state_sems)
    start(state_loads)
    moved_ref, doubled_ref, from_before, from_after = bufs
    loads[0].wait()
    loads[1].wait()
    lane = iota((SLOTS, 128), 1)
    for h in range(HEADS):
        head_lane = lane % HEADS == h
        for p in range(2):
            half = lane // HEAD == p
            cols = slice(p * 128, (p + 1) * 128)
            for t in range(STEPS):
                at = pl.ds(t * 8 + p * HEADS + h, SLOTS, stride=STEPS * 8)
                keys[at, :] = jnp.where(head_lane, cut(moved_ref, t)[:, cols], 0.0)
                vals[at, :] = jnp.where(half, cut(doubled_ref, t)[:, h * 128 : (h + 1) * 128], 0.0)
            whole = jnp.where(head_lane, cut(moved_ref, STEPS)[:, cols], 0.0)
            high = whole.astype(BF16).astype(F32)
            decays[pl.ds(p * HEADS + h, SLOTS, stride=16), :] = high
            decays[pl.ds(8 + p * HEADS + h, SLOTS, stride=16), :] = whole - high
    ones = ((iota((16, 128), 0) // HEADS) % 2 == iota((16, 128), 1) // HEAD).astype(BF16)
    for copy in loads[2:] + state_loads:
        copy.wait()
    place_received(where_ref, lookup_ref, from_before, from_after, state)
    news = []
    for q in range(SLOTS):
        here = slice(q * STATE_ROWS, (q + 1) * STATE_ROWS)
        rows = slice(q * STEPS * 8, (q + 1) * STEPS * 8)
        fade = dot_rows(decays[q * 16 : (q + 1) * 16, :].astype(BF16), ones)
        grown = dot_rows(keys[rows, :].astype(BF16), vals[rows, :].astype(BF16))
        fresh[here, :] = fade * state[here, :] + grown
        news.append(pltpu.make_async_copy(fresh.at[here, :], new_hbm.at[here, :], new_sems.at[q]))
        news[-1].start()
    for copy in news:
        copy.wait()


def finish_kernel(where_ref, tally_ref, x_hbm, parts_ref, out_ref, x_ref, sem):
    rows = out_ref.shape[0]
    begin = where_ref[2] * rows
    load = pltpu.make_async_copy(x_hbm.at[pl.ds(pl.multiple_of(begin, rows), rows), :], x_ref, sem)
    load.start()
    step = iota((STEPS * TILES, 128), 0) % STEPS
    load.wait()
    for q in range(rows // (STEPS * TILES)):
        here = slice(q * STEPS * TILES, (q + 1) * STEPS * TILES)
        total = x_ref[here, :].astype(F32)
        for n in range(parts_ref.shape[0]):
            total = total + parts_ref[n, here, :].astype(F32)
        tally = tally_ref[where_ref[2] * (rows // (STEPS * TILES)) + q]
        out_ref[here, :] = jnp.where(step < tally, total, 0.0).astype(BF16)


def cost(flops, bytes_accessed):
    return pl.CostEstimate(flops=flops, bytes_accessed=bytes_accessed, transcendentals=0)


def tiles_view(a):
    lead, mid, width = a.shape
    return a.reshape(lead, mid, width // 128, 128).transpose(0, 2, 1, 3).reshape(lead * width // 128 * mid, 128)


def tiles_back(a, lead, mid, width):
    return a.reshape(lead, width // 128, mid, 128).transpose(0, 2, 1, 3).reshape(lead, mid, width)


def shards(
    layer_entry_vectors,
    tally_of_tokens,
    prior_slot_lookup,
    memory_matrices,
    previous_standardized_entries,
    entry_standardize_scale,
    blend_coefficients,
    acceptance_projection_matrix,
    lookup_projection_matrix,
    payload_projection_matrix,
    forget_map_left_matrix,
    forget_map_right_matrix,
    feature_forget_logloglevel,
    present_token_boost,
    team_standardize_scale,
    final_projection_matrix,
):
    rings = lax.axis_size("seq")
    teams = lax.axis_size("tensor")
    device = lax.axis_index("seq")
    core = lax.axis_index("tensor") % 2
    where = jnp.stack([device, (device + rings - 1) % rings, core]).astype(jnp.int32)
    x = tiles_view(layer_entry_vectors)
    mem = tiles_view(memory_matrices)
    prev = previous_standardized_entries
    lookup, tally = prior_slot_lookup, tally_of_tokens
    left_t = forget_map_left_matrix.T
    shape, scratch, dma = jax.ShapeDtypeStruct, pltpu.VMEM, pltpu.SemaphoreType.DMA
    params = lambda mib: pltpu.CompilerParams(vmem_limit_bytes=mib << 20)
    like = lambda items: [scratch(a.shape, a.dtype) for a in items]
    state_buf = scratch((SLOTS * STATE_ROWS, 128), F32)
    rows_buf = scratch((SLOTS * STEPS * 8, 128), F32)

    packed, left = pl.pallas_call(
        pack_kernel,
        out_shape=[shape((PACK_ROWS, 128), F32), shape((teams,) + left_t.shape, BF16)],
        in_specs=spec(pltpu.SMEM, 1) + spec(pl.ANY, 4),
        out_specs=spec(pl.ANY, 2),
        scratch_shapes=[
            pltpu.SMEM(lookup.shape, jnp.int32), scratch(prev.shape, F32), scratch(left_t.shape, BF16),
            scratch((PACK_ROWS, 128), F32), dma((8 + teams,)),
        ],
        compiler_params=params(PACK_MIB),
        cost_estimate=cost(0, 1 << 20),
        name="pack",
    )(where, lookup, mem, prev, left_t)
    from_before = lax.ppermute(packed, "seq", [(i, (i + 1) % rings) for i in range(rings)])
    from_after = lax.ppermute(packed, "seq", [((i + 1) % rings, i) for i in range(rings)])
    left = lax.all_to_all(left, "tensor", 0, 0)

    operands = [
        x, entry_standardize_scale.reshape(TILES, 128), prev, from_before, from_after, blend_coefficients,
        acceptance_projection_matrix, lookup_projection_matrix, payload_projection_matrix,
    ]
    rkv, mixed_rows, new_shifts = pl.pallas_call(
        project_kernel,
        out_shape=[shape((3, ROWS, LOCAL), F32), shape((ROWS, WIDTH), BF16), shape((SLOTS, WIDTH), F32)],
        in_specs=spec(pltpu.SMEM, 3) + spec(pl.ANY, len(operands)),
        out_specs=spec(pltpu.VMEM, 3),
        scratch_shapes=like(operands)
        + [scratch((ROWS * TILES, 128), F32), scratch((SLOTS, WIDTH), F32), dma((len(operands),))],
        compiler_params=params(MAIN_MIB),
        cost_estimate=cost(6 * ROWS * WIDTH * LOCAL, 8 << 20),
        name="project",
    )(where, lookup, tally, *operands)

    operands = [
        mixed_rows, left, forget_map_right_matrix, feature_forget_logloglevel.reshape(2, 128),
        present_token_boost.reshape(2, 128), team_standardize_scale.reshape(2, 128), rkv, from_before, from_after,
        final_projection_matrix,
    ]
    part, moved, doubled = pl.pallas_call(
        step_kernel,
        out_shape=[
            shape((ROWS * TILES, 128), BF16), shape((ROWS + SLOTS, LOCAL), F32), shape((ROWS, HEADS * 128), F32),
        ],
        in_specs=spec(pltpu.SMEM, 3) + spec(pl.ANY, 1 + len(operands)),
        out_specs=spec(pltpu.VMEM, 3),
        scratch_shapes=like(operands)
        + [state_buf, rows_buf, rows_buf, scratch((ROWS * TILES, 128), F32), dma((len(operands),)), dma((SLOTS,))],
        compiler_params=params(MAIN_MIB),
        cost_estimate=cost(2 * ROWS * WIDTH * LOCAL, 4 << 20),
        name="step",
    )(where, lookup, tally, mem, *operands)

    operands = [moved, doubled, from_before, from_after]
    new_states = pl.pallas_call(
        update_kernel,
        out_shape=shape((SLOTS * STATE_ROWS, 128), F32),
        in_specs=spec(pltpu.SMEM, 2) + spec(pl.ANY, 1 + len(operands)),
        out_specs=spec(pl.ANY, 1)[0],
        scratch_shapes=like(operands)
        + [state_buf, rows_buf, rows_buf, scratch((SLOTS * 16, 128), F32), state_buf]
        + [dma((len(operands),)), dma((SLOTS,)), dma((SLOTS,))],
        compiler_params=params(MAIN_MIB),
        cost_estimate=cost(1 << 24, 8 << 20),
        name="update",
    )(where, lookup, mem, *operands)

    pairs = [[2 * i, 2 * i + 1] for i in range(teams // 2)]
    chips = [[2 * i + c for i in range(teams // 2)] for c in range(2)]
    half = ROWS * TILES // 2
    both = lax.all_gather(part, "tensor", axis_index_groups=pairs, tiled=False)
    mine = lax.dynamic_slice_in_dim(both, core * half, half, 1).astype(F32).sum(0).astype(BF16)
    spread = lax.all_to_all(
        jnp.broadcast_to(mine[None], (teams // 2,) + mine.shape), "tensor", 0, 0, axis_index_groups=chips
    )
    mixed = pl.pallas_call(
        finish_kernel,
        out_shape=shape((half, 128), BF16),
        in_specs=spec(pltpu.SMEM, 2) + spec(pl.ANY, 1) + spec(pltpu.VMEM, 1),
        out_specs=spec(pltpu.VMEM, 1)[0],
        scratch_shapes=[scratch((half, 128), BF16), dma],
        compiler_params=params(8),
        cost_estimate=cost(0, 1 << 19),
        name="finish",
    )(where, tally, x, spread)
    mixed = tiles_back(mixed, SLOTS // 2, STEPS, WIDTH)
    mixed = lax.all_gather(mixed, "tensor", axis_index_groups=pairs, tiled=True)
    return (
        mixed,
        tiles_back(new_states, SLOTS, HEADS, HEAD * HEAD),
        new_shifts,
    )


def solution(mesh):
    in_specs = (
        P("seq", None, None),
        P("seq"),
        P("seq"),
        P("seq", "tensor", None),
        P("seq", None),
        P(),
        P(),
        P(None, "tensor"),
        P(None, "tensor"),
        P(None, "tensor"),
        P("tensor", None),
        P(None, "tensor"),
        P("tensor"),
        P("tensor"),
        P("tensor"),
        P("tensor", None),
    )
    out_specs = (P("seq", None, None), P("seq", "tensor", None), P("seq", None))
    return jax.shard_map(shards, mesh=mesh, in_specs=in_specs, out_specs=out_specs, check_vma=False)
```

```python
import functools

import jax
import jax.numpy as jnp
from jax import lax
from jax.experimental import pallas as pl
from jax.experimental.pallas import tpu as pltpu
from jax.sharding import PartitionSpec as P

EPS = 1e-05
F32 = jnp.float32
BF16 = jnp.bfloat16
HEAD = 64
SLOTS = 16
STEPS = 4
WIDTH = 2048
HEADS = 4
LOCAL = HEADS * HEAD
TILES = WIDTH // 128
ROWS = SLOTS * STEPS
STATE_ROWS = HEADS * HEAD * HEAD // 128
PIECE = STATE_ROWS + TILES
PACK_ROWS = 2 * PIECE + 8
PACK_MIB, MAIN_MIB = 60, 52


def spec(space, count):
    return [pl.BlockSpec(memory_space=space)] * count


def dot(a, b):
    return jnp.dot(a, b, preferred_element_type=F32)


def dot_rows(a, b):
    return lax.dot_general(a, b, (((0,), (0,)), ((), ())), preferred_element_type=F32)


def split(a):
    hi = a.astype(BF16)
    return hi, (a - hi.astype(F32)).astype(BF16)


def dot_split(a, b):
    hi, lo = split(a)
    return dot(hi, b) + dot(lo, b)


def iota(shape, dim):
    return lax.broadcasted_iota(jnp.int32, shape, dim)


def column_of(tally_ref, shape):
    rows = iota(shape, 0)
    out = jnp.zeros(shape, jnp.int32)
    for q in range(SLOTS):
        out = jnp.where(rows == q, tally_ref[q], out)
    return out


def row_of(ref):
    return jnp.concatenate([ref[i : i + 1, :] for i in range(ref.shape[0])], axis=1)


def start(items):
    for copy in items:
        copy.start()


def place():
    count = lax.axis_size("seq")
    me = lax.axis_index("seq")
    return me, jnp.where(me == 0, count - 1, me - 1)


def pack_kernel(lookup_hbm, mem_hbm, prev_hbm, left_hbm, out_ref, left_out, lookup_ref, mem, prev, left, sems):
    loads = copies(
        (lookup_hbm, left_hbm, prev_hbm, mem_hbm), (lookup_ref, left, prev, mem), sems
    )
    start(loads)
    first = place()[0] * SLOTS
    loads[1].wait()
    spread = [pltpu.make_async_copy(left, left_out.at[n], sems.at[4 + n]) for n in range(left_out.shape[0])]
    start(spread)
    loads[0].wait()
    kept = jnp.int32(0)
    for q in range(SLOTS):
        at = lookup_ref[q] - first
        own = (at >= 0) & (at < SLOTS)
        kept = kept | jnp.where(own, jnp.int32(1) << jnp.where(own, at, 0), 0)
    low, high = jnp.int32(0), jnp.int32(0)
    for s in range(SLOTS):
        high = jnp.where((kept >> s) & 1 == 0, s, high)
        low = jnp.where((kept >> (SLOTS - 1 - s)) & 1 == 0, SLOTS - 1 - s, low)
    out_ref[2 * PIECE :, :] = jnp.where(iota((8, 128), 0) == 0, first + low, first + high).astype(F32)
    loads[2].wait()
    for n, slot in enumerate((low, high)):
        row = prev[pl.ds(slot, 1), :]
        at = n * PIECE + STATE_ROWS
        for c in range(TILES):
            out_ref[at + c : at + c + 1, :] = row[:, c * 128 : (c + 1) * 128]
    loads[3].wait()
    for n, slot in enumerate((low, high)):
        begin = pl.multiple_of(slot * STATE_ROWS, STATE_ROWS)
        out_ref[n * PIECE : n * PIECE + STATE_ROWS, :] = mem[pl.ds(begin, STATE_ROWS), :]
    for copy in spread:
        copy.wait()


def pick(recv_ref, wanted, begin, count):
    is_low = recv_ref[2 * PIECE : 2 * PIECE + 1, :] == wanted.astype(F32)
    return jnp.where(is_low, recv_ref[begin : begin + count, :], recv_ref[PIECE + begin : PIECE + begin + count, :])


def sources(where, lookup_ref, q):
    wanted = lookup_ref[q]
    owner = wanted // SLOTS
    own = owner == where[0]
    before = owner == where[1]
    at = jnp.where(own, wanted - where[0] * SLOTS, 0)
    return wanted, own, before, at


def copies(sources_, targets, sems):
    return [pltpu.make_async_copy(a, b, sems.at[n]) for n, (a, b) in enumerate(zip(sources_, targets))]


def state_copies(where, lookup_ref, mem_hbm, state, sems):
    out = []
    for q in range(SLOTS):
        at = sources(where, lookup_ref, q)[3]
        out.append(
            pltpu.make_async_copy(
                mem_hbm.at[pl.ds(pl.multiple_of(at * STATE_ROWS, STATE_ROWS), STATE_ROWS), :],
                state.at[pl.ds(q * STATE_ROWS, STATE_ROWS), :],
                sems.at[q],
            )
        )
    return out


def place_received(where, lookup_ref, from_before, from_after, state):
    for q in range(SLOTS):
        wanted, own, before, _ = sources(where, lookup_ref, q)
        here = slice(q * STATE_ROWS, (q + 1) * STATE_ROWS)

        @pl.when(jnp.logical_not(own) & before)
        def _():
            state[here, :] = pick(from_before, wanted, 0, STATE_ROWS)

        @pl.when(jnp.logical_not(own) & jnp.logical_not(before))
        def _():
            state[here, :] = pick(from_after, wanted, 0, STATE_ROWS)


def cut(a, t):
    return a[t * SLOTS : (t + 1) * SLOTS, :]


def norm_kernel(tally_ref, x_hbm, gain_hbm, xn_ref, last_ref, x_ref, gain_ref, x32, sems):
    loads = copies((x_hbm, gain_hbm), (x_ref, gain_ref), sems)
    start(loads)
    loads[0].wait()
    loads[1].wait()
    x32[...] = x_ref[...].astype(F32)
    gain = row_of(gain_ref)
    normed = []
    for t in range(STEPS):
        row = jnp.concatenate([x32[pl.ds(c * STEPS + t, SLOTS, stride=STEPS * TILES), :] for c in range(TILES)], axis=1)
        center = row - jnp.mean(row, axis=-1, keepdims=True)
        spread = jnp.mean(center * center, axis=-1, keepdims=True)
        normed.append(center * lax.rsqrt(spread + EPS) * gain)
    tally = column_of(tally_ref, (SLOTS, 128))[:, :1]
    last = normed[0]
    for t in range(1, STEPS):
        last = jnp.where(tally == t + 1, normed[t], last)
    last_ref[...] = last
    for t in range(STEPS):
        xn_ref[t * SLOTS : (t + 1) * SLOTS, :] = normed[t]


def main_kernel(lookup_ref, tally_ref, mem_hbm, *refs):
    count = 14
    hbm, (part_ref, moved_ref, doubled_ref) = refs[:count], refs[count : count + 3]
    bufs = refs[count + 3 : 2 * count + 3]
    shift, state, reads, heads, part, sems, state_sems = refs[2 * count + 3 :]
    where = place()
    loads = copies(hbm, bufs, sems)
    start(loads[:-1])
    state_loads = state_copies(where, lookup_ref, mem_hbm, state, state_sems)
    start(state_loads)
    loads[-1].start()
    xn_ref, prev_ref, from_before, from_after, blend_ref = bufs[:5]
    left_ref, right_ref, base_ref, boost_ref, team_ref, final_ref = bufs[8:]
    tally = column_of(tally_ref, (SLOTS, 128))[:, :1]
    for n in range(5):
        loads[n].wait()
    for q in range(SLOTS):
        wanted, own, before, at = sources(where, lookup_ref, q)

        @pl.when(own)
        def _():
            shift[q : q + 1, :] = prev_ref[pl.ds(at, 1), :]

        @pl.when(jnp.logical_not(own))
        def _():
            rows = jnp.where(
                before, pick(from_before, wanted, STATE_ROWS, TILES), pick(from_after, wanted, STATE_ROWS, TILES)
            )
            for c in range(TILES):
                shift[q : q + 1, c * 128 : (c + 1) * 128] = rows[c : c + 1, :]

    xn = xn_ref[...]
    change = jnp.concatenate([shift[...], xn[: (STEPS - 1) * SLOTS, :]], axis=0) - xn

    def mix(which):
        return (xn + change * blend_ref[which : which + 1, :]).astype(BF16)

    mixed_rows = mix(3)
    rkv = []
    for n in range(3):
        loads[5 + n].wait()
        rkv.append(dot(mix(n), bufs[5 + n][...]))
    for n in range(8, 13):
        loads[n].wait()
    pre = jnp.zeros((ROWS, left_ref.shape[1]), F32)
    chunk = left_ref.shape[2]
    for n in range(left_ref.shape[0]):
        pre = pre + lax.dot_general(
            mixed_rows[:, n * chunk : (n + 1) * chunk], left_ref[n], (((1,), (1,)), ((), ())), preferred_element_type=F32
        )
    lora = jnp.tanh(pre).astype(BF16)
    decay = jnp.exp(-jnp.exp(row_of(base_ref) + dot(lora, right_ref[...])))
    r = [cut(rkv[0], t) for t in range(STEPS)]
    k = [cut(rkv[1], t) for t in range(STEPS)]
    v = [cut(rkv[2], t) for t in range(STEPS)]
    d = [jnp.where(tally > t, cut(decay, t), 1.0) for t in range(STEPS)]
    kept = [jnp.where(tally > t, k[t], 0.0) for t in range(STEPS)]
    boost = row_of(boost_ref)

    run, reach = r[0] * 0.0 + 1.0, []
    for t in range(STEPS):
        reach.append(r[t] * run)
        run = run * d[t]
    tail, coefs = None, [None] * STEPS
    for t in reversed(range(STEPS)):
        coefs[t] = kept[t] if tail is None else kept[t] * tail
        tail = d[t] if tail is None else tail * d[t]
    pairs, terms = [], []
    for t in range(STEPS):
        pairs.append((t, t))
        terms.append(r[t] * boost * k[t])
        weight = r[t]
        for s in reversed(range(t)):
            pairs.append((t, s))
            terms.append(weight * kept[s])
            weight = weight * d[s]
    row256, col256 = iota((LOCAL, LOCAL), 0), iota((LOCAL, LOCAL), 1)
    same_head = (row256 // HEAD == col256 // HEAD).astype(BF16)
    sums = dot_split(jnp.concatenate(terms, axis=0), same_head)
    within = [None] * STEPS
    for n, (t, s) in enumerate(pairs):
        term = cut(sums, n) * v[s]
        within[t] = term if within[t] is None else within[t] + term

    source = (col256 % HEADS) * HEAD + ((col256 // HEADS) % (HEAD // 2)) * 2 + col256 // 128
    reorder = (row256 == source).astype(BF16)
    moved = dot_split(jnp.concatenate(reach + coefs + [run], axis=0), reorder)
    moved_ref[...] = moved[STEPS * SLOTS :, :]
    rowd, cold = iota((LOCAL, HEADS * 128), 0), iota((LOCAL, HEADS * 128), 1)
    double = (rowd == (cold // 128) * HEAD + cold % HEAD).astype(BF16)
    doubled_ref[...] = dot(rkv[2].astype(BF16), double)

    lane = iota((SLOTS, 128), 1)
    for h in range(HEADS):
        head_lane = lane % HEADS == h
        for p in range(2):
            for t in range(STEPS):
                at = pl.ds(t * 8 + p * HEADS + h, SLOTS, stride=STEPS * 8)
                reads[at, :] = jnp.where(head_lane, cut(moved, t)[:, p * 128 : (p + 1) * 128], 0.0)
    for copy in state_loads:
        copy.wait()
    place_received(where, lookup_ref, from_before, from_after, state)
    for q in range(SLOTS):
        rows = slice(q * STEPS * 8, (q + 1) * STEPS * 8)
        now = state[q * STATE_ROWS : (q + 1) * STATE_ROWS, :]
        heads[rows, :] = dot(reads[rows, :].astype(BF16), now.astype(BF16))

    outs = []
    left_half = lane < HEAD
    for t in range(STEPS):
        def read(p, h):
            return heads[pl.ds(t * 8 + p * HEADS + h, SLOTS, stride=STEPS * 8), :]

        cols = []
        for h in range(0, HEADS, 2):
            a, b, c, e = read(0, h), read(1, h), read(0, h + 1), read(1, h + 1)
            cols.append(jnp.where(left_half, a, e) + pltpu.roll(jnp.where(left_half, c, b), HEAD, 1))
        outs.append(jnp.concatenate(cols, axis=1) + within[t])
    y = jnp.concatenate(outs, axis=0)
    center = y - dot_split(y, same_head) * (1.0 / HEAD)
    spread = dot_split(center * center, same_head) * (1.0 / HEAD)
    g = (center * lax.rsqrt(spread + EPS) * row_of(team_ref)).astype(BF16)
    loads[13].wait()
    proj = dot(g, final_ref[...])
    for t in range(STEPS):
        for c in range(TILES):
            part[pl.ds(c * STEPS + t, SLOTS, stride=STEPS * TILES), :] = cut(proj, t)[:, c * 128 : (c + 1) * 128]
    part_ref[...] = part[...].astype(BF16)


def update_kernel(lookup_ref, mem_hbm, *refs):
    count = 4
    hbm, new_hbm, bufs = refs[:count], refs[count], refs[count + 1 : 2 * count + 1]
    state, keys, vals, decays, fresh, sems, state_sems, new_sems = refs[2 * count + 1 :]
    where = place()
    loads = copies(hbm, bufs, sems)
    start(loads)
    state_loads = state_copies(where, lookup_ref, mem_hbm, state, state_sems)
    start(state_loads)
    moved_ref, doubled_ref, from_before, from_after = bufs
    loads[0].wait()
    loads[1].wait()
    lane = iota((SLOTS, 128), 1)
    for h in range(HEADS):
        head_lane = lane % HEADS == h
        for p in range(2):
            half = lane // HEAD == p
            cols = slice(p * 128, (p + 1) * 128)
            for t in range(STEPS):
                at = pl.ds(t * 8 + p * HEADS + h, SLOTS, stride=STEPS * 8)
                keys[at, :] = jnp.where(head_lane, cut(moved_ref, t)[:, cols], 0.0)
                vals[at, :] = jnp.where(half, cut(doubled_ref, t)[:, h * 128 : (h + 1) * 128], 0.0)
            whole = jnp.where(head_lane, cut(moved_ref, STEPS)[:, cols], 0.0)
            high = whole.astype(BF16).astype(F32)
            decays[pl.ds(p * HEADS + h, SLOTS, stride=16), :] = high
            decays[pl.ds(8 + p * HEADS + h, SLOTS, stride=16), :] = whole - high
    ones = ((iota((16, 128), 0) // HEADS) % 2 == iota((16, 128), 1) // HEAD).astype(BF16)
    for copy in loads[2:] + state_loads:
        copy.wait()
    place_received(where, lookup_ref, from_before, from_after, state)
    news = []
    for q in range(SLOTS):
        here = slice(q * STATE_ROWS, (q + 1) * STATE_ROWS)
        rows = slice(q * STEPS * 8, (q + 1) * STEPS * 8)
        fade = dot_rows(decays[q * 16 : (q + 1) * 16, :].astype(BF16), ones)
        grown = dot_rows(keys[rows, :].astype(BF16), vals[rows, :].astype(BF16))
        fresh[here, :] = fade * state[here, :] + grown
        news.append(pltpu.make_async_copy(fresh.at[here, :], new_hbm.at[here, :], new_sems.at[q]))
        news[-1].start()
    for copy in news:
        copy.wait()


def finish_kernel(tally_ref, x_hbm, parts_ref, out_ref, x_ref, sem):
    rows = out_ref.shape[0]
    core = lax.axis_index("tensor") % 2
    begin = core * rows
    load = pltpu.make_async_copy(x_hbm.at[pl.ds(pl.multiple_of(begin, rows), rows), :], x_ref, sem)
    load.start()
    step = iota((STEPS * TILES, 128), 0) % STEPS
    load.wait()
    for q in range(rows // (STEPS * TILES)):
        here = slice(q * STEPS * TILES, (q + 1) * STEPS * TILES)
        total = x_ref[here, :].astype(F32)
        for n in range(parts_ref.shape[0]):
            total = total + parts_ref[n, here, :].astype(F32)
        tally = tally_ref[core * (rows // (STEPS * TILES)) + q]
        out_ref[here, :] = jnp.where(step < tally, total, 0.0).astype(BF16)


def cost(flops, bytes_accessed):
    return pl.CostEstimate(flops=flops, bytes_accessed=bytes_accessed, transcendentals=0)


def tiles_view(a):
    lead, mid, width = a.shape
    return a.reshape(lead, mid, width // 128, 128).transpose(0, 2, 1, 3).reshape(lead * width // 128 * mid, 128)


def tiles_back(a, lead, mid, width):
    return a.reshape(lead, width // 128, mid, 128).transpose(0, 2, 1, 3).reshape(lead, mid, width)


def shards(
    layer_entry_vectors,
    tally_of_tokens,
    prior_slot_lookup,
    memory_matrices,
    previous_standardized_entries,
    entry_standardize_scale,
    blend_coefficients,
    acceptance_projection_matrix,
    lookup_projection_matrix,
    payload_projection_matrix,
    forget_map_left_matrix,
    forget_map_right_matrix,
    feature_forget_logloglevel,
    present_token_boost,
    team_standardize_scale,
    final_projection_matrix,
):
    rings = lax.axis_size("seq")
    teams = lax.axis_size("tensor")
    core = lax.axis_index("tensor") % 2
    x = tiles_view(layer_entry_vectors)
    mem = tiles_view(memory_matrices)
    prev = previous_standardized_entries
    lookup, tally = prior_slot_lookup, tally_of_tokens
    left_t = forget_map_left_matrix.T
    shape, scratch, dma = jax.ShapeDtypeStruct, pltpu.VMEM, pltpu.SemaphoreType.DMA
    params = lambda mib: pltpu.CompilerParams(vmem_limit_bytes=mib << 20)
    like = lambda items: [scratch(a.shape, a.dtype) for a in items]
    state_buf = scratch((SLOTS * STATE_ROWS, 128), F32)
    rows_buf = scratch((SLOTS * STEPS * 8, 128), F32)

    packed, left = pl.pallas_call(
        pack_kernel,
        out_shape=[shape((PACK_ROWS, 128), F32), shape((teams,) + left_t.shape, BF16)],
        in_specs=spec(pl.ANY, 4),
        out_specs=spec(pltpu.VMEM, 1) + spec(pl.ANY, 1),
        scratch_shapes=[pltpu.SMEM(lookup.shape, jnp.int32)] + like([mem, prev, left_t]) + [dma((4 + teams,))],
        compiler_params=params(PACK_MIB),
        cost_estimate=cost(0, 1 << 20),
        name="pack",
    )(lookup, mem, prev, left_t)
    from_before = lax.ppermute(packed, "seq", [(i, (i + 1) % rings) for i in range(rings)])
    from_after = lax.ppermute(packed, "seq", [((i + 1) % rings, i) for i in range(rings)])
    left = lax.all_to_all(left, "tensor", 0, 0)

    gain = entry_standardize_scale.reshape(TILES, 128)
    xn, new_shifts = pl.pallas_call(
        norm_kernel,
        out_shape=[shape((ROWS, WIDTH), F32), shape((SLOTS, WIDTH), F32)],
        in_specs=spec(pltpu.SMEM, 1) + spec(pl.ANY, 2),
        out_specs=spec(pltpu.VMEM, 2),
        scratch_shapes=like([x, gain]) + [scratch((ROWS * TILES, 128), F32), dma((2,))],
        compiler_params=params(MAIN_MIB),
        cost_estimate=cost(0, 4 << 20),
        name="norm",
    )(tally, x, gain)

    operands = [
        xn, prev, from_before, from_after, blend_coefficients,
        acceptance_projection_matrix, lookup_projection_matrix, payload_projection_matrix,
        left, forget_map_right_matrix, feature_forget_logloglevel.reshape(2, 128),
        present_token_boost.reshape(2, 128), team_standardize_scale.reshape(2, 128), final_projection_matrix,
    ]
    part, moved, doubled = pl.pallas_call(
        main_kernel,
        out_shape=[
            shape((ROWS * TILES, 128), BF16), shape((ROWS + SLOTS, LOCAL), F32), shape((ROWS, HEADS * 128), F32),
        ],
        in_specs=spec(pltpu.SMEM, 2) + spec(pl.ANY, 1 + len(operands)),
        out_specs=spec(pltpu.VMEM, 3),
        scratch_shapes=like(operands)
        + [scratch((SLOTS, WIDTH), F32), state_buf, rows_buf, rows_buf, scratch((ROWS * TILES, 128), F32)]
        + [dma((len(operands),)), dma((SLOTS,))],
        compiler_params=params(MAIN_MIB),
        cost_estimate=cost(8 * ROWS * WIDTH * LOCAL, 8 << 20),
        name="main",
    )(lookup, tally, mem, *operands)

    operands = [moved, doubled, from_before, from_after]
    new_states = pl.pallas_call(
        update_kernel,
        out_shape=shape((SLOTS * STATE_ROWS, 128), F32),
        in_specs=spec(pltpu.SMEM, 1) + spec(pl.ANY, 1 + len(operands)),
        out_specs=spec(pl.ANY, 1)[0],
        scratch_shapes=like(operands)
        + [state_buf, rows_buf, rows_buf, scratch((SLOTS * 16, 128), F32), state_buf]
        + [dma((len(operands),)), dma((SLOTS,)), dma((SLOTS,))],
        compiler_params=params(MAIN_MIB),
        cost_estimate=cost(1 << 24, 8 << 20),
        name="update",
    )(lookup, mem, *operands)

    pairs = [[2 * i, 2 * i + 1] for i in range(teams // 2)]
    chips = [[2 * i + c for i in range(teams // 2)] for c in range(2)]
    half = ROWS * TILES // 2
    both = lax.all_gather(part, "tensor", axis_index_groups=pairs, tiled=False)
    mine = lax.dynamic_slice_in_dim(both, core * half, half, 1).astype(F32).sum(0).astype(BF16)
    spread = lax.all_to_all(
        jnp.broadcast_to(mine[None], (teams // 2,) + mine.shape), "tensor", 0, 0, axis_index_groups=chips
    )
    mixed = pl.pallas_call(
        finish_kernel,
        out_shape=shape((half, 128), BF16),
        in_specs=spec(pltpu.SMEM, 1) + spec(pl.ANY, 1) + spec(pltpu.VMEM, 1),
        out_specs=spec(pltpu.VMEM, 1)[0],
        scratch_shapes=[scratch((half, 128), BF16), dma],
        compiler_params=params(8),
        cost_estimate=cost(0, 1 << 19),
        name="finish",
    )(tally, x, spread)
    mixed = tiles_back(mixed, SLOTS // 2, STEPS, WIDTH)
    mixed = lax.all_gather(mixed, "tensor", axis_index_groups=pairs, tiled=True)
    return (
        mixed,
        tiles_back(new_states, SLOTS, HEADS, HEAD * HEAD),
        new_shifts,
    )


def solution(mesh):
    in_specs = (
        P("seq", None, None),
        P("seq"),
        P("seq"),
        P("seq", "tensor", None),
        P("seq", None),
        P(),
        P(),
        P(None, "tensor"),
        P(None, "tensor"),
        P(None, "tensor"),
        P("tensor", None),
        P(None, "tensor"),
        P("tensor"),
        P("tensor"),
        P("tensor"),
        P("tensor", None),
    )
    out_specs = (P("seq", None, None), P("seq", "tensor", None), P("seq", None))
    return jax.shard_map(shards, mesh=mesh, in_specs=in_specs, out_specs=out_specs, check_vma=False)
```

```python
import functools

import jax
import jax.numpy as jnp
from jax import lax
from jax.experimental import pallas as pl
from jax.experimental.pallas import tpu as pltpu
from jax.sharding import PartitionSpec as P

EPS = 1e-05
F32 = jnp.float32
BF16 = jnp.bfloat16
HEAD = 64
SLOTS = 16
STEPS = 4
WIDTH = 2048
HEADS = 4
LOCAL = HEADS * HEAD
TILES = WIDTH // 128
ROWS = SLOTS * STEPS
STATE_ROWS = HEADS * HEAD * HEAD // 128
PIECE = STATE_ROWS + TILES
PACK_ROWS = 2 * PIECE + 16
PACK_MIB, MAIN_MIB = 60, 52


def spec(space, count):
    return [pl.BlockSpec(memory_space=space)] * count


def dot(a, b):
    return jnp.dot(a, b, preferred_element_type=F32)


def dot_rows(a, b):
    return lax.dot_general(a, b, (((0,), (0,)), ((), ())), preferred_element_type=F32)


def split(a):
    hi = a.astype(BF16)
    return hi, (a - hi.astype(F32)).astype(BF16)


def dot_split(a, b):
    hi, lo = split(a)
    return dot(hi, b) + dot(lo, b)


def iota(shape, dim):
    return lax.broadcasted_iota(jnp.int32, shape, dim)


def column_of(tally_ref, shape):
    rows = iota(shape, 0)
    out = jnp.zeros(shape, jnp.int32)
    for q in range(SLOTS):
        out = jnp.where(rows == q, tally_ref[q], out)
    return out


def row_of(ref):
    return jnp.concatenate([ref[i : i + 1, :] for i in range(ref.shape[0])], axis=1)


def start(items):
    for copy in items:
        copy.start()


def place():
    count = lax.axis_size("seq")
    me = lax.axis_index("seq")
    return me, jnp.where(me == 0, count - 1, me - 1)


def pack_kernel(lookup_hbm, prev_hbm, mem_hbm, left_hbm, out_ref, left_out, lookup_ref, prev, mem, left, tile, sems):
    loads = copies((lookup_hbm, prev_hbm, mem_hbm, left_hbm), (lookup_ref, prev, mem, left), sems)
    start(loads)
    first = place()[0] * SLOTS
    loads[3].wait()
    sends = [pltpu.make_async_copy(left, left_out.at[n], sems.at[4 + n]) for n in range(left_out.shape[0])]
    start(sends)
    loads[0].wait()
    kept = jnp.int32(0)
    for q in range(SLOTS):
        at = lookup_ref[q] - first
        own = (at >= 0) & (at < SLOTS)
        kept = kept | jnp.where(own, jnp.int32(1) << jnp.where(own, at, 0), 0)
    low, high = jnp.int32(0), jnp.int32(0)
    for s in range(SLOTS):
        high = jnp.where((kept >> s) & 1 == 0, s, high)
        low = jnp.where((kept >> (SLOTS - 1 - s)) & 1 == 0, SLOTS - 1 - s, low)
    out_ref[2 * PIECE :, :] = jnp.full((16, 128), low, jnp.int32).astype(F32).astype(BF16)
    loads[1].wait()
    for n, slot in enumerate((low, high)):
        row = prev[pl.ds(slot, 1), :]
        for c in range(TILES):
            tile[n * TILES + c : n * TILES + c + 1, :] = row[:, c * 128 : (c + 1) * 128]
    loads[2].wait()
    for n, slot in enumerate((low, high)):
        begin = pl.multiple_of(slot * STATE_ROWS, STATE_ROWS)
        out_ref[n * PIECE : n * PIECE + STATE_ROWS, :] = mem[pl.ds(begin, STATE_ROWS), :].astype(BF16)
        out_ref[n * PIECE + STATE_ROWS : (n + 1) * PIECE, :] = tile[n * TILES : (n + 1) * TILES, :].astype(BF16)
    for copy in sends:
        copy.wait()


def pick(recv_ref, wanted, begin, count):
    low = recv_ref[2 * PIECE :, :].astype(F32)[:1, :]
    is_low = low == (wanted % SLOTS).astype(F32)
    rows = [recv_ref[at : at + count, :].astype(F32) for at in (begin, PIECE + begin)]
    return jnp.where(is_low, rows[0], rows[1])


def sources(where, lookup_ref, q):
    wanted = lookup_ref[q]
    owner = wanted // SLOTS
    own = owner == where[0]
    before = owner == where[1]
    at = jnp.where(own, wanted - where[0] * SLOTS, 0)
    return wanted, own, before, at


def copies(sources_, targets, sems):
    return [pltpu.make_async_copy(a, b, sems.at[n]) for n, (a, b) in enumerate(zip(sources_, targets))]


def state_copies(where, lookup_ref, mem_hbm, state, sems):
    out = []
    for q in range(SLOTS):
        at = sources(where, lookup_ref, q)[3]
        out.append(
            pltpu.make_async_copy(
                mem_hbm.at[pl.ds(pl.multiple_of(at * STATE_ROWS, STATE_ROWS), STATE_ROWS), :],
                state.at[pl.ds(q * STATE_ROWS, STATE_ROWS), :],
                sems.at[q],
            )
        )
    return out


def place_received(where, lookup_ref, from_before, from_after, state):
    for q in range(SLOTS):
        wanted, own, before, _ = sources(where, lookup_ref, q)
        here = slice(q * STATE_ROWS, (q + 1) * STATE_ROWS)

        @pl.when(jnp.logical_not(own) & before)
        def _():
            state[here, :] = pick(from_before, wanted, 0, STATE_ROWS)

        @pl.when(jnp.logical_not(own) & jnp.logical_not(before))
        def _():
            state[here, :] = pick(from_after, wanted, 0, STATE_ROWS)


def cut(a, t):
    return a[t * SLOTS : (t + 1) * SLOTS, :]


def norm_kernel(tally_ref, x_hbm, gain_hbm, xn_ref, last_ref, x_ref, gain_ref, x32, sems):
    loads = copies((x_hbm, gain_hbm), (x_ref, gain_ref), sems)
    start(loads)
    loads[0].wait()
    loads[1].wait()
    x32[...] = x_ref[...].astype(F32)
    gain = row_of(gain_ref)
    normed = []
    for t in range(STEPS):
        row = jnp.concatenate([x32[pl.ds(c * STEPS + t, SLOTS, stride=STEPS * TILES), :] for c in range(TILES)], axis=1)
        center = row - jnp.mean(row, axis=-1, keepdims=True)
        spread = jnp.mean(center * center, axis=-1, keepdims=True)
        normed.append(center * lax.rsqrt(spread + EPS) * gain)
    tally = column_of(tally_ref, (SLOTS, 128))[:, :1]
    last = normed[0]
    for t in range(1, STEPS):
        last = jnp.where(tally == t + 1, normed[t], last)
    last_ref[...] = last
    for t in range(STEPS):
        xn_ref[t * SLOTS : (t + 1) * SLOTS, :] = normed[t]


def main_kernel(lookup_ref, tally_ref, mem_hbm, *refs):
    count = 14
    hbm, (part_ref, moved_ref, vals_ref) = refs[:count], refs[count : count + 3]
    bufs = refs[count + 3 : 2 * count + 3]
    shift, state, reads, heads, part, sems, state_sems = refs[2 * count + 3 :]
    where = place()
    loads = copies(hbm, bufs, sems)
    start(loads[:-1])
    state_loads = state_copies(where, lookup_ref, mem_hbm, state, state_sems)
    start(state_loads)
    loads[-1].start()
    xn_ref, prev_ref, from_after, from_before, blend_ref = bufs[:5]
    left_ref, right_ref, base_ref, boost_ref, team_ref, final_ref = bufs[8:]
    tally = column_of(tally_ref, (SLOTS, 128))[:, :1]
    for n in range(5):
        loads[n].wait()
    for q in range(SLOTS):
        wanted, own, before, at = sources(where, lookup_ref, q)

        @pl.when(own)
        def _():
            shift[q : q + 1, :] = prev_ref[pl.ds(at, 1), :]

        @pl.when(jnp.logical_not(own))
        def _():
            rows = jnp.where(
                before, pick(from_before, wanted, STATE_ROWS, TILES), pick(from_after, wanted, STATE_ROWS, TILES)
            )
            for c in range(TILES):
                shift[q : q + 1, c * 128 : (c + 1) * 128] = rows[c : c + 1, :]

    xn = xn_ref[...]
    change = jnp.concatenate([shift[...], xn[: (STEPS - 1) * SLOTS, :]], axis=0) - xn

    def mix(which):
        return (xn + change * blend_ref[which : which + 1, :]).astype(BF16)

    mixed_rows = mix(3)
    rkv = []
    for n in range(3):
        loads[5 + n].wait()
        rkv.append(dot(mix(n), bufs[5 + n][...]))
    for n in range(8, 13):
        loads[n].wait()
    pre = jnp.zeros((ROWS, left_ref.shape[1]), F32)
    chunk = left_ref.shape[2]
    for n in range(left_ref.shape[0]):
        pre = pre + lax.dot_general(
            mixed_rows[:, n * chunk : (n + 1) * chunk], left_ref[n], (((1,), (1,)), ((), ())), preferred_element_type=F32
        )
    lora = jnp.tanh(pre).astype(BF16)
    decay = jnp.exp(-jnp.exp(row_of(base_ref) + dot(lora, right_ref[...])))
    r = [cut(rkv[0], t) for t in range(STEPS)]
    k = [cut(rkv[1], t) for t in range(STEPS)]
    v = [cut(rkv[2], t) for t in range(STEPS)]
    d = [jnp.where(tally > t, cut(decay, t), 1.0) for t in range(STEPS)]
    kept = [jnp.where(tally > t, k[t], 0.0) for t in range(STEPS)]
    boost = row_of(boost_ref)

    run, reach = r[0] * 0.0 + 1.0, []
    for t in range(STEPS):
        reach.append(r[t] * run)
        run = run * d[t]
    tail, coefs = None, [None] * STEPS
    for t in reversed(range(STEPS)):
        coefs[t] = kept[t] if tail is None else kept[t] * tail
        tail = d[t] if tail is None else tail * d[t]
    pairs, terms = [], []
    for t in range(STEPS):
        pairs.append((t, t))
        terms.append(r[t] * boost * k[t])
        weight = r[t]
        for s in reversed(range(t)):
            pairs.append((t, s))
            terms.append(weight * kept[s])
            weight = weight * d[s]
    row256, col256 = iota((LOCAL, LOCAL), 0), iota((LOCAL, LOCAL), 1)
    same_head = (row256 // HEAD == col256 // HEAD).astype(BF16)
    sums = dot_split(jnp.concatenate(terms, axis=0), same_head)
    within = [None] * STEPS
    for n, (t, s) in enumerate(pairs):
        term = cut(sums, n) * v[s]
        within[t] = term if within[t] is None else within[t] + term

    source = (col256 % HEADS) * HEAD + ((col256 // HEADS) % (HEAD // 2)) * 2 + col256 // 128
    reorder = (row256 == source).astype(BF16)
    moved = dot_split(jnp.concatenate(reach + coefs + [run], axis=0), reorder)
    moved_ref[...] = moved[STEPS * SLOTS :, :]
    vals_ref[...] = rkv[2]

    lane = iota((SLOTS, 128), 1)
    for h in range(HEADS):
        head_lane = lane % HEADS == h
        for p in range(2):
            for t in range(STEPS):
                at = pl.ds(t * 8 + p * HEADS + h, SLOTS, stride=STEPS * 8)
                reads[at, :] = jnp.where(head_lane, cut(moved, t)[:, p * 128 : (p + 1) * 128], 0.0)
    for copy in state_loads:
        copy.wait()
    place_received(where, lookup_ref, from_before, from_after, state)
    for q in range(SLOTS):
        rows = slice(q * STEPS * 8, (q + 1) * STEPS * 8)
        now = state[q * STATE_ROWS : (q + 1) * STATE_ROWS, :]
        heads[rows, :] = dot(reads[rows, :].astype(BF16), now.astype(BF16))

    outs = []
    left_half = lane < HEAD
    for t in range(STEPS):
        def read(p, h):
            return heads[pl.ds(t * 8 + p * HEADS + h, SLOTS, stride=STEPS * 8), :]

        cols = []
        for h in range(0, HEADS, 2):
            a, b, c, e = read(0, h), read(1, h), read(0, h + 1), read(1, h + 1)
            cols.append(jnp.where(left_half, a, e) + pltpu.roll(jnp.where(left_half, c, b), HEAD, 1))
        outs.append(jnp.concatenate(cols, axis=1) + within[t])
    y = jnp.concatenate(outs, axis=0)
    center = y - dot_split(y, same_head) * (1.0 / HEAD)
    spread = dot_split(center * center, same_head) * (1.0 / HEAD)
    g = (center * lax.rsqrt(spread + EPS) * row_of(team_ref)).astype(BF16)
    loads[13].wait()
    proj = dot(g, final_ref[...])
    for t in range(STEPS):
        for c in range(TILES):
            part[pl.ds(c * STEPS + t, SLOTS, stride=STEPS * TILES), :] = cut(proj, t)[:, c * 128 : (c + 1) * 128]
    part_ref[...] = part[...].astype(BF16)


def update_kernel(lookup_ref, mem_hbm, *refs):
    count = 4
    hbm, new_hbm, bufs = refs[:count], refs[count], refs[count + 1 : 2 * count + 1]
    state, keys, vals, decays, fresh, sems, state_sems, new_sems = refs[2 * count + 1 :]
    where = place()
    loads = copies(hbm, bufs, sems)
    start(loads)
    state_loads = state_copies(where, lookup_ref, mem_hbm, state, state_sems)
    start(state_loads)
    moved_ref, vals_ref, from_after, from_before = bufs
    loads[0].wait()
    loads[1].wait()
    rowd, cold = iota((LOCAL, HEADS * 128), 0), iota((LOCAL, HEADS * 128), 1)
    double = (rowd == (cold // 128) * HEAD + cold % HEAD).astype(BF16)
    doubled = dot(vals_ref[...].astype(BF16), double)
    lane = iota((SLOTS, 128), 1)
    for h in range(HEADS):
        head_lane = lane % HEADS == h
        for p in range(2):
            half = lane // HEAD == p
            cols = slice(p * 128, (p + 1) * 128)
            for t in range(STEPS):
                at = pl.ds(t * 8 + p * HEADS + h, SLOTS, stride=STEPS * 8)
                keys[at, :] = jnp.where(head_lane, cut(moved_ref, t)[:, cols], 0.0)
                vals[at, :] = jnp.where(half, cut(doubled, t)[:, h * 128 : (h + 1) * 128], 0.0)
            whole = jnp.where(head_lane, cut(moved_ref, STEPS)[:, cols], 0.0)
            high = whole.astype(BF16).astype(F32)
            decays[pl.ds(p * HEADS + h, SLOTS, stride=16), :] = high
            decays[pl.ds(8 + p * HEADS + h, SLOTS, stride=16), :] = whole - high
    ones = ((iota((16, 128), 0) // HEADS) % 2 == iota((16, 128), 1) // HEAD).astype(BF16)
    for copy in loads[2:] + state_loads:
        copy.wait()
    place_received(where, lookup_ref, from_before, from_after, state)
    news = []
    for q in range(SLOTS):
        here = slice(q * STATE_ROWS, (q + 1) * STATE_ROWS)
        rows = slice(q * STEPS * 8, (q + 1) * STEPS * 8)
        fade = dot_rows(decays[q * 16 : (q + 1) * 16, :].astype(BF16), ones)
        grown = dot_rows(keys[rows, :].astype(BF16), vals[rows, :].astype(BF16))
        fresh[here, :] = fade * state[here, :] + grown
        news.append(pltpu.make_async_copy(fresh.at[here, :], new_hbm.at[here, :], new_sems.at[q]))
        news[-1].start()
    for copy in news:
        copy.wait()


def finish_kernel(tally_ref, x_hbm, parts_ref, out_ref, x_ref, sem):
    rows = out_ref.shape[0]
    core = lax.axis_index("tensor") % 2
    begin = core * rows
    load = pltpu.make_async_copy(x_hbm.at[pl.ds(pl.multiple_of(begin, rows), rows), :], x_ref, sem)
    load.start()
    step = iota((STEPS * TILES, 128), 0) % STEPS
    load.wait()
    for q in range(rows // (STEPS * TILES)):
        here = slice(q * STEPS * TILES, (q + 1) * STEPS * TILES)
        total = x_ref[here, :].astype(F32)
        for n in range(parts_ref.shape[0]):
            total = total + parts_ref[n, here, :].astype(F32)
        tally = tally_ref[core * (rows // (STEPS * TILES)) + q]
        out_ref[here, :] = jnp.where(step < tally, total, 0.0).astype(BF16)


def cost(flops, bytes_accessed):
    return pl.CostEstimate(flops=flops, bytes_accessed=bytes_accessed, transcendentals=0)


def tiles_view(a):
    lead, mid, width = a.shape
    return a.reshape(lead, mid, width // 128, 128).transpose(0, 2, 1, 3).reshape(lead * width // 128 * mid, 128)


def tiles_back(a, lead, mid, width):
    return a.reshape(lead, width // 128, mid, 128).transpose(0, 2, 1, 3).reshape(lead, mid, width)


def shards(
    layer_entry_vectors,
    tally_of_tokens,
    prior_slot_lookup,
    memory_matrices,
    previous_standardized_entries,
    entry_standardize_scale,
    blend_coefficients,
    acceptance_projection_matrix,
    lookup_projection_matrix,
    payload_projection_matrix,
    forget_map_left_matrix,
    forget_map_right_matrix,
    feature_forget_logloglevel,
    present_token_boost,
    team_standardize_scale,
    final_projection_matrix,
):
    rings = lax.axis_size("seq")
    teams = lax.axis_size("tensor")
    core = lax.axis_index("tensor") % 2
    x = tiles_view(layer_entry_vectors)
    mem = tiles_view(memory_matrices)
    prev = previous_standardized_entries
    lookup, tally = prior_slot_lookup, tally_of_tokens
    left_t = forget_map_left_matrix.T
    shape, scratch, dma = jax.ShapeDtypeStruct, pltpu.VMEM, pltpu.SemaphoreType.DMA
    params = lambda mib: pltpu.CompilerParams(vmem_limit_bytes=mib << 20)
    like = lambda items: [scratch(a.shape, a.dtype) for a in items]
    state_buf = scratch((SLOTS * STATE_ROWS, 128), F32)
    rows_buf = scratch((SLOTS * STEPS * 8, 128), F32)

    packed, left = pl.pallas_call(
        pack_kernel,
        out_shape=[shape((PACK_ROWS, 128), BF16), shape((teams,) + left_t.shape, BF16)],
        in_specs=spec(pl.ANY, 4),
        out_specs=spec(pltpu.VMEM, 1) + spec(pl.ANY, 1),
        scratch_shapes=[pltpu.SMEM(lookup.shape, jnp.int32)]
        + like([prev, mem, left_t])
        + [scratch((2 * TILES, 128), F32), dma((4 + teams,))],
        compiler_params=params(PACK_MIB),
        cost_estimate=cost(0, 1 << 20),
        name="pack",
    )(lookup, prev, mem, left_t)
    from_after = lax.ppermute(packed, "seq", [((i + 1) % rings, i) for i in range(rings)])
    from_before = lax.ppermute(packed, "seq", [(i, (i + 1) % rings) for i in range(rings)])
    left = lax.all_to_all(left, "tensor", 0, 0)

    gain = entry_standardize_scale.reshape(TILES, 128)
    xn, new_shifts = pl.pallas_call(
        norm_kernel,
        out_shape=[shape((ROWS, WIDTH), F32), shape((SLOTS, WIDTH), F32)],
        in_specs=spec(pltpu.SMEM, 1) + spec(pl.ANY, 2),
        out_specs=spec(pltpu.VMEM, 2),
        scratch_shapes=like([x, gain]) + [scratch((ROWS * TILES, 128), F32), dma((2,))],
        compiler_params=params(MAIN_MIB),
        cost_estimate=cost(0, 4 << 20),
        name="norm",
    )(tally, x, gain)

    operands = [
        xn, prev, from_after, from_before, blend_coefficients,
        acceptance_projection_matrix, lookup_projection_matrix, payload_projection_matrix,
        left, forget_map_right_matrix, feature_forget_logloglevel.reshape(2, 128),
        present_token_boost.reshape(2, 128), team_standardize_scale.reshape(2, 128), final_projection_matrix,
    ]
    part, moved, values = pl.pallas_call(
        main_kernel,
        out_shape=[
            shape((ROWS * TILES, 128), BF16), shape((ROWS + SLOTS, LOCAL), F32), shape((ROWS, LOCAL), F32),
        ],
        in_specs=spec(pltpu.SMEM, 2) + spec(pl.ANY, 1 + len(operands)),
        out_specs=spec(pltpu.VMEM, 3),
        scratch_shapes=like(operands)
        + [scratch((SLOTS, WIDTH), F32), state_buf, rows_buf, rows_buf, scratch((ROWS * TILES, 128), F32)]
        + [dma((len(operands),)), dma((SLOTS,))],
        compiler_params=params(MAIN_MIB),
        cost_estimate=cost(8 * ROWS * WIDTH * LOCAL, 8 << 20),
        name="main",
    )(lookup, tally, mem, *operands)

    operands = [moved, values, from_after, from_before]
    new_states = pl.pallas_call(
        update_kernel,
        out_shape=shape((SLOTS * STATE_ROWS, 128), F32),
        in_specs=spec(pltpu.SMEM, 1) + spec(pl.ANY, 1 + len(operands)),
        out_specs=spec(pl.ANY, 1)[0],
        scratch_shapes=like(operands)
        + [state_buf, rows_buf, rows_buf, scratch((SLOTS * 16, 128), F32), state_buf]
        + [dma((len(operands),)), dma((SLOTS,)), dma((SLOTS,))],
        compiler_params=params(MAIN_MIB),
        cost_estimate=cost(1 << 24, 8 << 20),
        name="update",
    )(lookup, mem, *operands)

    pairs = [[2 * i, 2 * i + 1] for i in range(teams // 2)]
    chips = [[2 * i + c for i in range(teams // 2)] for c in range(2)]
    half = ROWS * TILES // 2
    both = lax.all_gather(part, "tensor", axis_index_groups=pairs, tiled=False)
    mine = lax.dynamic_slice_in_dim(both, core * half, half, 1).astype(F32).sum(0).astype(BF16)
    spread = lax.all_to_all(
        jnp.broadcast_to(mine[None], (teams // 2,) + mine.shape), "tensor", 0, 0, axis_index_groups=chips
    )
    mixed = pl.pallas_call(
        finish_kernel,
        out_shape=shape((half, 128), BF16),
        in_specs=spec(pltpu.SMEM, 1) + spec(pl.ANY, 1) + spec(pltpu.VMEM, 1),
        out_specs=spec(pltpu.VMEM, 1)[0],
        scratch_shapes=[scratch((half, 128), BF16), dma],
        compiler_params=params(8),
        cost_estimate=cost(0, 1 << 19),
        name="finish",
    )(tally, x, spread)
    mixed = tiles_back(mixed, SLOTS // 2, STEPS, WIDTH)
    mixed = lax.all_gather(mixed, "tensor", axis_index_groups=pairs, tiled=True)
    return (
        mixed,
        tiles_back(new_states, SLOTS, HEADS, HEAD * HEAD),
        new_shifts,
    )


def solution(mesh):
    in_specs = (
        P("seq", None, None),
        P("seq"),
        P("seq"),
        P("seq", "tensor", None),
        P("seq", None),
        P(),
        P(),
        P(None, "tensor"),
        P(None, "tensor"),
        P(None, "tensor"),
        P("tensor", None),
        P(None, "tensor"),
        P("tensor"),
        P("tensor"),
        P("tensor"),
        P("tensor", None),
    )
    out_specs = (P("seq", None, None), P("seq", "tensor", None), P("seq", None))
    return jax.shard_map(shards, mesh=mesh, in_specs=in_specs, out_specs=out_specs, check_vma=False)
```

```python
import functools

import jax
import jax.numpy as jnp
from jax import lax
from jax.experimental import pallas as pl
from jax.experimental.pallas import tpu as pltpu
from jax.sharding import PartitionSpec as P

EPS = 1e-05
F32 = jnp.float32
BF16 = jnp.bfloat16
HEAD = 64
SLOTS = 16
STEPS = 4
WIDTH = 2048
HEADS = 4
LOCAL = HEADS * HEAD
TILES = WIDTH // 128
ROWS = SLOTS * STEPS
STATE_ROWS = HEADS * HEAD * HEAD // 128
PIECE = STATE_ROWS + TILES
PACK_ROWS = 2 * PIECE + 16
PACK_MIB, MAIN_MIB = 60, 52


def spec(space, count):
    return [pl.BlockSpec(memory_space=space)] * count


def dot(a, b):
    return jnp.dot(a, b, preferred_element_type=F32)


def dot_rows(a, b):
    return lax.dot_general(a, b, (((0,), (0,)), ((), ())), preferred_element_type=F32)


def split(a):
    hi = a.astype(BF16)
    return hi, (a - hi.astype(F32)).astype(BF16)


def dot_split(a, b):
    hi, lo = split(a)
    return dot(hi, b) + dot(lo, b)


def iota(shape, dim):
    return lax.broadcasted_iota(jnp.int32, shape, dim)


def column_of(tally_ref, shape):
    rows = iota(shape, 0)
    out = jnp.zeros(shape, jnp.int32)
    for q in range(SLOTS):
        out = jnp.where(rows == q, tally_ref[q], out)
    return out


def row_of(ref):
    return jnp.concatenate([ref[i : i + 1, :] for i in range(ref.shape[0])], axis=1)


def start(items):
    for copy in items:
        copy.start()


def place():
    count = lax.axis_size("seq")
    me = lax.axis_index("seq")
    return me, jnp.where(me == 0, count - 1, me - 1)


def pack_kernel(lookup_hbm, prev_hbm, mem_hbm, left_hbm, out_ref, left_out, lookup_ref, prev, mem, left, tile, sems):
    loads = copies((lookup_hbm, prev_hbm, mem_hbm, left_hbm), (lookup_ref, prev, mem, left), sems)
    start(loads)
    first = place()[0] * SLOTS
    loads[3].wait()
    sends = [pltpu.make_async_copy(left, left_out.at[n], sems.at[4 + n]) for n in range(left_out.shape[0])]
    start(sends)
    loads[0].wait()
    kept = jnp.int32(0)
    for q in range(SLOTS):
        at = lookup_ref[q] - first
        own = (at >= 0) & (at < SLOTS)
        kept = kept | jnp.where(own, jnp.int32(1) << jnp.where(own, at, 0), 0)
    low, high = jnp.int32(0), jnp.int32(0)
    for s in range(SLOTS):
        high = jnp.where((kept >> s) & 1 == 0, s, high)
        low = jnp.where((kept >> (SLOTS - 1 - s)) & 1 == 0, SLOTS - 1 - s, low)
    out_ref[2 * PIECE :, :] = jnp.full((16, 128), low, jnp.int32).astype(F32).astype(BF16)
    loads[1].wait()
    for n, slot in enumerate((low, high)):
        row = prev[pl.ds(slot, 1), :]
        for c in range(TILES):
            tile[n * TILES + c : n * TILES + c + 1, :] = row[:, c * 128 : (c + 1) * 128]
    loads[2].wait()
    for n, slot in enumerate((low, high)):
        begin = pl.multiple_of(slot * STATE_ROWS, STATE_ROWS)
        out_ref[n * PIECE : n * PIECE + STATE_ROWS, :] = mem[pl.ds(begin, STATE_ROWS), :].astype(BF16)
        out_ref[n * PIECE + STATE_ROWS : (n + 1) * PIECE, :] = tile[n * TILES : (n + 1) * TILES, :].astype(BF16)
    for copy in sends:
        copy.wait()


def pick(recv_ref, wanted, begin, count):
    low = recv_ref[2 * PIECE :, :].astype(F32)[:1, :]
    is_low = low == (wanted % SLOTS).astype(F32)
    rows = [recv_ref[at : at + count, :].astype(F32) for at in (begin, PIECE + begin)]
    return jnp.where(is_low, rows[0], rows[1])


def sources(where, lookup_ref, q):
    wanted = lookup_ref[q]
    owner = wanted // SLOTS
    own = owner == where[0]
    before = owner == where[1]
    at = jnp.where(own, wanted - where[0] * SLOTS, 0)
    return wanted, own, before, at


def copies(sources_, targets, sems):
    return [pltpu.make_async_copy(a, b, sems.at[n]) for n, (a, b) in enumerate(zip(sources_, targets))]


def state_copies(where, lookup_ref, mem_hbm, state, sems):
    out = []
    for q in range(SLOTS):
        at = sources(where, lookup_ref, q)[3]
        out.append(
            pltpu.make_async_copy(
                mem_hbm.at[pl.ds(pl.multiple_of(at * STATE_ROWS, STATE_ROWS), STATE_ROWS), :],
                state.at[pl.ds(q * STATE_ROWS, STATE_ROWS), :],
                sems.at[q],
            )
        )
    return out


def place_received(where, lookup_ref, from_before, from_after, state):
    for q in range(SLOTS):
        wanted, own, before, _ = sources(where, lookup_ref, q)
        here = slice(q * STATE_ROWS, (q + 1) * STATE_ROWS)

        @pl.when(jnp.logical_not(own) & before)
        def _():
            state[here, :] = pick(from_before, wanted, 0, STATE_ROWS)

        @pl.when(jnp.logical_not(own) & jnp.logical_not(before))
        def _():
            state[here, :] = pick(from_after, wanted, 0, STATE_ROWS)


def cut(a, t):
    return a[t * SLOTS : (t + 1) * SLOTS, :]


def main_kernel(lookup_ref, tally_ref, mem_hbm, *refs):
    count = 15
    hbm, (part_ref, moved_ref, vals_ref, last_ref) = refs[:count], refs[count : count + 4]
    bufs = refs[count + 4 : 2 * count + 4]
    x32, shift, state, reads, heads, part, sems, state_sems = refs[2 * count + 4 :]
    where = place()
    loads = copies(hbm, bufs, sems)
    start(loads[:-1])
    state_loads = state_copies(where, lookup_ref, mem_hbm, state, state_sems)
    start(state_loads)
    loads[-1].start()
    x_ref, gain_ref, prev_ref, from_after, from_before, blend_ref = bufs[:6]
    left_ref, right_ref, base_ref, boost_ref, team_ref, final_ref = bufs[9:]
    loads[0].wait()
    loads[1].wait()
    x32[...] = x_ref[...].astype(F32)
    gain = row_of(gain_ref)
    normed = []
    for t in range(STEPS):
        row = jnp.concatenate([x32[pl.ds(c * STEPS + t, SLOTS, stride=STEPS * TILES), :] for c in range(TILES)], axis=1)
        center = row - jnp.mean(row, axis=-1, keepdims=True)
        spread = jnp.mean(center * center, axis=-1, keepdims=True)
        normed.append(center * lax.rsqrt(spread + EPS) * gain)
    tally = column_of(tally_ref, (SLOTS, 128))[:, :1]
    last = normed[0]
    for t in range(1, STEPS):
        last = jnp.where(tally == t + 1, normed[t], last)
    last_ref[...] = last
    for n in range(2, 6):
        loads[n].wait()
    for q in range(SLOTS):
        wanted, own, before, at = sources(where, lookup_ref, q)

        @pl.when(own)
        def _():
            shift[q : q + 1, :] = prev_ref[pl.ds(at, 1), :]

        @pl.when(jnp.logical_not(own))
        def _():
            rows = jnp.where(
                before, pick(from_before, wanted, STATE_ROWS, TILES), pick(from_after, wanted, STATE_ROWS, TILES)
            )
            for c in range(TILES):
                shift[q : q + 1, c * 128 : (c + 1) * 128] = rows[c : c + 1, :]

    xn = jnp.concatenate(normed, axis=0)
    change = jnp.concatenate([shift[...]] + normed[:-1], axis=0) - xn

    def mix(which):
        return (xn + change * blend_ref[which : which + 1, :]).astype(BF16)

    mixed_rows = mix(3)
    rkv = []
    for n in range(3):
        loads[6 + n].wait()
        rkv.append(dot(mix(n), bufs[6 + n][...]))
    for n in range(9, 14):
        loads[n].wait()
    pre = jnp.zeros((ROWS, left_ref.shape[1]), F32)
    chunk = left_ref.shape[2]
    for n in range(left_ref.shape[0]):
        pre = pre + lax.dot_general(
            mixed_rows[:, n * chunk : (n + 1) * chunk], left_ref[n], (((1,), (1,)), ((), ())), preferred_element_type=F32
        )
    lora = jnp.tanh(pre).astype(BF16)
    decay = jnp.exp(-jnp.exp(row_of(base_ref) + dot(lora, right_ref[...])))
    r = [cut(rkv[0], t) for t in range(STEPS)]
    k = [cut(rkv[1], t) for t in range(STEPS)]
    v = [cut(rkv[2], t) for t in range(STEPS)]
    d = [jnp.where(tally > t, cut(decay, t), 1.0) for t in range(STEPS)]
    kept = [jnp.where(tally > t, k[t], 0.0) for t in range(STEPS)]
    boost = row_of(boost_ref)

    run, reach = r[0] * 0.0 + 1.0, []
    for t in range(STEPS):
        reach.append(r[t] * run)
        run = run * d[t]
    tail, coefs = None, [None] * STEPS
    for t in reversed(range(STEPS)):
        coefs[t] = kept[t] if tail is None else kept[t] * tail
        tail = d[t] if tail is None else tail * d[t]
    pairs, terms = [], []
    for t in range(STEPS):
        pairs.append((t, t))
        terms.append(r[t] * boost * k[t])
        weight = r[t]
        for s in reversed(range(t)):
            pairs.append((t, s))
            terms.append(weight * kept[s])
            weight = weight * d[s]
    row256, col256 = iota((LOCAL, LOCAL), 0), iota((LOCAL, LOCAL), 1)
    same_head = (row256 // HEAD == col256 // HEAD).astype(BF16)
    sums = dot_split(jnp.concatenate(terms, axis=0), same_head)
    within = [None] * STEPS
    for n, (t, s) in enumerate(pairs):
        term = cut(sums, n) * v[s]
        within[t] = term if within[t] is None else within[t] + term

    source = (col256 % HEADS) * HEAD + ((col256 // HEADS) % (HEAD // 2)) * 2 + col256 // 128
    reorder = (row256 == source).astype(BF16)
    moved = dot_split(jnp.concatenate(reach + coefs + [run], axis=0), reorder)
    moved_ref[...] = moved[STEPS * SLOTS :, :]
    vals_ref[...] = rkv[2]

    lane = iota((SLOTS, 128), 1)
    for h in range(HEADS):
        head_lane = lane % HEADS == h
        for p in range(2):
            for t in range(STEPS):
                at = pl.ds(t * 8 + p * HEADS + h, SLOTS, stride=STEPS * 8)
                reads[at, :] = jnp.where(head_lane, cut(moved, t)[:, p * 128 : (p + 1) * 128], 0.0)
    for copy in state_loads:
        copy.wait()
    place_received(where, lookup_ref, from_before, from_after, state)
    for q in range(SLOTS):
        rows = slice(q * STEPS * 8, (q + 1) * STEPS * 8)
        now = state[q * STATE_ROWS : (q + 1) * STATE_ROWS, :]
        heads[rows, :] = dot(reads[rows, :].astype(BF16), now.astype(BF16))

    outs = []
    left_half = lane < HEAD
    for t in range(STEPS):
        def read(p, h):
            return heads[pl.ds(t * 8 + p * HEADS + h, SLOTS, stride=STEPS * 8), :]

        cols = []
        for h in range(0, HEADS, 2):
            a, b, c, e = read(0, h), read(1, h), read(0, h + 1), read(1, h + 1)
            cols.append(jnp.where(left_half, a, e) + pltpu.roll(jnp.where(left_half, c, b), HEAD, 1))
        outs.append(jnp.concatenate(cols, axis=1) + within[t])
    y = jnp.concatenate(outs, axis=0)
    center = y - dot_split(y, same_head) * (1.0 / HEAD)
    spread = dot_split(center * center, same_head) * (1.0 / HEAD)
    g = (center * lax.rsqrt(spread + EPS) * row_of(team_ref)).astype(BF16)
    loads[14].wait()
    proj = dot(g, final_ref[...])
    for t in range(STEPS):
        for c in range(TILES):
            part[pl.ds(c * STEPS + t, SLOTS, stride=STEPS * TILES), :] = cut(proj, t)[:, c * 128 : (c + 1) * 128]
    part_ref[...] = part[...].astype(BF16)


def update_kernel(lookup_ref, mem_hbm, *refs):
    count = 4
    hbm, new_hbm, bufs = refs[:count], refs[count], refs[count + 1 : 2 * count + 1]
    state, keys, vals, decays, fresh, sems, state_sems, new_sems = refs[2 * count + 1 :]
    where = place()
    loads = copies(hbm, bufs, sems)
    start(loads)
    state_loads = state_copies(where, lookup_ref, mem_hbm, state, state_sems)
    start(state_loads)
    moved_ref, vals_ref, from_after, from_before = bufs
    loads[0].wait()
    loads[1].wait()
    rowd, cold = iota((LOCAL, HEADS * 128), 0), iota((LOCAL, HEADS * 128), 1)
    double = (rowd == (cold // 128) * HEAD + cold % HEAD).astype(BF16)
    doubled = dot(vals_ref[...].astype(BF16), double)
    lane = iota((SLOTS, 128), 1)
    for h in range(HEADS):
        head_lane = lane % HEADS == h
        for p in range(2):
            half = lane // HEAD == p
            cols = slice(p * 128, (p + 1) * 128)
            for t in range(STEPS):
                at = pl.ds(t * 8 + p * HEADS + h, SLOTS, stride=STEPS * 8)
                keys[at, :] = jnp.where(head_lane, cut(moved_ref, t)[:, cols], 0.0)
                vals[at, :] = jnp.where(half, cut(doubled, t)[:, h * 128 : (h + 1) * 128], 0.0)
            whole = jnp.where(head_lane, cut(moved_ref, STEPS)[:, cols], 0.0)
            high = whole.astype(BF16).astype(F32)
            decays[pl.ds(p * HEADS + h, SLOTS, stride=16), :] = high
            decays[pl.ds(8 + p * HEADS + h, SLOTS, stride=16), :] = whole - high
    ones = ((iota((16, 128), 0) // HEADS) % 2 == iota((16, 128), 1) // HEAD).astype(BF16)
    for copy in loads[2:] + state_loads:
        copy.wait()
    place_received(where, lookup_ref, from_before, from_after, state)
    news = []
    for q in range(SLOTS):
        here = slice(q * STATE_ROWS, (q + 1) * STATE_ROWS)
        rows = slice(q * STEPS * 8, (q + 1) * STEPS * 8)
        fade = dot_rows(decays[q * 16 : (q + 1) * 16, :].astype(BF16), ones)
        grown = dot_rows(keys[rows, :].astype(BF16), vals[rows, :].astype(BF16))
        fresh[here, :] = fade * state[here, :] + grown
        news.append(pltpu.make_async_copy(fresh.at[here, :], new_hbm.at[here, :], new_sems.at[q]))
        news[-1].start()
    for copy in news:
        copy.wait()


def cost(flops, bytes_accessed):
    return pl.CostEstimate(flops=flops, bytes_accessed=bytes_accessed, transcendentals=0)


def tiles_view(a):
    lead, mid, width = a.shape
    return a.reshape(lead, mid, width // 128, 128).transpose(0, 2, 1, 3).reshape(lead * width // 128 * mid, 128)


def tiles_back(a, lead, mid, width):
    return a.reshape(lead, width // 128, mid, 128).transpose(0, 2, 1, 3).reshape(lead, mid, width)


def shards(
    layer_entry_vectors,
    tally_of_tokens,
    prior_slot_lookup,
    memory_matrices,
    previous_standardized_entries,
    entry_standardize_scale,
    blend_coefficients,
    acceptance_projection_matrix,
    lookup_projection_matrix,
    payload_projection_matrix,
    forget_map_left_matrix,
    forget_map_right_matrix,
    feature_forget_logloglevel,
    present_token_boost,
    team_standardize_scale,
    final_projection_matrix,
):
    rings = lax.axis_size("seq")
    teams = lax.axis_size("tensor")
    core = lax.axis_index("tensor") % 2
    x = tiles_view(layer_entry_vectors)
    mem = tiles_view(memory_matrices)
    prev = previous_standardized_entries
    lookup, tally = prior_slot_lookup, tally_of_tokens
    left_t = forget_map_left_matrix.T
    shape, scratch, dma = jax.ShapeDtypeStruct, pltpu.VMEM, pltpu.SemaphoreType.DMA
    params = lambda mib: pltpu.CompilerParams(vmem_limit_bytes=mib << 20)
    like = lambda items: [scratch(a.shape, a.dtype) for a in items]
    state_buf = scratch((SLOTS * STATE_ROWS, 128), F32)
    rows_buf = scratch((SLOTS * STEPS * 8, 128), F32)

    packed, left = pl.pallas_call(
        pack_kernel,
        out_shape=[shape((PACK_ROWS, 128), BF16), shape((teams,) + left_t.shape, BF16)],
        in_specs=spec(pl.ANY, 4),
        out_specs=spec(pltpu.VMEM, 1) + spec(pl.ANY, 1),
        scratch_shapes=[pltpu.SMEM(lookup.shape, jnp.int32)]
        + like([prev, mem, left_t])
        + [scratch((2 * TILES, 128), F32), dma((4 + teams,))],
        compiler_params=params(PACK_MIB),
        cost_estimate=cost(0, 1 << 20),
        name="pack",
    )(lookup, prev, mem, left_t)
    from_after = lax.ppermute(packed, "seq", [((i + 1) % rings, i) for i in range(rings)])
    from_before = lax.ppermute(packed, "seq", [(i, (i + 1) % rings) for i in range(rings)])
    left = lax.all_to_all(left, "tensor", 0, 0)

    operands = [
        x, entry_standardize_scale.reshape(TILES, 128), prev, from_after, from_before, blend_coefficients,
        acceptance_projection_matrix, lookup_projection_matrix, payload_projection_matrix,
        left, forget_map_right_matrix, feature_forget_logloglevel.reshape(2, 128),
        present_token_boost.reshape(2, 128), team_standardize_scale.reshape(2, 128), final_projection_matrix,
    ]
    part, moved, values, new_shifts = pl.pallas_call(
        main_kernel,
        out_shape=[
            shape((ROWS * TILES, 128), BF16), shape((ROWS + SLOTS, LOCAL), F32), shape((ROWS, LOCAL), F32),
            shape((SLOTS, WIDTH), F32),
        ],
        in_specs=spec(pltpu.SMEM, 2) + spec(pl.ANY, 1 + len(operands)),
        out_specs=spec(pltpu.VMEM, 4),
        scratch_shapes=like(operands)
        + [scratch((ROWS * TILES, 128), F32), scratch((SLOTS, WIDTH), F32), state_buf, rows_buf, rows_buf, scratch((ROWS * TILES, 128), F32)]
        + [dma((len(operands),)), dma((SLOTS,))],
        compiler_params=params(MAIN_MIB),
        cost_estimate=cost(8 * ROWS * WIDTH * LOCAL, 8 << 20),
        name="main",
    )(lookup, tally, mem, *operands)

    operands = [moved, values, from_after, from_before]
    new_states = pl.pallas_call(
        update_kernel,
        out_shape=shape((SLOTS * STATE_ROWS, 128), F32),
        in_specs=spec(pltpu.SMEM, 1) + spec(pl.ANY, 1 + len(operands)),
        out_specs=spec(pl.ANY, 1)[0],
        scratch_shapes=like(operands)
        + [state_buf, rows_buf, rows_buf, scratch((SLOTS * 16, 128), F32), state_buf]
        + [dma((len(operands),)), dma((SLOTS,)), dma((SLOTS,))],
        compiler_params=params(MAIN_MIB),
        cost_estimate=cost(1 << 24, 8 << 20),
        name="update",
    )(lookup, mem, *operands)

    pairs = [[2 * i, 2 * i + 1] for i in range(teams // 2)]
    chips = [[2 * i + c for i in range(teams // 2)] for c in range(2)]
    half = ROWS * TILES // 2
    both = lax.all_gather(part, "tensor", axis_index_groups=pairs, tiled=False)
    mine = lax.dynamic_slice_in_dim(both, core * half, half, 1).astype(F32).sum(0).astype(BF16)
    spread = lax.all_to_all(
        jnp.broadcast_to(mine[None], (teams // 2,) + mine.shape), "tensor", 0, 0, axis_index_groups=chips
    )
    total = tiles_back(spread.astype(F32).sum(0).astype(BF16), SLOTS // 2, STEPS, WIDTH)
    proj = lax.all_gather(total, "tensor", axis_index_groups=pairs, tiled=True)
    valid = tally[:, None, None] > jnp.arange(STEPS, dtype=jnp.int32)[None, :, None]
    mixed = jnp.where(valid, layer_entry_vectors.astype(F32) + proj.astype(F32), 0.0).astype(BF16)
    return (
        mixed,
        tiles_back(new_states, SLOTS, HEADS, HEAD * HEAD),
        new_shifts,
    )


def solution(mesh):
    in_specs = (
        P("seq", None, None),
        P("seq"),
        P("seq"),
        P("seq", "tensor", None),
        P("seq", None),
        P(),
        P(),
        P(None, "tensor"),
        P(None, "tensor"),
        P(None, "tensor"),
        P("tensor", None),
        P(None, "tensor"),
        P("tensor"),
        P("tensor"),
        P("tensor"),
        P("tensor", None),
    )
    out_specs = (P("seq", None, None), P("seq", "tensor", None), P("seq", None))
    return jax.shard_map(shards, mesh=mesh, in_specs=in_specs, out_specs=out_specs, check_vma=False)
```

```python
import functools

import jax
import jax.numpy as jnp
from jax import lax
from jax.experimental import pallas as pl
from jax.experimental.pallas import tpu as pltpu
from jax.sharding import PartitionSpec as P

EPS = 1e-05
F32 = jnp.float32
BF16 = jnp.bfloat16
HEAD = 64
SLOTS = 16
STEPS = 4
WIDTH = 2048
HEADS = 4
LOCAL = HEADS * HEAD
TILES = WIDTH // 128
ROWS = SLOTS * STEPS
STATE_ROWS = HEADS * HEAD * HEAD // 128
PIECE = STATE_ROWS + TILES
PACK_ROWS = 2 * PIECE + 16
CAME, TALLY, META = SLOTS, SLOTS + 16, 64
PACK_MIB, MAIN_MIB = 60, 52


def spec(space, count):
    return [pl.BlockSpec(memory_space=space)] * count


def dot(a, b):
    return jnp.dot(a, b, preferred_element_type=F32)


def dot_rows(a, b):
    return lax.dot_general(a, b, (((0,), (0,)), ((), ())), preferred_element_type=F32)


def split(a):
    hi = a.astype(BF16)
    return hi, (a - hi.astype(F32)).astype(BF16)


def dot_split(a, b):
    hi, lo = split(a)
    return dot(hi, b) + dot(lo, b)


def iota(shape, dim):
    return lax.broadcasted_iota(jnp.int32, shape, dim)


def column_of(meta_ref, shape):
    rows = iota(shape, 0)
    out = jnp.zeros(shape, jnp.int32)
    for q in range(SLOTS):
        out = jnp.where(rows == q, meta_ref[TALLY + q], out)
    return out


def row_of(ref):
    return jnp.concatenate([ref[i : i + 1, :] for i in range(ref.shape[0])], axis=1)


def start(items):
    for copy in items:
        copy.start()


def place():
    count = lax.axis_size("seq")
    me = lax.axis_index("seq")
    return me, jnp.where(me == 0, count - 1, me - 1)


def pack_kernel(
    lookup_hbm, tally_hbm, prev_hbm, mem_hbm, left_hbm, out_ref, left_out, meta_ref,
    lookup_ref, tally_ref, prev, mem, left, tile, sems,
):
    loads = copies(
        (lookup_hbm, prev_hbm, mem_hbm, left_hbm, tally_hbm), (lookup_ref, prev, mem, left, tally_ref), sems
    )
    start(loads)
    me, behind = place()
    first = me * SLOTS
    loads[3].wait()
    sends = [pltpu.make_async_copy(left, left_out.at[n], sems.at[5 + n]) for n in range(left_out.shape[0])]
    start(sends)
    loads[0].wait()
    kept = jnp.int32(0)
    slots, wants = [jnp.int32(0)] * 2, [jnp.int32(0)] * 2
    for q in range(SLOTS):
        at = lookup_ref[q] - first
        own = (at >= 0) & (at < SLOTS)
        at = jnp.where(own, at, 0)
        kept = kept | jnp.where(own, jnp.int32(1) << at, 0)
        meta_ref[q] = at
        owner = lookup_ref[q] >> (SLOTS.bit_length() - 1)
        for n, mine in enumerate((jnp.logical_not(own) & (owner == behind), jnp.logical_not(own) & (owner != behind))):
            slots[n] = jnp.where(mine, q, slots[n])
            wants[n] = jnp.where(mine, lookup_ref[q] & (SLOTS - 1), wants[n])
    for n in range(2):
        meta_ref[CAME + n] = slots[n]
        meta_ref[CAME + 2 + n] = wants[n]
    low, high = jnp.int32(0), jnp.int32(0)
    for s in range(SLOTS):
        high = jnp.where((kept >> s) & 1 == 0, s, high)
        low = jnp.where((kept >> (SLOTS - 1 - s)) & 1 == 0, SLOTS - 1 - s, low)
    out_ref[2 * PIECE :, :] = jnp.full((16, 128), low, jnp.int32).astype(F32).astype(BF16)
    loads[1].wait()
    for n, slot in enumerate((low, high)):
        row = prev[pl.ds(slot, 1), :]
        for c in range(TILES):
            tile[n * TILES + c : n * TILES + c + 1, :] = row[:, c * 128 : (c + 1) * 128]
    loads[2].wait()
    for n, slot in enumerate((low, high)):
        begin = pl.multiple_of(slot * STATE_ROWS, STATE_ROWS)
        out_ref[n * PIECE : n * PIECE + STATE_ROWS, :] = mem[pl.ds(begin, STATE_ROWS), :].astype(BF16)
        out_ref[n * PIECE + STATE_ROWS : (n + 1) * PIECE, :] = tile[n * TILES : (n + 1) * TILES, :].astype(BF16)
    loads[4].wait()
    for q in range(SLOTS):
        meta_ref[TALLY + q] = tally_ref[q]
    for copy in sends:
        copy.wait()


def pick(recv_ref, wanted, begin, count):
    low = recv_ref[2 * PIECE :, :].astype(F32)[:1, :]
    is_low = low == wanted.astype(F32)
    rows = [recv_ref[at : at + count, :].astype(F32) for at in (begin, PIECE + begin)]
    return jnp.where(is_low, rows[0], rows[1])


def copies(sources_, targets, sems):
    return [pltpu.make_async_copy(a, b, sems.at[n]) for n, (a, b) in enumerate(zip(sources_, targets))]


def cut(a, t):
    return a[t * SLOTS : (t + 1) * SLOTS, :]


def state_copies(meta_ref, mem_hbm, state, sems):
    return [
        pltpu.make_async_copy(
            mem_hbm.at[pl.ds(pl.multiple_of(meta_ref[q] * STATE_ROWS, STATE_ROWS), STATE_ROWS), :],
            state.at[pl.ds(q * STATE_ROWS, STATE_ROWS), :],
            sems.at[q],
        )
        for q in range(SLOTS)
    ]


def place_received(meta_ref, received, state):
    for n, recv_ref in enumerate(received):
        begin = pl.multiple_of(meta_ref[CAME + n] * STATE_ROWS, STATE_ROWS)
        state[pl.ds(begin, STATE_ROWS), :] = pick(recv_ref, meta_ref[CAME + 2 + n], 0, STATE_ROWS)


def main_kernel(meta_ref, mem_hbm, *refs):
    count = 15
    hbm, (part_ref, moved_ref, vals_ref, last_ref) = refs[:count], refs[count : count + 4]
    bufs = refs[count + 4 : 2 * count + 4]
    x32, shift, state, reads, heads, part, sems, state_sems = refs[2 * count + 4 :]
    loads = copies(hbm, bufs, sems)
    start(loads[:-1])
    state_loads = state_copies(meta_ref, mem_hbm, state, state_sems)
    start(state_loads)
    loads[-1].start()
    x_ref, gain_ref, prev_ref, from_after, from_before, blend_ref = bufs[:6]
    left_ref, right_ref, base_ref, boost_ref, team_ref, final_ref = bufs[9:]
    loads[0].wait()
    loads[1].wait()
    x32[...] = x_ref[...].astype(F32)
    gain = row_of(gain_ref)
    normed = []
    for t in range(STEPS):
        row = jnp.concatenate([x32[pl.ds(c * STEPS + t, SLOTS, stride=STEPS * TILES), :] for c in range(TILES)], axis=1)
        center = row - jnp.mean(row, axis=-1, keepdims=True)
        spread = jnp.mean(center * center, axis=-1, keepdims=True)
        normed.append(center * lax.rsqrt(spread + EPS) * gain)
    tally = column_of(meta_ref, (SLOTS, 128))[:, :1]
    last = normed[0]
    for t in range(1, STEPS):
        last = jnp.where(tally == t + 1, normed[t], last)
    last_ref[...] = last
    for n in range(2, 6):
        loads[n].wait()
    for q in range(SLOTS):
        shift[q : q + 1, :] = prev_ref[pl.ds(meta_ref[q], 1), :]
    slot = iota((SLOTS, 128), 0)
    moved_rows = [
        pick(recv_ref, meta_ref[CAME + 2 + n], STATE_ROWS, TILES) for n, recv_ref in enumerate((from_before, from_after))
    ]
    shift_in = []
    for c in range(TILES):
        col = shift[:, c * 128 : (c + 1) * 128]
        for n, rows in enumerate(moved_rows):
            col = jnp.where(slot == meta_ref[CAME + n], rows[c : c + 1, :], col)
        shift_in.append(col)
    xn = jnp.concatenate(normed, axis=0)
    change = jnp.concatenate([jnp.concatenate(shift_in, axis=1)] + normed[:-1], axis=0) - xn

    def mix(which):
        return (xn + change * blend_ref[which : which + 1, :]).astype(BF16)

    mixed_rows = mix(3)
    rkv = []
    for n in range(3):
        loads[6 + n].wait()
        rkv.append(dot(mix(n), bufs[6 + n][...]))
    for n in range(9, 14):
        loads[n].wait()
    pre = jnp.zeros((ROWS, left_ref.shape[1]), F32)
    chunk = left_ref.shape[2]
    for n in range(left_ref.shape[0]):
        pre = pre + lax.dot_general(
            mixed_rows[:, n * chunk : (n + 1) * chunk], left_ref[n], (((1,), (1,)), ((), ())), preferred_element_type=F32
        )
    lora = jnp.tanh(pre).astype(BF16)
    decay = jnp.exp(-jnp.exp(row_of(base_ref) + dot(lora, right_ref[...])))
    r = [cut(rkv[0], t) for t in range(STEPS)]
    k = [cut(rkv[1], t) for t in range(STEPS)]
    v = [cut(rkv[2], t) for t in range(STEPS)]
    d = [jnp.where(tally > t, cut(decay, t), 1.0) for t in range(STEPS)]
    kept = [jnp.where(tally > t, k[t], 0.0) for t in range(STEPS)]
    boost = row_of(boost_ref)

    run, reach = r[0] * 0.0 + 1.0, []
    for t in range(STEPS):
        reach.append(r[t] * run)
        run = run * d[t]
    tail, coefs = None, [None] * STEPS
    for t in reversed(range(STEPS)):
        coefs[t] = kept[t] if tail is None else kept[t] * tail
        tail = d[t] if tail is None else tail * d[t]
    pairs, terms = [], []
    for t in range(STEPS):
        pairs.append((t, t))
        terms.append(r[t] * boost * k[t])
        weight = r[t]
        for s in reversed(range(t)):
            pairs.append((t, s))
            terms.append(weight * kept[s])
            weight = weight * d[s]
    row256, col256 = iota((LOCAL, LOCAL), 0), iota((LOCAL, LOCAL), 1)
    same_head = (row256 // HEAD == col256 // HEAD).astype(BF16)
    sums = dot_split(jnp.concatenate(terms, axis=0), same_head)
    within = [None] * STEPS
    for n, (t, s) in enumerate(pairs):
        term = cut(sums, n) * v[s]
        within[t] = term if within[t] is None else within[t] + term

    source = (col256 % HEADS) * HEAD + ((col256 // HEADS) % (HEAD // 2)) * 2 + col256 // 128
    reorder = (row256 == source).astype(BF16)
    moved = dot_split(jnp.concatenate(reach + coefs + [run], axis=0), reorder)
    moved_ref[...] = moved[STEPS * SLOTS :, :]
    vals_ref[...] = rkv[2]

    lane = iota((SLOTS, 128), 1)
    for h in range(HEADS):
        head_lane = lane % HEADS == h
        for p in range(2):
            for t in range(STEPS):
                at = pl.ds(t * 8 + p * HEADS + h, SLOTS, stride=STEPS * 8)
                reads[at, :] = jnp.where(head_lane, cut(moved, t)[:, p * 128 : (p + 1) * 128], 0.0)
    for copy in state_loads:
        copy.wait()
    place_received(meta_ref, (from_before, from_after), state)
    for q in range(SLOTS):
        rows = slice(q * STEPS * 8, (q + 1) * STEPS * 8)
        now = state[q * STATE_ROWS : (q + 1) * STATE_ROWS, :]
        heads[rows, :] = dot(reads[rows, :].astype(BF16), now.astype(BF16))

    outs = []
    left_half = lane < HEAD
    for t in range(STEPS):
        def read(p, h):
            return heads[pl.ds(t * 8 + p * HEADS + h, SLOTS, stride=STEPS * 8), :]

        cols = []
        for h in range(0, HEADS, 2):
            a, b, c, e = read(0, h), read(1, h), read(0, h + 1), read(1, h + 1)
            cols.append(jnp.where(left_half, a, e) + pltpu.roll(jnp.where(left_half, c, b), HEAD, 1))
        outs.append(jnp.concatenate(cols, axis=1) + within[t])
    y = jnp.concatenate(outs, axis=0)
    center = y - dot_split(y, same_head) * (1.0 / HEAD)
    spread = dot_split(center * center, same_head) * (1.0 / HEAD)
    g = (center * lax.rsqrt(spread + EPS) * row_of(team_ref)).astype(BF16)
    loads[14].wait()
    proj = dot(g, final_ref[...])
    for t in range(STEPS):
        for c in range(TILES):
            part[pl.ds(c * STEPS + t, SLOTS, stride=STEPS * TILES), :] = cut(proj, t)[:, c * 128 : (c + 1) * 128]
    part_ref[...] = part[...].astype(BF16)


def update_kernel(meta_ref, mem_hbm, *refs):
    count = 4
    hbm, new_hbm, bufs = refs[:count], refs[count], refs[count + 1 : 2 * count + 1]
    state, keys, vals, decays, fresh, sems, state_sems, new_sems = refs[2 * count + 1 :]
    loads = copies(hbm, bufs, sems)
    start(loads)
    state_loads = state_copies(meta_ref, mem_hbm, state, state_sems)
    start(state_loads)
    moved_ref, vals_ref, from_after, from_before = bufs
    loads[0].wait()
    loads[1].wait()
    rowd, cold = iota((LOCAL, HEADS * 128), 0), iota((LOCAL, HEADS * 128), 1)
    double = (rowd == (cold // 128) * HEAD + cold % HEAD).astype(BF16)
    doubled = dot(vals_ref[...].astype(BF16), double)
    lane = iota((SLOTS, 128), 1)
    for h in range(HEADS):
        head_lane = lane % HEADS == h
        for p in range(2):
            half = lane // HEAD == p
            cols = slice(p * 128, (p + 1) * 128)
            for t in range(STEPS):
                at = pl.ds(t * 8 + p * HEADS + h, SLOTS, stride=STEPS * 8)
                keys[at, :] = jnp.where(head_lane, cut(moved_ref, t)[:, cols], 0.0)
                vals[at, :] = jnp.where(half, cut(doubled, t)[:, h * 128 : (h + 1) * 128], 0.0)
            whole = jnp.where(head_lane, cut(moved_ref, STEPS)[:, cols], 0.0)
            high = whole.astype(BF16).astype(F32)
            decays[pl.ds(p * HEADS + h, SLOTS, stride=16), :] = high
            decays[pl.ds(8 + p * HEADS + h, SLOTS, stride=16), :] = whole - high
    ones = ((iota((16, 128), 0) // HEADS) % 2 == iota((16, 128), 1) // HEAD).astype(BF16)
    for copy in loads[2:] + state_loads:
        copy.wait()
    place_received(meta_ref, (from_before, from_after), state)
    news = []
    for q in range(SLOTS):
        here = slice(q * STATE_ROWS, (q + 1) * STATE_ROWS)
        rows = slice(q * STEPS * 8, (q + 1) * STEPS * 8)
        fade = dot_rows(decays[q * 16 : (q + 1) * 16, :].astype(BF16), ones)
        grown = dot_rows(keys[rows, :].astype(BF16), vals[rows, :].astype(BF16))
        fresh[here, :] = fade * state[here, :] + grown
        news.append(pltpu.make_async_copy(fresh.at[here, :], new_hbm.at[here, :], new_sems.at[q]))
        news[-1].start()
    for copy in news:
        copy.wait()


def cost(flops, bytes_accessed):
    return pl.CostEstimate(flops=flops, bytes_accessed=bytes_accessed, transcendentals=0)


def tiles_view(a):
    lead, mid, width = a.shape
    return a.reshape(lead, mid, width // 128, 128).transpose(0, 2, 1, 3).reshape(lead * width // 128 * mid, 128)


def tiles_back(a, lead, mid, width):
    return a.reshape(lead, width // 128, mid, 128).transpose(0, 2, 1, 3).reshape(lead, mid, width)


def shards(
    layer_entry_vectors,
    tally_of_tokens,
    prior_slot_lookup,
    memory_matrices,
    previous_standardized_entries,
    entry_standardize_scale,
    blend_coefficients,
    acceptance_projection_matrix,
    lookup_projection_matrix,
    payload_projection_matrix,
    forget_map_left_matrix,
    forget_map_right_matrix,
    feature_forget_logloglevel,
    present_token_boost,
    team_standardize_scale,
    final_projection_matrix,
):
    rings = lax.axis_size("seq")
    teams = lax.axis_size("tensor")
    core = lax.axis_index("tensor") % 2
    x = tiles_view(layer_entry_vectors)
    mem = tiles_view(memory_matrices)
    prev = previous_standardized_entries
    lookup, tally = prior_slot_lookup, tally_of_tokens
    left_t = forget_map_left_matrix.T
    shape, scratch, dma = jax.ShapeDtypeStruct, pltpu.VMEM, pltpu.SemaphoreType.DMA
    params = lambda mib: pltpu.CompilerParams(vmem_limit_bytes=mib << 20)
    like = lambda items: [scratch(a.shape, a.dtype) for a in items]
    state_buf = scratch((SLOTS * STATE_ROWS, 128), F32)
    rows_buf = scratch((SLOTS * STEPS * 8, 128), F32)

    packed, left, meta = pl.pallas_call(
        pack_kernel,
        out_shape=[
            shape((PACK_ROWS, 128), BF16), shape((teams,) + left_t.shape, BF16), shape((META,), jnp.int32),
        ],
        in_specs=spec(pl.ANY, 5),
        out_specs=spec(pltpu.VMEM, 1) + spec(pl.ANY, 1) + spec(pltpu.SMEM, 1),
        scratch_shapes=[pltpu.SMEM(lookup.shape, jnp.int32)] * 2
        + like([prev, mem, left_t])
        + [scratch((2 * TILES, 128), F32), dma((5 + teams,))],
        compiler_params=params(PACK_MIB),
        cost_estimate=cost(0, 1 << 20),
        name="pack",
    )(lookup, tally, prev, mem, left_t)
    from_after = lax.ppermute(packed, "seq", [((i + 1) % rings, i) for i in range(rings)])
    from_before = lax.ppermute(packed, "seq", [(i, (i + 1) % rings) for i in range(rings)])
    left = lax.all_to_all(left, "tensor", 0, 0)

    operands = [
        x, entry_standardize_scale.reshape(TILES, 128), prev, from_after, from_before, blend_coefficients,
        acceptance_projection_matrix, lookup_projection_matrix, payload_projection_matrix,
        left, forget_map_right_matrix, feature_forget_logloglevel.reshape(2, 128),
        present_token_boost.reshape(2, 128), team_standardize_scale.reshape(2, 128), final_projection_matrix,
    ]
    part, moved, values, new_shifts = pl.pallas_call(
        main_kernel,
        out_shape=[
            shape((ROWS * TILES, 128), BF16), shape((ROWS + SLOTS, LOCAL), F32), shape((ROWS, LOCAL), F32),
            shape((SLOTS, WIDTH), F32),
        ],
        in_specs=spec(pltpu.SMEM, 1) + spec(pl.ANY, 1 + len(operands)),
        out_specs=spec(pltpu.VMEM, 4),
        scratch_shapes=like(operands)
        + [scratch((ROWS * TILES, 128), F32), scratch((SLOTS, WIDTH), F32), state_buf, rows_buf, rows_buf, scratch((ROWS * TILES, 128), F32)]
        + [dma((len(operands),)), dma((SLOTS,))],
        compiler_params=params(MAIN_MIB),
        cost_estimate=cost(8 * ROWS * WIDTH * LOCAL, 8 << 20),
        name="main",
    )(meta, mem, *operands)

    operands = [moved, values, from_after, from_before]
    new_states = pl.pallas_call(
        update_kernel,
        out_shape=shape((SLOTS * STATE_ROWS, 128), F32),
        in_specs=spec(pltpu.SMEM, 1) + spec(pl.ANY, 1 + len(operands)),
        out_specs=spec(pl.ANY, 1)[0],
        scratch_shapes=like(operands)
        + [state_buf, rows_buf, rows_buf, scratch((SLOTS * 16, 128), F32), state_buf]
        + [dma((len(operands),)), dma((SLOTS,)), dma((SLOTS,))],
        compiler_params=params(MAIN_MIB),
        cost_estimate=cost(1 << 24, 8 << 20),
        name="update",
    )(meta, mem, *operands)

    pairs = [[2 * i, 2 * i + 1] for i in range(teams // 2)]
    chips = [[2 * i + c for i in range(teams // 2)] for c in range(2)]
    half = ROWS * TILES // 2
    both = lax.all_gather(part, "tensor", axis_index_groups=pairs, tiled=False)
    mine = lax.dynamic_slice_in_dim(both, core * half, half, 1).astype(F32).sum(0).astype(BF16)
    spread = lax.all_to_all(
        jnp.broadcast_to(mine[None], (teams // 2,) + mine.shape), "tensor", 0, 0, axis_index_groups=chips
    )
    total = tiles_back(spread.astype(F32).sum(0).astype(BF16), SLOTS // 2, STEPS, WIDTH)
    proj = lax.all_gather(total, "tensor", axis_index_groups=pairs, tiled=True)
    valid = tally[:, None, None] > jnp.arange(STEPS, dtype=jnp.int32)[None, :, None]
    mixed = jnp.where(valid, layer_entry_vectors.astype(F32) + proj.astype(F32), 0.0).astype(BF16)
    return (
        mixed,
        tiles_back(new_states, SLOTS, HEADS, HEAD * HEAD),
        new_shifts,
    )


def solution(mesh):
    in_specs = (
        P("seq", None, None),
        P("seq"),
        P("seq"),
        P("seq", "tensor", None),
        P("seq", None),
        P(),
        P(),
        P(None, "tensor"),
        P(None, "tensor"),
        P(None, "tensor"),
        P("tensor", None),
        P(None, "tensor"),
        P("tensor"),
        P("tensor"),
        P("tensor"),
        P("tensor", None),
    )
    out_specs = (P("seq", None, None), P("seq", "tensor", None), P("seq", None))
    return jax.shard_map(shards, mesh=mesh, in_specs=in_specs, out_specs=out_specs, check_vma=False)
```

```python
import functools

import jax
import jax.numpy as jnp
from jax import lax
from jax.experimental import pallas as pl
from jax.experimental.pallas import tpu as pltpu
from jax.sharding import PartitionSpec as P

EPS = 1e-05
F32 = jnp.float32
BF16 = jnp.bfloat16
HEAD = 64
SLOTS = 16
STEPS = 4
WIDTH = 2048
HEADS = 4
LOCAL = HEADS * HEAD
TILES = WIDTH // 128
ROWS = SLOTS * STEPS
STATE_ROWS = HEADS * HEAD * HEAD // 128
PIECE = STATE_ROWS + TILES
PACK_ROWS = 2 * PIECE + 16
CAME, TALLY, META = SLOTS, SLOTS + 16, 64
PACK_MIB, MAIN_MIB = 60, 52


def spec(space, count):
    return [pl.BlockSpec(memory_space=space)] * count


def dot(a, b):
    return jnp.dot(a, b, preferred_element_type=F32)


def dot_rows(a, b):
    return lax.dot_general(a, b, (((0,), (0,)), ((), ())), preferred_element_type=F32)


def split(a):
    hi = a.astype(BF16)
    return hi, (a - hi.astype(F32)).astype(BF16)


def dot_split(a, b):
    hi, lo = split(a)
    return dot(hi, b) + dot(lo, b)


def iota(shape, dim):
    return lax.broadcasted_iota(jnp.int32, shape, dim)


def column_of(meta_ref, shape):
    rows = iota(shape, 0)
    out = jnp.zeros(shape, jnp.int32)
    for q in range(SLOTS):
        out = jnp.where(rows == q, meta_ref[TALLY + q], out)
    return out


def row_of(ref):
    return jnp.concatenate([ref[i : i + 1, :] for i in range(ref.shape[0])], axis=1)


def start(items):
    for copy in items:
        copy.start()


def place():
    count = lax.axis_size("seq")
    me = lax.axis_index("seq")
    return me, jnp.where(me == 0, count - 1, me - 1)


def pack_kernel(
    lookup_hbm, tally_hbm, prev_hbm, mem_hbm, left_hbm, out_ref, left_out, meta_ref,
    lookup_ref, tally_ref, prev, mem, left, tile, sems,
):
    loads = copies(
        (lookup_hbm, prev_hbm, mem_hbm, left_hbm, tally_hbm), (lookup_ref, prev, mem, left, tally_ref), sems
    )
    start(loads)
    me, behind = place()
    first = me * SLOTS
    loads[3].wait()
    sends = [pltpu.make_async_copy(left, left_out.at[n], sems.at[5 + n]) for n in range(left_out.shape[0])]
    start(sends)
    loads[0].wait()
    kept = jnp.int32(0)
    slots, wants = [jnp.int32(0)] * 2, [jnp.int32(0)] * 2
    for q in range(SLOTS):
        at = lookup_ref[q] - first
        own = (at >= 0) & (at < SLOTS)
        at = jnp.where(own, at, 0)
        kept = kept | jnp.where(own, jnp.int32(1) << at, 0)
        meta_ref[q] = at
        owner = lookup_ref[q] >> (SLOTS.bit_length() - 1)
        for n, mine in enumerate((jnp.logical_not(own) & (owner == behind), jnp.logical_not(own) & (owner != behind))):
            slots[n] = jnp.where(mine, q, slots[n])
            wants[n] = jnp.where(mine, lookup_ref[q] & (SLOTS - 1), wants[n])
    low, high = jnp.int32(0), jnp.int32(0)
    for s in range(SLOTS):
        high = jnp.where((kept >> s) & 1 == 0, s, high)
        low = jnp.where((kept >> (SLOTS - 1 - s)) & 1 == 0, SLOTS - 1 - s, low)
    for n, free in enumerate((low, high)):
        meta_ref[slots[n]] = free
        meta_ref[CAME + n] = slots[n]
        meta_ref[CAME + 2 + n] = wants[n]
        meta_ref[CAME + 4 + n] = free
    out_ref[2 * PIECE :, :] = jnp.full((16, 128), low, jnp.int32).astype(F32).astype(BF16)
    loads[1].wait()
    for n, slot in enumerate((low, high)):
        row = prev[pl.ds(slot, 1), :]
        for c in range(TILES):
            tile[n * TILES + c : n * TILES + c + 1, :] = row[:, c * 128 : (c + 1) * 128]
    loads[2].wait()
    for n, slot in enumerate((low, high)):
        begin = pl.multiple_of(slot * STATE_ROWS, STATE_ROWS)
        out_ref[n * PIECE : n * PIECE + STATE_ROWS, :] = mem[pl.ds(begin, STATE_ROWS), :].astype(BF16)
        out_ref[n * PIECE + STATE_ROWS : (n + 1) * PIECE, :] = tile[n * TILES : (n + 1) * TILES, :].astype(BF16)
    loads[4].wait()
    for q in range(SLOTS):
        meta_ref[TALLY + q] = tally_ref[q]
    for copy in sends:
        copy.wait()


def pick(recv_ref, wanted, begin, count):
    low = recv_ref[2 * PIECE :, :].astype(F32)[:1, :]
    is_low = low == wanted.astype(F32)
    rows = [recv_ref[at : at + count, :].astype(F32) for at in (begin, PIECE + begin)]
    return jnp.where(is_low, rows[0], rows[1])


def copies(sources_, targets, sems):
    return [pltpu.make_async_copy(a, b, sems.at[n]) for n, (a, b) in enumerate(zip(sources_, targets))]


def cut(a, t):
    return a[t * SLOTS : (t + 1) * SLOTS, :]


def place_received(meta_ref, received, state):
    for n, recv_ref in enumerate(received):
        begin = pl.multiple_of(meta_ref[CAME + 4 + n] * STATE_ROWS, STATE_ROWS)
        state[pl.ds(begin, STATE_ROWS), :] = pick(recv_ref, meta_ref[CAME + 2 + n], 0, STATE_ROWS)


def state_of(meta_ref, state, q):
    return state[pl.ds(pl.multiple_of(meta_ref[q] * STATE_ROWS, STATE_ROWS), STATE_ROWS), :]


def main_kernel(meta_ref, mem_hbm, *refs):
    count = 15
    hbm, (part_ref, moved_ref, vals_ref, last_ref) = refs[:count], refs[count : count + 4]
    bufs = refs[count + 4 : 2 * count + 4]
    x32, shift, state, reads, heads, part, ordered, sems, state_sem = refs[2 * count + 4 :]
    loads = copies(hbm, bufs, sems)
    start(loads[:-1])
    state_load = pltpu.make_async_copy(mem_hbm, state, state_sem)
    state_load.start()
    loads[-1].start()
    x_ref, gain_ref, prev_ref, from_after, from_before, blend_ref = bufs[:6]
    left_ref, right_ref, base_ref, boost_ref, team_ref, final_ref = bufs[9:]
    loads[0].wait()
    loads[1].wait()
    x32[...] = x_ref[...].astype(F32)
    gain = row_of(gain_ref)
    normed = []
    for t in range(STEPS):
        row = jnp.concatenate([x32[pl.ds(c * STEPS + t, SLOTS, stride=STEPS * TILES), :] for c in range(TILES)], axis=1)
        center = row - jnp.mean(row, axis=-1, keepdims=True)
        spread = jnp.mean(center * center, axis=-1, keepdims=True)
        normed.append(center * lax.rsqrt(spread + EPS) * gain)
    tally = column_of(meta_ref, (SLOTS, 128))[:, :1]
    last = normed[0]
    for t in range(1, STEPS):
        last = jnp.where(tally == t + 1, normed[t], last)
    last_ref[...] = last
    for n in range(2, 6):
        loads[n].wait()
    for q in range(SLOTS):
        shift[q : q + 1, :] = prev_ref[pl.ds(meta_ref[q], 1), :]
    slot = iota((SLOTS, 128), 0)
    moved_rows = [
        pick(recv_ref, meta_ref[CAME + 2 + n], STATE_ROWS, TILES) for n, recv_ref in enumerate((from_before, from_after))
    ]
    shift_in = []
    for c in range(TILES):
        col = shift[:, c * 128 : (c + 1) * 128]
        for n, rows in enumerate(moved_rows):
            col = jnp.where(slot == meta_ref[CAME + n], rows[c : c + 1, :], col)
        shift_in.append(col)
    xn = jnp.concatenate(normed, axis=0)
    change = jnp.concatenate([jnp.concatenate(shift_in, axis=1)] + normed[:-1], axis=0) - xn

    def mix(which):
        return (xn + change * blend_ref[which : which + 1, :]).astype(BF16)

    mixed_rows = mix(3)
    rkv = []
    for n in range(3):
        loads[6 + n].wait()
        rkv.append(dot(mix(n), bufs[6 + n][...]))
    for n in range(9, 14):
        loads[n].wait()
    pre = jnp.zeros((ROWS, left_ref.shape[1]), F32)
    chunk = left_ref.shape[2]
    for n in range(left_ref.shape[0]):
        pre = pre + lax.dot_general(
            mixed_rows[:, n * chunk : (n + 1) * chunk], left_ref[n], (((1,), (1,)), ((), ())), preferred_element_type=F32
        )
    lora = jnp.tanh(pre).astype(BF16)
    decay = jnp.exp(-jnp.exp(row_of(base_ref) + dot(lora, right_ref[...])))
    r = [cut(rkv[0], t) for t in range(STEPS)]
    k = [cut(rkv[1], t) for t in range(STEPS)]
    v = [cut(rkv[2], t) for t in range(STEPS)]
    d = [jnp.where(tally > t, cut(decay, t), 1.0) for t in range(STEPS)]
    kept = [jnp.where(tally > t, k[t], 0.0) for t in range(STEPS)]
    boost = row_of(boost_ref)

    run, reach = r[0] * 0.0 + 1.0, []
    for t in range(STEPS):
        reach.append(r[t] * run)
        run = run * d[t]
    tail, coefs = None, [None] * STEPS
    for t in reversed(range(STEPS)):
        coefs[t] = kept[t] if tail is None else kept[t] * tail
        tail = d[t] if tail is None else tail * d[t]
    pairs, terms = [], []
    for t in range(STEPS):
        pairs.append((t, t))
        terms.append(r[t] * boost * k[t])
        weight = r[t]
        for s in reversed(range(t)):
            pairs.append((t, s))
            terms.append(weight * kept[s])
            weight = weight * d[s]
    row256, col256 = iota((LOCAL, LOCAL), 0), iota((LOCAL, LOCAL), 1)
    same_head = (row256 // HEAD == col256 // HEAD).astype(BF16)
    sums = dot_split(jnp.concatenate(terms, axis=0), same_head)
    within = [None] * STEPS
    for n, (t, s) in enumerate(pairs):
        term = cut(sums, n) * v[s]
        within[t] = term if within[t] is None else within[t] + term

    source = (col256 % HEADS) * HEAD + ((col256 // HEADS) % (HEAD // 2)) * 2 + col256 // 128
    reorder = (row256 == source).astype(BF16)
    moved = dot_split(jnp.concatenate(reach + coefs + [run], axis=0), reorder)
    moved_ref[...] = moved[STEPS * SLOTS :, :]
    vals_ref[...] = rkv[2]

    lane = iota((SLOTS, 128), 1)
    for h in range(HEADS):
        head_lane = lane % HEADS == h
        for p in range(2):
            for t in range(STEPS):
                at = pl.ds(t * 8 + p * HEADS + h, SLOTS, stride=STEPS * 8)
                reads[at, :] = jnp.where(head_lane, cut(moved, t)[:, p * 128 : (p + 1) * 128], 0.0)
    state_load.wait()
    place_received(meta_ref, (from_before, from_after), state)
    for q in range(SLOTS):
        rows = slice(q * STEPS * 8, (q + 1) * STEPS * 8)
        now = state_of(meta_ref, state, q)
        heads[rows, :] = dot(reads[rows, :].astype(BF16), now.astype(BF16))

    outs = []
    left_half = lane < HEAD
    for t in range(STEPS):
        def read(p, h):
            return heads[pl.ds(t * 8 + p * HEADS + h, SLOTS, stride=STEPS * 8), :]

        cols = []
        for h in range(0, HEADS, 2):
            a, b, c, e = read(0, h), read(1, h), read(0, h + 1), read(1, h + 1)
            cols.append(jnp.where(left_half, a, e) + pltpu.roll(jnp.where(left_half, c, b), HEAD, 1))
        outs.append(jnp.concatenate(cols, axis=1) + within[t])
    y = jnp.concatenate(outs, axis=0)
    center = y - dot_split(y, same_head) * (1.0 / HEAD)
    spread = dot_split(center * center, same_head) * (1.0 / HEAD)
    g = center * lax.rsqrt(spread + EPS) * row_of(team_ref)
    for t in range(STEPS):
        for c in range(LOCAL // 128):
            ordered[c, pl.ds(t, SLOTS, stride=STEPS), :] = cut(g, t)[:, c * 128 : (c + 1) * 128]
    g = jnp.concatenate([ordered[c] for c in range(LOCAL // 128)], axis=1).astype(BF16)
    loads[14].wait()
    proj = dot(g, final_ref[...])
    for q in range(SLOTS):
        rows = proj[q * STEPS : (q + 1) * STEPS, :]
        for c in range(0, TILES, 2):
            at = (q * TILES + c) * STEPS
            part[at : at + 2 * STEPS, :] = jnp.concatenate(
                [rows[:, c * 128 : (c + 1) * 128], rows[:, (c + 1) * 128 : (c + 2) * 128]], axis=0
            )
    part_ref[...] = part[...].astype(BF16)


def update_kernel(meta_ref, mem_hbm, *refs):
    count = 4
    hbm, new_hbm, bufs = refs[:count], refs[count], refs[count + 1 : 2 * count + 1]
    state, keys, vals, decays, fresh, sems, state_sem, new_sems = refs[2 * count + 1 :]
    loads = copies(hbm, bufs, sems)
    start(loads)
    state_load = pltpu.make_async_copy(mem_hbm, state, state_sem)
    state_load.start()
    moved_ref, vals_ref, from_after, from_before = bufs
    loads[0].wait()
    loads[1].wait()
    rowd, cold = iota((LOCAL, HEADS * 128), 0), iota((LOCAL, HEADS * 128), 1)
    double = (rowd == (cold // 128) * HEAD + cold % HEAD).astype(BF16)
    doubled = dot(vals_ref[...].astype(BF16), double)
    lane = iota((SLOTS, 128), 1)
    for h in range(HEADS):
        head_lane = lane % HEADS == h
        for p in range(2):
            half = lane // HEAD == p
            cols = slice(p * 128, (p + 1) * 128)
            for t in range(STEPS):
                at = pl.ds(t * 8 + p * HEADS + h, SLOTS, stride=STEPS * 8)
                keys[at, :] = jnp.where(head_lane, cut(moved_ref, t)[:, cols], 0.0)
                vals[at, :] = jnp.where(half, cut(doubled, t)[:, h * 128 : (h + 1) * 128], 0.0)
            whole = jnp.where(head_lane, cut(moved_ref, STEPS)[:, cols], 0.0)
            high = whole.astype(BF16).astype(F32)
            decays[pl.ds(p * HEADS + h, SLOTS, stride=16), :] = high
            decays[pl.ds(8 + p * HEADS + h, SLOTS, stride=16), :] = whole - high
    ones = ((iota((16, 128), 0) // HEADS) % 2 == iota((16, 128), 1) // HEAD).astype(BF16)
    for copy in loads[2:] + [state_load]:
        copy.wait()
    place_received(meta_ref, (from_before, from_after), state)
    news = []
    for q in range(SLOTS):
        here = slice(q * STATE_ROWS, (q + 1) * STATE_ROWS)
        rows = slice(q * STEPS * 8, (q + 1) * STEPS * 8)
        fade = dot_rows(decays[q * 16 : (q + 1) * 16, :].astype(BF16), ones)
        grown = dot_rows(keys[rows, :].astype(BF16), vals[rows, :].astype(BF16))
        fresh[here, :] = fade * state_of(meta_ref, state, q) + grown
        news.append(pltpu.make_async_copy(fresh.at[here, :], new_hbm.at[here, :], new_sems.at[q]))
        news[-1].start()
    for copy in news:
        copy.wait()


def cost(flops, bytes_accessed):
    return pl.CostEstimate(flops=flops, bytes_accessed=bytes_accessed, transcendentals=0)


def tiles_view(a):
    lead, mid, width = a.shape
    return a.reshape(lead, mid, width // 128, 128).transpose(0, 2, 1, 3).reshape(lead * width // 128 * mid, 128)


def tiles_back(a, lead, mid, width):
    return a.reshape(lead, width // 128, mid, 128).transpose(0, 2, 1, 3).reshape(lead, mid, width)


def shards(
    layer_entry_vectors,
    tally_of_tokens,
    prior_slot_lookup,
    memory_matrices,
    previous_standardized_entries,
    entry_standardize_scale,
    blend_coefficients,
    acceptance_projection_matrix,
    lookup_projection_matrix,
    payload_projection_matrix,
    forget_map_left_matrix,
    forget_map_right_matrix,
    feature_forget_logloglevel,
    present_token_boost,
    team_standardize_scale,
    final_projection_matrix,
):
    rings = lax.axis_size("seq")
    teams = lax.axis_size("tensor")
    core = lax.axis_index("tensor") % 2
    x = tiles_view(layer_entry_vectors)
    mem = tiles_view(memory_matrices)
    prev = previous_standardized_entries
    lookup, tally = prior_slot_lookup, tally_of_tokens
    left_t = forget_map_left_matrix.T
    shape, scratch, dma = jax.ShapeDtypeStruct, pltpu.VMEM, pltpu.SemaphoreType.DMA
    params = lambda mib: pltpu.CompilerParams(vmem_limit_bytes=mib << 20)
    like = lambda items: [scratch(a.shape, a.dtype) for a in items]
    state_buf = scratch((SLOTS * STATE_ROWS, 128), F32)
    rows_buf = scratch((SLOTS * STEPS * 8, 128), F32)

    packed, left, meta = pl.pallas_call(
        pack_kernel,
        out_shape=[
            shape((PACK_ROWS, 128), BF16), shape((teams,) + left_t.shape, BF16), shape((META,), jnp.int32),
        ],
        in_specs=spec(pl.ANY, 5),
        out_specs=spec(pltpu.VMEM, 1) + spec(pl.ANY, 1) + spec(pltpu.SMEM, 1),
        scratch_shapes=[pltpu.SMEM(lookup.shape, jnp.int32)] * 2
        + like([prev, mem, left_t])
        + [scratch((2 * TILES, 128), F32), dma((5 + teams,))],
        compiler_params=params(PACK_MIB),
        cost_estimate=cost(0, 1 << 20),
        name="pack",
    )(lookup, tally, prev, mem, left_t)
    from_after = lax.ppermute(packed, "seq", [((i + 1) % rings, i) for i in range(rings)])
    from_before = lax.ppermute(packed, "seq", [(i, (i + 1) % rings) for i in range(rings)])
    left = lax.all_to_all(left, "tensor", 0, 0)

    operands = [
        x, entry_standardize_scale.reshape(TILES, 128), prev, from_after, from_before, blend_coefficients,
        acceptance_projection_matrix, lookup_projection_matrix, payload_projection_matrix,
        left, forget_map_right_matrix, feature_forget_logloglevel.reshape(2, 128),
        present_token_boost.reshape(2, 128), team_standardize_scale.reshape(2, 128), final_projection_matrix,
    ]
    part, moved, values, new_shifts = pl.pallas_call(
        main_kernel,
        out_shape=[
            shape((ROWS * TILES, 128), BF16), shape((ROWS + SLOTS, LOCAL), F32), shape((ROWS, LOCAL), F32),
            shape((SLOTS, WIDTH), F32),
        ],
        in_specs=spec(pltpu.SMEM, 1) + spec(pl.ANY, 1 + len(operands)),
        out_specs=spec(pltpu.VMEM, 4),
        scratch_shapes=like(operands)
        + [scratch((ROWS * TILES, 128), F32), scratch((SLOTS, WIDTH), F32), state_buf, rows_buf, rows_buf, scratch((ROWS * TILES, 128), F32)]
        + [scratch((LOCAL // 128, ROWS, 128), F32), dma((len(operands),)), dma],
        compiler_params=params(MAIN_MIB),
        cost_estimate=cost(8 * ROWS * WIDTH * LOCAL, 8 << 20),
        name="main",
    )(meta, mem, *operands)

    operands = [moved, values, from_after, from_before]
    new_states = pl.pallas_call(
        update_kernel,
        out_shape=shape((SLOTS * STATE_ROWS, 128), F32),
        in_specs=spec(pltpu.SMEM, 1) + spec(pl.ANY, 1 + len(operands)),
        out_specs=spec(pl.ANY, 1)[0],
        scratch_shapes=like(operands)
        + [state_buf, rows_buf, rows_buf, scratch((SLOTS * 16, 128), F32), state_buf]
        + [dma((len(operands),)), dma, dma((SLOTS,))],
        compiler_params=params(MAIN_MIB),
        cost_estimate=cost(1 << 24, 8 << 20),
        name="update",
    )(meta, mem, *operands)

    pairs = [[2 * i, 2 * i + 1] for i in range(teams // 2)]
    chips = [[2 * i + c for i in range(teams // 2)] for c in range(2)]
    half = ROWS * TILES // 2
    both = lax.all_gather(part, "tensor", axis_index_groups=pairs, tiled=False)
    mine = lax.dynamic_slice_in_dim(both, core * half, half, 1).astype(F32).sum(0).astype(BF16)
    spread = lax.all_to_all(
        jnp.broadcast_to(mine[None], (teams // 2,) + mine.shape), "tensor", 0, 0, axis_index_groups=chips
    )
    total = tiles_back(spread.astype(F32).sum(0).astype(BF16), SLOTS // 2, STEPS, WIDTH)
    proj = lax.all_gather(total, "tensor", axis_index_groups=pairs, tiled=True)
    valid = tally[:, None, None] > jnp.arange(STEPS, dtype=jnp.int32)[None, :, None]
    mixed = jnp.where(valid, layer_entry_vectors.astype(F32) + proj.astype(F32), 0.0).astype(BF16)
    return (
        mixed,
        tiles_back(new_states, SLOTS, HEADS, HEAD * HEAD),
        new_shifts,
    )


def solution(mesh):
    in_specs = (
        P("seq", None, None),
        P("seq"),
        P("seq"),
        P("seq", "tensor", None),
        P("seq", None),
        P(),
        P(),
        P(None, "tensor"),
        P(None, "tensor"),
        P(None, "tensor"),
        P("tensor", None),
        P(None, "tensor"),
        P("tensor"),
        P("tensor"),
        P("tensor"),
        P("tensor", None),
    )
    out_specs = (P("seq", None, None), P("seq", "tensor", None), P("seq", None))
    return jax.shard_map(shards, mesh=mesh, in_specs=in_specs, out_specs=out_specs, check_vma=False)
```

```python
import functools

import jax
import jax.numpy as jnp
from jax import lax
from jax.experimental import pallas as pl
from jax.experimental.pallas import tpu as pltpu
from jax.sharding import PartitionSpec as P

EPS = 1e-05
F32 = jnp.float32
BF16 = jnp.bfloat16
HEAD = 64
SLOTS = 16
STEPS = 4
WIDTH = 2048
HEADS = 4
LOCAL = HEADS * HEAD
TILES = WIDTH // 128
ROWS = SLOTS * STEPS
STATE_ROWS = HEADS * HEAD * HEAD // 128
PIECE = STATE_ROWS + TILES
PACK_ROWS = 2 * PIECE + 16
CAME, TALLY, META = SLOTS, SLOTS + 16, 64
PACK_MIB, MAIN_MIB = 60, 52


def spec(space, count):
    return [pl.BlockSpec(memory_space=space)] * count


def dot(a, b):
    return jnp.dot(a, b, preferred_element_type=F32)


def dot_rows(a, b):
    return lax.dot_general(a, b, (((0,), (0,)), ((), ())), preferred_element_type=F32)


def split(a):
    hi = a.astype(BF16)
    return hi, (a - hi.astype(F32)).astype(BF16)


def dot_split(a, b):
    hi, lo = split(a)
    return dot(hi, b) + dot(lo, b)


def iota(shape, dim):
    return lax.broadcasted_iota(jnp.int32, shape, dim)


def column_of(meta_ref, shape):
    rows = iota(shape, 0)
    out = jnp.zeros(shape, jnp.int32)
    for q in range(SLOTS):
        out = jnp.where(rows == q, meta_ref[TALLY + q], out)
    return out


def row_of(ref):
    return jnp.concatenate([ref[i : i + 1, :] for i in range(ref.shape[0])], axis=1)


def start(items):
    for copy in items:
        copy.start()


def place():
    count = lax.axis_size("seq")
    me = lax.axis_index("seq")
    return me, jnp.where(me == 0, count - 1, me - 1)


def pack_kernel(
    lookup_hbm, tally_hbm, prev_hbm, mem_hbm, left_hbm, out_ref, left_out, meta_ref,
    lookup_ref, tally_ref, prev, mem, left, tile, sems,
):
    loads = copies(
        (lookup_hbm, prev_hbm, mem_hbm, left_hbm, tally_hbm), (lookup_ref, prev, mem, left, tally_ref), sems
    )
    start(loads)
    me, behind = place()
    first = me * SLOTS
    loads[3].wait()
    sends = [pltpu.make_async_copy(left, left_out.at[n], sems.at[5 + n]) for n in range(left_out.shape[0])]
    start(sends)
    loads[0].wait()
    kept = jnp.int32(0)
    slots, wants = [jnp.int32(0)] * 2, [jnp.int32(0)] * 2
    for q in range(SLOTS):
        at = lookup_ref[q] - first
        own = (at >= 0) & (at < SLOTS)
        at = jnp.where(own, at, 0)
        kept = kept | jnp.where(own, jnp.int32(1) << at, 0)
        meta_ref[q] = at
        owner = lookup_ref[q] >> (SLOTS.bit_length() - 1)
        for n, mine in enumerate((jnp.logical_not(own) & (owner == behind), jnp.logical_not(own) & (owner != behind))):
            slots[n] = jnp.where(mine, q, slots[n])
            wants[n] = jnp.where(mine, lookup_ref[q] & (SLOTS - 1), wants[n])
    low, high = jnp.int32(0), jnp.int32(0)
    for s in range(SLOTS):
        high = jnp.where((kept >> s) & 1 == 0, s, high)
        low = jnp.where((kept >> (SLOTS - 1 - s)) & 1 == 0, SLOTS - 1 - s, low)
    for n, free in enumerate((low, high)):
        meta_ref[slots[n]] = free
        meta_ref[CAME + n] = slots[n]
        meta_ref[CAME + 2 + n] = wants[n]
        meta_ref[CAME + 4 + n] = free
    out_ref[2 * PIECE :, :] = jnp.full((16, 128), low, jnp.int32).astype(F32).astype(BF16)
    loads[1].wait()
    for n, slot in enumerate((low, high)):
        row = prev[pl.ds(slot, 1), :]
        for c in range(TILES):
            tile[n * TILES + c : n * TILES + c + 1, :] = row[:, c * 128 : (c + 1) * 128]
    loads[2].wait()
    for n, slot in enumerate((low, high)):
        begin = pl.multiple_of(slot * STATE_ROWS, STATE_ROWS)
        out_ref[n * PIECE : n * PIECE + STATE_ROWS, :] = mem[pl.ds(begin, STATE_ROWS), :].astype(BF16)
        out_ref[n * PIECE + STATE_ROWS : (n + 1) * PIECE, :] = tile[n * TILES : (n + 1) * TILES, :].astype(BF16)
    loads[4].wait()
    for q in range(SLOTS):
        meta_ref[TALLY + q] = tally_ref[q]
    for copy in sends:
        copy.wait()


def pick(recv_ref, wanted, begin, count):
    low = recv_ref[2 * PIECE :, :].astype(F32)[:1, :]
    is_low = low == wanted.astype(F32)
    rows = [recv_ref[at : at + count, :].astype(F32) for at in (begin, PIECE + begin)]
    return jnp.where(is_low, rows[0], rows[1])


def copies(sources_, targets, sems):
    return [pltpu.make_async_copy(a, b, sems.at[n]) for n, (a, b) in enumerate(zip(sources_, targets))]


def cut(a, t):
    return a[t * SLOTS : (t + 1) * SLOTS, :]


def place_received(meta_ref, received, state):
    for n, recv_ref in enumerate(received):
        begin = pl.multiple_of(meta_ref[CAME + 4 + n] * STATE_ROWS, STATE_ROWS)
        state[pl.ds(begin, STATE_ROWS), :] = pick(recv_ref, meta_ref[CAME + 2 + n], 0, STATE_ROWS)


def state_of(meta_ref, state, q):
    return state[pl.ds(pl.multiple_of(meta_ref[q] * STATE_ROWS, STATE_ROWS), STATE_ROWS), :]


def norm_kernel(meta_ref, x_hbm, gain_hbm, *refs):
    hbm, (xn_ref, last_ref, small_ref), (x_ref, gain_ref), bufs = refs[:3], refs[3:6], refs[6:8], refs[8:11]
    x32, sems = refs[11:]
    loads = copies((x_hbm, gain_hbm) + hbm, (x_ref, gain_ref) + bufs, sems)
    start(loads)
    loads[0].wait()
    loads[1].wait()
    x32[...] = x_ref[...].astype(F32)
    gain = row_of(gain_ref)
    normed = []
    for t in range(STEPS):
        row = jnp.concatenate([x32[pl.ds(c * STEPS + t, SLOTS, stride=STEPS * TILES), :] for c in range(TILES)], axis=1)
        center = row - jnp.mean(row, axis=-1, keepdims=True)
        spread = jnp.mean(center * center, axis=-1, keepdims=True)
        normed.append(center * lax.rsqrt(spread + EPS) * gain)
    tally = column_of(meta_ref, (SLOTS, 128))[:, :1]
    last = normed[0]
    for t in range(1, STEPS):
        last = jnp.where(tally == t + 1, normed[t], last)
    last_ref[...] = last
    for t in range(STEPS):
        xn_ref[t * SLOTS : (t + 1) * SLOTS, :] = normed[t]
    small_ref[6:8, :] = jnp.zeros((2, 128), F32)
    for n in range(3):
        loads[2 + n].wait()
        small_ref[2 * n : 2 * n + 2, :] = bufs[n][...]


def main_kernel(meta_ref, mem_hbm, *refs):
    count = 12
    hbm, (part_ref, moved_ref, vals_ref) = refs[:count], refs[count : count + 3]
    bufs = refs[count + 3 : 2 * count + 3]
    shift, state, reads, heads, part, ordered, sems, state_sem = refs[2 * count + 3 :]
    loads = copies(hbm, bufs, sems)
    start(loads[:-1])
    state_load = pltpu.make_async_copy(mem_hbm, state, state_sem)
    state_load.start()
    loads[-1].start()
    xn_ref, prev_ref, from_after, from_before, blend_ref = bufs[:5]
    left_ref, right_ref, small_ref, final_ref = bufs[8:]
    tally = column_of(meta_ref, (SLOTS, 128))[:, :1]
    for n in range(5):
        loads[n].wait()
    for q in range(SLOTS):
        shift[q : q + 1, :] = prev_ref[pl.ds(meta_ref[q], 1), :]
    slot = iota((SLOTS, 128), 0)
    moved_rows = [
        pick(recv_ref, meta_ref[CAME + 2 + n], STATE_ROWS, TILES) for n, recv_ref in enumerate((from_before, from_after))
    ]
    shift_in = []
    for c in range(TILES):
        col = shift[:, c * 128 : (c + 1) * 128]
        for n, rows in enumerate(moved_rows):
            col = jnp.where(slot == meta_ref[CAME + n], rows[c : c + 1, :], col)
        shift_in.append(col)
    xn = xn_ref[...]
    change = jnp.concatenate([jnp.concatenate(shift_in, axis=1), xn[: (STEPS - 1) * SLOTS, :]], axis=0) - xn

    def mix(which):
        return (xn + change * blend_ref[which : which + 1, :]).astype(BF16)

    mixed_rows = mix(3)
    rkv = []
    for n in range(3):
        loads[5 + n].wait()
        rkv.append(dot(mix(n), bufs[5 + n][...]))
    for n in range(8, 11):
        loads[n].wait()
    pre = jnp.zeros((ROWS, left_ref.shape[1]), F32)
    chunk = left_ref.shape[2]
    for n in range(left_ref.shape[0]):
        pre = pre + lax.dot_general(
            mixed_rows[:, n * chunk : (n + 1) * chunk], left_ref[n], (((1,), (1,)), ((), ())), preferred_element_type=F32
        )
    lora = jnp.tanh(pre).astype(BF16)
    decay = jnp.exp(-jnp.exp(row_of(small_ref[0:2, :]) + dot(lora, right_ref[...])))
    r = [cut(rkv[0], t) for t in range(STEPS)]
    k = [cut(rkv[1], t) for t in range(STEPS)]
    v = [cut(rkv[2], t) for t in range(STEPS)]
    d = [jnp.where(tally > t, cut(decay, t), 1.0) for t in range(STEPS)]
    kept = [jnp.where(tally > t, k[t], 0.0) for t in range(STEPS)]
    boost = row_of(small_ref[2:4, :])

    run, reach = r[0] * 0.0 + 1.0, []
    for t in range(STEPS):
        reach.append(r[t] * run)
        run = run * d[t]
    tail, coefs = None, [None] * STEPS
    for t in reversed(range(STEPS)):
        coefs[t] = kept[t] if tail is None else kept[t] * tail
        tail = d[t] if tail is None else tail * d[t]
    pairs, terms = [], []
    for t in range(STEPS):
        pairs.append((t, t))
        terms.append(r[t] * boost * k[t])
        weight = r[t]
        for s in reversed(range(t)):
            pairs.append((t, s))
            terms.append(weight * kept[s])
            weight = weight * d[s]
    row256, col256 = iota((LOCAL, LOCAL), 0), iota((LOCAL, LOCAL), 1)
    same_head = (row256 // HEAD == col256 // HEAD).astype(BF16)
    sums = dot_split(jnp.concatenate(terms, axis=0), same_head)
    within = [None] * STEPS
    for n, (t, s) in enumerate(pairs):
        term = cut(sums, n) * v[s]
        within[t] = term if within[t] is None else within[t] + term

    source = (col256 % HEADS) * HEAD + ((col256 // HEADS) % (HEAD // 2)) * 2 + col256 // 128
    reorder = (row256 == source).astype(BF16)
    moved = dot_split(jnp.concatenate(reach + coefs + [run], axis=0), reorder)
    moved_ref[...] = moved[STEPS * SLOTS :, :]
    vals_ref[...] = rkv[2]

    lane = iota((SLOTS, 128), 1)
    for h in range(HEADS):
        head_lane = lane % HEADS == h
        for p in range(2):
            for t in range(STEPS):
                at = pl.ds(t * 8 + p * HEADS + h, SLOTS, stride=STEPS * 8)
                reads[at, :] = jnp.where(head_lane, cut(moved, t)[:, p * 128 : (p + 1) * 128], 0.0)
    state_load.wait()
    place_received(meta_ref, (from_before, from_after), state)
    for q in range(SLOTS):
        rows = slice(q * STEPS * 8, (q + 1) * STEPS * 8)
        now = state_of(meta_ref, state, q)
        heads[rows, :] = dot(reads[rows, :].astype(BF16), now.astype(BF16))

    outs = []
    left_half = lane < HEAD
    for t in range(STEPS):
        def read(p, h):
            return heads[pl.ds(t * 8 + p * HEADS + h, SLOTS, stride=STEPS * 8), :]

        cols = []
        for h in range(0, HEADS, 2):
            a, b, c, e = read(0, h), read(1, h), read(0, h + 1), read(1, h + 1)
            cols.append(jnp.where(left_half, a, e) + pltpu.roll(jnp.where(left_half, c, b), HEAD, 1))
        outs.append(jnp.concatenate(cols, axis=1) + within[t])
    y = jnp.concatenate(outs, axis=0)
    center = y - dot_split(y, same_head) * (1.0 / HEAD)
    spread = dot_split(center * center, same_head) * (1.0 / HEAD)
    g = center * lax.rsqrt(spread + EPS) * row_of(small_ref[4:6, :])
    for t in range(STEPS):
        for c in range(LOCAL // 128):
            ordered[c, pl.ds(t, SLOTS, stride=STEPS), :] = cut(g, t)[:, c * 128 : (c + 1) * 128]
    g = jnp.concatenate([ordered[c] for c in range(LOCAL // 128)], axis=1).astype(BF16)
    loads[11].wait()
    proj = dot(g, final_ref[...])
    for q in range(SLOTS):
        rows = proj[q * STEPS : (q + 1) * STEPS, :]
        for c in range(0, TILES, 2):
            at = (q * TILES + c) * STEPS
            part[at : at + 2 * STEPS, :] = jnp.concatenate(
                [rows[:, c * 128 : (c + 1) * 128], rows[:, (c + 1) * 128 : (c + 2) * 128]], axis=0
            )
    part_ref[...] = part[...].astype(BF16)


def update_kernel(meta_ref, mem_hbm, *refs):
    count = 4
    hbm, new_hbm, bufs = refs[:count], refs[count], refs[count + 1 : 2 * count + 1]
    state, keys, vals, decays, fresh, sems, state_sem, new_sems = refs[2 * count + 1 :]
    loads = copies(hbm, bufs, sems)
    start(loads)
    state_load = pltpu.make_async_copy(mem_hbm, state, state_sem)
    state_load.start()
    moved_ref, vals_ref, from_after, from_before = bufs
    loads[0].wait()
    loads[1].wait()
    rowd, cold = iota((LOCAL, HEADS * 128), 0), iota((LOCAL, HEADS * 128), 1)
    double = (rowd == (cold // 128) * HEAD + cold % HEAD).astype(BF16)
    doubled = dot(vals_ref[...].astype(BF16), double)
    lane = iota((SLOTS, 128), 1)
    for h in range(HEADS):
        head_lane = lane % HEADS == h
        for p in range(2):
            half = lane // HEAD == p
            cols = slice(p * 128, (p + 1) * 128)
            for t in range(STEPS):
                at = pl.ds(t * 8 + p * HEADS + h, SLOTS, stride=STEPS * 8)
                keys[at, :] = jnp.where(head_lane, cut(moved_ref, t)[:, cols], 0.0)
                vals[at, :] = jnp.where(half, cut(doubled, t)[:, h * 128 : (h + 1) * 128], 0.0)
            whole = jnp.where(head_lane, cut(moved_ref, STEPS)[:, cols], 0.0)
            high = whole.astype(BF16).astype(F32)
            decays[pl.ds(p * HEADS + h, SLOTS, stride=16), :] = high
            decays[pl.ds(8 + p * HEADS + h, SLOTS, stride=16), :] = whole - high
    ones = ((iota((16, 128), 0) // HEADS) % 2 == iota((16, 128), 1) // HEAD).astype(BF16)
    for copy in loads[2:] + [state_load]:
        copy.wait()
    place_received(meta_ref, (from_before, from_after), state)
    news = []
    for q in range(SLOTS):
        here = slice(q * STATE_ROWS, (q + 1) * STATE_ROWS)
        rows = slice(q * STEPS * 8, (q + 1) * STEPS * 8)
        fade = dot_rows(decays[q * 16 : (q + 1) * 16, :].astype(BF16), ones)
        grown = dot_rows(keys[rows, :].astype(BF16), vals[rows, :].astype(BF16))
        fresh[here, :] = fade * state_of(meta_ref, state, q) + grown
        news.append(pltpu.make_async_copy(fresh.at[here, :], new_hbm.at[here, :], new_sems.at[q]))
        news[-1].start()
    for copy in news:
        copy.wait()


def cost(flops, bytes_accessed):
    return pl.CostEstimate(flops=flops, bytes_accessed=bytes_accessed, transcendentals=0)


def tiles_view(a):
    lead, mid, width = a.shape
    return a.reshape(lead, mid, width // 128, 128).transpose(0, 2, 1, 3).reshape(lead * width // 128 * mid, 128)


def tiles_back(a, lead, mid, width):
    return a.reshape(lead, width // 128, mid, 128).transpose(0, 2, 1, 3).reshape(lead, mid, width)


def shards(
    layer_entry_vectors,
    tally_of_tokens,
    prior_slot_lookup,
    memory_matrices,
    previous_standardized_entries,
    entry_standardize_scale,
    blend_coefficients,
    acceptance_projection_matrix,
    lookup_projection_matrix,
    payload_projection_matrix,
    forget_map_left_matrix,
    forget_map_right_matrix,
    feature_forget_logloglevel,
    present_token_boost,
    team_standardize_scale,
    final_projection_matrix,
):
    rings = lax.axis_size("seq")
    teams = lax.axis_size("tensor")
    core = lax.axis_index("tensor") % 2
    x = tiles_view(layer_entry_vectors)
    mem = tiles_view(memory_matrices)
    prev = previous_standardized_entries
    lookup, tally = prior_slot_lookup, tally_of_tokens
    left_t = forget_map_left_matrix.T
    shape, scratch, dma = jax.ShapeDtypeStruct, pltpu.VMEM, pltpu.SemaphoreType.DMA
    params = lambda mib: pltpu.CompilerParams(vmem_limit_bytes=mib << 20)
    like = lambda items: [scratch(a.shape, a.dtype) for a in items]
    state_buf = scratch((SLOTS * STATE_ROWS, 128), F32)
    rows_buf = scratch((SLOTS * STEPS * 8, 128), F32)

    packed, left, meta = pl.pallas_call(
        pack_kernel,
        out_shape=[
            shape((PACK_ROWS, 128), BF16), shape((teams,) + left_t.shape, BF16), shape((META,), jnp.int32),
        ],
        in_specs=spec(pl.ANY, 5),
        out_specs=spec(pltpu.VMEM, 1) + spec(pl.ANY, 1) + spec(pltpu.SMEM, 1),
        scratch_shapes=[pltpu.SMEM(lookup.shape, jnp.int32)] * 2
        + like([prev, mem, left_t])
        + [scratch((2 * TILES, 128), F32), dma((5 + teams,))],
        compiler_params=params(PACK_MIB),
        cost_estimate=cost(0, 1 << 20),
        name="pack",
    )(lookup, tally, prev, mem, left_t)
    from_after = lax.ppermute(packed, "seq", [((i + 1) % rings, i) for i in range(rings)])
    from_before = lax.ppermute(packed, "seq", [(i, (i + 1) % rings) for i in range(rings)])
    left = lax.all_to_all(left, "tensor", 0, 0)

    gain = entry_standardize_scale.reshape(TILES, 128)
    vectors = [
        v.reshape(2, 128) for v in (feature_forget_logloglevel, present_token_boost, team_standardize_scale)
    ]
    xn, new_shifts, small = pl.pallas_call(
        norm_kernel,
        out_shape=[shape((ROWS, WIDTH), F32), shape((SLOTS, WIDTH), F32), shape((8, 128), F32)],
        in_specs=spec(pltpu.SMEM, 1) + spec(pl.ANY, 5),
        out_specs=spec(pltpu.VMEM, 3),
        scratch_shapes=like([x, gain] + vectors) + [scratch((ROWS * TILES, 128), F32), dma((5,))],
        compiler_params=params(MAIN_MIB),
        cost_estimate=cost(0, 4 << 20),
        name="norm",
    )(meta, x, gain, *vectors)

    operands = [
        xn, prev, from_after, from_before, blend_coefficients,
        acceptance_projection_matrix, lookup_projection_matrix, payload_projection_matrix,
        left, forget_map_right_matrix, small, final_projection_matrix,
    ]
    part, moved, values = pl.pallas_call(
        main_kernel,
        out_shape=[
            shape((ROWS * TILES, 128), BF16), shape((ROWS + SLOTS, LOCAL), F32), shape((ROWS, LOCAL), F32),
        ],
        in_specs=spec(pltpu.SMEM, 1) + spec(pl.ANY, 1 + len(operands)),
        out_specs=spec(pltpu.VMEM, 3),
        scratch_shapes=like(operands)
        + [scratch((SLOTS, WIDTH), F32), state_buf, rows_buf, rows_buf, scratch((ROWS * TILES, 128), F32)]
        + [scratch((LOCAL // 128, ROWS, 128), F32), dma((len(operands),)), dma],
        compiler_params=params(MAIN_MIB),
        cost_estimate=cost(8 * ROWS * WIDTH * LOCAL, 8 << 20),
        name="main",
    )(meta, mem, *operands)

    operands = [moved, values, from_after, from_before]
    new_states = pl.pallas_call(
        update_kernel,
        out_shape=shape((SLOTS * STATE_ROWS, 128), F32),
        in_specs=spec(pltpu.SMEM, 1) + spec(pl.ANY, 1 + len(operands)),
        out_specs=spec(pl.ANY, 1)[0],
        scratch_shapes=like(operands)
        + [state_buf, rows_buf, rows_buf, scratch((SLOTS * 16, 128), F32), state_buf]
        + [dma((len(operands),)), dma, dma((SLOTS,))],
        compiler_params=params(MAIN_MIB),
        cost_estimate=cost(1 << 24, 8 << 20),
        name="update",
    )(meta, mem, *operands)

    pairs = [[2 * i, 2 * i + 1] for i in range(teams // 2)]
    chips = [[2 * i + c for i in range(teams // 2)] for c in range(2)]
    half = ROWS * TILES // 2
    both = lax.all_gather(part, "tensor", axis_index_groups=pairs, tiled=False)
    mine = lax.dynamic_slice_in_dim(both, core * half, half, 1).astype(F32).sum(0).astype(BF16)
    spread = lax.all_to_all(
        jnp.broadcast_to(mine[None], (teams // 2,) + mine.shape), "tensor", 0, 0, axis_index_groups=chips
    )
    total = tiles_back(spread.astype(F32).sum(0).astype(BF16), SLOTS // 2, STEPS, WIDTH)
    proj = lax.all_gather(total, "tensor", axis_index_groups=pairs, tiled=True)
    valid = tally[:, None, None] > jnp.arange(STEPS, dtype=jnp.int32)[None, :, None]
    mixed = jnp.where(valid, layer_entry_vectors.astype(F32) + proj.astype(F32), 0.0).astype(BF16)
    return (
        mixed,
        tiles_back(new_states, SLOTS, HEADS, HEAD * HEAD),
        new_shifts,
    )


def solution(mesh):
    in_specs = (
        P("seq", None, None),
        P("seq"),
        P("seq"),
        P("seq", "tensor", None),
        P("seq", None),
        P(),
        P(),
        P(None, "tensor"),
        P(None, "tensor"),
        P(None, "tensor"),
        P("tensor", None),
        P(None, "tensor"),
        P("tensor"),
        P("tensor"),
        P("tensor"),
        P("tensor", None),
    )
    out_specs = (P("seq", None, None), P("seq", "tensor", None), P("seq", None))
    return jax.shard_map(shards, mesh=mesh, in_specs=in_specs, out_specs=out_specs, check_vma=False)
```

```python
import functools

import jax
import jax.numpy as jnp
from jax import lax
from jax.experimental import pallas as pl
from jax.experimental.pallas import tpu as pltpu
from jax.sharding import PartitionSpec as P

EPS = 1e-05
F32 = jnp.float32
BF16 = jnp.bfloat16
HEAD = 64
SLOTS = 16
STEPS = 4
WIDTH = 2048
HEADS = 4
LOCAL = HEADS * HEAD
TILES = WIDTH // 128
ROWS = SLOTS * STEPS
STATE_ROWS = HEADS * HEAD * HEAD // 128
PIECE = STATE_ROWS + TILES
PACK_ROWS = 2 * PIECE + 16
CAME, TALLY, META = SLOTS, SLOTS + 16, 64
READ_STRIDE = STEPS * 8 + 8
PACK_MIB, MAIN_MIB = 60, 52


def spec(space, count):
    return [pl.BlockSpec(memory_space=space)] * count


def dot(a, b):
    return jnp.dot(a, b, preferred_element_type=F32)


def dot_rows(a, b):
    return lax.dot_general(a, b, (((0,), (0,)), ((), ())), preferred_element_type=F32)


def split(a):
    hi = a.astype(BF16)
    return hi, (a - hi.astype(F32)).astype(BF16)


def dot_split(a, b):
    hi, lo = split(a)
    return dot(hi, b) + dot(lo, b)


def iota(shape, dim):
    return lax.broadcasted_iota(jnp.int32, shape, dim)


def column_of(meta_ref, shape):
    rows = iota(shape, 0)
    out = jnp.zeros(shape, jnp.int32)
    for q in range(SLOTS):
        out = jnp.where(rows == q, meta_ref[TALLY + q], out)
    return out


def row_of(ref):
    return jnp.concatenate([ref[i : i + 1, :] for i in range(ref.shape[0])], axis=1)


def start(items):
    for copy in items:
        copy.start()


def place():
    count = lax.axis_size("seq")
    me = lax.axis_index("seq")
    return me, jnp.where(me == 0, count - 1, me - 1)


def pack_kernel(
    lookup_hbm, tally_hbm, prev_hbm, mem_hbm, left_hbm, out_ref, left_out, meta_ref,
    lookup_ref, tally_ref, prev, mem, left, tile, sems,
):
    loads = copies(
        (lookup_hbm, prev_hbm, mem_hbm, left_hbm, tally_hbm), (lookup_ref, prev, mem, left, tally_ref), sems
    )
    start(loads)
    me, behind = place()
    first = me * SLOTS
    loads[3].wait()
    sends = [pltpu.make_async_copy(left, left_out.at[n], sems.at[5 + n]) for n in range(left_out.shape[0])]
    start(sends)
    loads[0].wait()
    kept = jnp.int32(0)
    slots, wants = [jnp.int32(0)] * 2, [jnp.int32(0)] * 2
    for q in range(SLOTS):
        at = lookup_ref[q] - first
        own = (at >= 0) & (at < SLOTS)
        at = jnp.where(own, at, 0)
        kept = kept | jnp.where(own, jnp.int32(1) << at, 0)
        meta_ref[q] = at
        owner = lookup_ref[q] >> (SLOTS.bit_length() - 1)
        for n, mine in enumerate((jnp.logical_not(own) & (owner == behind), jnp.logical_not(own) & (owner != behind))):
            slots[n] = jnp.where(mine, q, slots[n])
            wants[n] = jnp.where(mine, lookup_ref[q] & (SLOTS - 1), wants[n])
    low, high = jnp.int32(0), jnp.int32(0)
    for s in range(SLOTS):
        high = jnp.where((kept >> s) & 1 == 0, s, high)
        low = jnp.where((kept >> (SLOTS - 1 - s)) & 1 == 0, SLOTS - 1 - s, low)
    for n, free in enumerate((low, high)):
        meta_ref[slots[n]] = free
        meta_ref[CAME + n] = slots[n]
        meta_ref[CAME + 2 + n] = wants[n]
        meta_ref[CAME + 4 + n] = free
    out_ref[2 * PIECE :, :] = jnp.full((16, 128), low, jnp.int32).astype(F32).astype(BF16)
    loads[1].wait()
    for n, slot in enumerate((low, high)):
        row = prev[pl.ds(slot, 1), :]
        for c in range(TILES):
            tile[n * TILES + c : n * TILES + c + 1, :] = row[:, c * 128 : (c + 1) * 128]
    loads[2].wait()
    for n, slot in enumerate((low, high)):
        begin = pl.multiple_of(slot * STATE_ROWS, STATE_ROWS)
        out_ref[n * PIECE : n * PIECE + STATE_ROWS, :] = mem[pl.ds(begin, STATE_ROWS), :].astype(BF16)
        out_ref[n * PIECE + STATE_ROWS : (n + 1) * PIECE, :] = tile[n * TILES : (n + 1) * TILES, :].astype(BF16)
    loads[4].wait()
    for q in range(SLOTS):
        meta_ref[TALLY + q] = tally_ref[q]
    for copy in sends:
        copy.wait()


def pick(recv_ref, wanted, begin, count):
    low = recv_ref[2 * PIECE :, :].astype(F32)[:1, :]
    is_low = low == wanted.astype(F32)
    rows = [recv_ref[at : at + count, :].astype(F32) for at in (begin, PIECE + begin)]
    return jnp.where(is_low, rows[0], rows[1])


def copies(sources_, targets, sems):
    return [pltpu.make_async_copy(a, b, sems.at[n]) for n, (a, b) in enumerate(zip(sources_, targets))]


def cut(a, t):
    return a[t * SLOTS : (t + 1) * SLOTS, :]


def place_received(meta_ref, received, state):
    for n, recv_ref in enumerate(received):
        begin = pl.multiple_of(meta_ref[CAME + 4 + n] * STATE_ROWS, STATE_ROWS)
        state[pl.ds(begin, STATE_ROWS), :] = pick(recv_ref, meta_ref[CAME + 2 + n], 0, STATE_ROWS)


def state_of(meta_ref, state, q):
    return state[pl.ds(pl.multiple_of(meta_ref[q] * STATE_ROWS, STATE_ROWS), STATE_ROWS), :]


def norm_kernel(meta_ref, x_hbm, gain_hbm, *refs):
    hbm, (xn_ref, last_ref, small_ref), (x_ref, gain_ref), bufs = refs[:3], refs[3:6], refs[6:8], refs[8:11]
    x32, sems = refs[11:]
    loads = copies((x_hbm, gain_hbm) + hbm, (x_ref, gain_ref) + bufs, sems)
    start(loads)
    loads[0].wait()
    loads[1].wait()
    x32[...] = x_ref[...].astype(F32)
    gain = row_of(gain_ref)
    normed = []
    for t in range(STEPS):
        row = jnp.concatenate([x32[pl.ds(c * STEPS + t, SLOTS, stride=STEPS * TILES), :] for c in range(TILES)], axis=1)
        center = row - jnp.mean(row, axis=-1, keepdims=True)
        spread = jnp.mean(center * center, axis=-1, keepdims=True)
        normed.append(center * lax.rsqrt(spread + EPS) * gain)
    tally = column_of(meta_ref, (SLOTS, 128))[:, :1]
    last = normed[0]
    for t in range(1, STEPS):
        last = jnp.where(tally == t + 1, normed[t], last)
    last_ref[...] = last
    for t in range(STEPS):
        xn_ref[t * SLOTS : (t + 1) * SLOTS, :] = normed[t]
    small_ref[6:8, :] = jnp.zeros((2, 128), F32)
    for n in range(3):
        loads[2 + n].wait()
        small_ref[2 * n : 2 * n + 2, :] = bufs[n][...]


def main_kernel(meta_ref, mem_hbm, *refs):
    count = 12
    hbm, (part_ref, moved_ref, vals_ref) = refs[:count], refs[count : count + 3]
    bufs = refs[count + 3 : 2 * count + 3]
    shift, state, reads, heads, part, ordered, sems, state_sem = refs[2 * count + 3 :]
    loads = copies(hbm, bufs, sems)
    start(loads[5:8] + loads[:5] + loads[8:-1])
    state_load = pltpu.make_async_copy(mem_hbm, state, state_sem)
    state_load.start()
    loads[-1].start()
    xn_ref, prev_ref, from_after, from_before, blend_ref = bufs[:5]
    left_ref, right_ref, small_ref, final_ref = bufs[8:]
    tally = column_of(meta_ref, (SLOTS, 128))[:, :1]
    for n in range(5):
        loads[n].wait()
    for q in range(SLOTS):
        shift[q : q + 1, :] = prev_ref[pl.ds(meta_ref[q], 1), :]
    slot = iota((SLOTS, 128), 0)
    moved_rows = [
        pick(recv_ref, meta_ref[CAME + 2 + n], STATE_ROWS, TILES) for n, recv_ref in enumerate((from_before, from_after))
    ]
    shift_in = []
    for c in range(TILES):
        col = shift[:, c * 128 : (c + 1) * 128]
        for n, rows in enumerate(moved_rows):
            col = jnp.where(slot == meta_ref[CAME + n], rows[c : c + 1, :], col)
        shift_in.append(col)
    xn = xn_ref[...]
    change = jnp.concatenate([jnp.concatenate(shift_in, axis=1), xn[: (STEPS - 1) * SLOTS, :]], axis=0) - xn

    def mix(which):
        return (xn + change * blend_ref[which : which + 1, :]).astype(BF16)

    mixed_rows = mix(3)
    for n in range(8, 11):
        loads[n].wait()
    pre = jnp.zeros((ROWS, left_ref.shape[1]), F32)
    chunk = left_ref.shape[2]
    for n in range(left_ref.shape[0]):
        pre = pre + lax.dot_general(
            mixed_rows[:, n * chunk : (n + 1) * chunk], left_ref[n], (((1,), (1,)), ((), ())), preferred_element_type=F32
        )
    lora = jnp.tanh(pre).astype(BF16)
    decay = jnp.exp(-jnp.exp(row_of(small_ref[0:2, :]) + dot(lora, right_ref[...])))
    row256, col256 = iota((LOCAL, LOCAL), 0), iota((LOCAL, LOCAL), 1)
    same_head = (row256 // HEAD == col256 // HEAD).astype(BF16)
    source = (col256 % HEADS) * HEAD + ((col256 // HEADS) % (HEAD // 2)) * 2 + col256 // 128
    reorder = (row256 == source).astype(BF16)
    rkv = []
    for n in range(3):
        loads[5 + n].wait()
        rkv.append(dot(mix(n), bufs[5 + n][...]))
    r = [cut(rkv[0], t) for t in range(STEPS)]
    k = [cut(rkv[1], t) for t in range(STEPS)]
    v = [cut(rkv[2], t) for t in range(STEPS)]
    d = [jnp.where(tally > t, cut(decay, t), 1.0) for t in range(STEPS)]
    kept = [jnp.where(tally > t, k[t], 0.0) for t in range(STEPS)]
    boost = row_of(small_ref[2:4, :])

    run, reach = jnp.ones_like(r[0]), []
    for t in range(STEPS):
        reach.append(r[t] * run)
        run = run * d[t]
    tail, coefs = None, [None] * STEPS
    for t in reversed(range(STEPS)):
        coefs[t] = kept[t] if tail is None else kept[t] * tail
        tail = d[t] if tail is None else tail * d[t]
    pairs, terms = [], []
    for t in range(STEPS):
        pairs.append((t, t))
        terms.append(r[t] * boost * k[t])
        weight = r[t]
        for s in reversed(range(t)):
            pairs.append((t, s))
            terms.append(weight * kept[s])
            weight = weight * d[s]
    sums = dot_split(jnp.concatenate(terms, axis=0), same_head)
    within = [None] * STEPS
    for n, (t, s) in enumerate(pairs):
        term = cut(sums, n) * v[s]
        within[t] = term if within[t] is None else within[t] + term

    moved = dot_split(jnp.concatenate(reach + coefs + [run], axis=0), reorder)
    moved_ref[...] = moved[STEPS * SLOTS :, :]
    vals_ref[...] = rkv[2]

    lane = iota((SLOTS, 128), 1)
    for h in range(HEADS):
        head_lane = lane % HEADS == h
        for p in range(2):
            for t in range(STEPS):
                at = pl.ds(t * 8 + p * HEADS + h, SLOTS, stride=READ_STRIDE)
                reads[at, :] = jnp.where(head_lane, cut(moved, t)[:, p * 128 : (p + 1) * 128], 0.0)
    state_load.wait()
    place_received(meta_ref, (from_before, from_after), state)
    for q in range(SLOTS):
        rows = slice(q * READ_STRIDE, q * READ_STRIDE + STEPS * 8)
        now = state_of(meta_ref, state, q)
        heads[rows, :] = dot(reads[rows, :].astype(BF16), now.astype(BF16))

    outs = []
    left_half = lane < HEAD
    for t in range(STEPS):
        def read(p, h):
            return heads[pl.ds(t * 8 + p * HEADS + h, SLOTS, stride=READ_STRIDE), :]

        cols = []
        for h in range(0, HEADS, 2):
            a, b, c, e = read(0, h), read(1, h), read(0, h + 1), read(1, h + 1)
            cols.append(jnp.where(left_half, a, e) + pltpu.roll(jnp.where(left_half, c, b), HEAD, 1))
        outs.append(jnp.concatenate(cols, axis=1) + within[t])
    y = jnp.concatenate(outs, axis=0)
    center = y - dot_split(y, same_head) * (1.0 / HEAD)
    spread = dot_split(center * center, same_head) * (1.0 / HEAD)
    g = center * lax.rsqrt(spread + EPS) * row_of(small_ref[4:6, :])
    for t in range(STEPS):
        for c in range(LOCAL // 128):
            ordered[c, pl.ds(t, SLOTS, stride=STEPS), :] = cut(g, t)[:, c * 128 : (c + 1) * 128]
    g = jnp.concatenate([ordered[c] for c in range(LOCAL // 128)], axis=1).astype(BF16)
    loads[11].wait()
    proj = dot(g, final_ref[...])
    for q in range(SLOTS):
        rows = proj[q * STEPS : (q + 1) * STEPS, :]
        for c in range(0, TILES, 2):
            at = (q * TILES + c) * STEPS
            part[at : at + 2 * STEPS, :] = jnp.concatenate(
                [rows[:, c * 128 : (c + 1) * 128], rows[:, (c + 1) * 128 : (c + 2) * 128]], axis=0
            )
    part_ref[...] = part[...].astype(BF16)


def update_kernel(meta_ref, mem_hbm, *refs):
    count = 4
    hbm, new_hbm, bufs = refs[:count], refs[count], refs[count + 1 : 2 * count + 1]
    state, keys, vals, decays, fresh, sems, state_sem, new_sems = refs[2 * count + 1 :]
    loads = copies(hbm, bufs, sems)
    start(loads)
    state_load = pltpu.make_async_copy(mem_hbm, state, state_sem)
    state_load.start()
    moved_ref, vals_ref, from_after, from_before = bufs
    loads[0].wait()
    loads[1].wait()
    rowd, cold = iota((LOCAL, HEADS * 128), 0), iota((LOCAL, HEADS * 128), 1)
    double = (rowd == (cold // 128) * HEAD + cold % HEAD).astype(BF16)
    doubled = dot(vals_ref[...].astype(BF16), double)
    lane = iota((SLOTS, 128), 1)
    for h in range(HEADS):
        head_lane = lane % HEADS == h
        for p in range(2):
            half = lane // HEAD == p
            cols = slice(p * 128, (p + 1) * 128)
            for t in range(STEPS):
                at = pl.ds(t * 8 + p * HEADS + h, SLOTS, stride=STEPS * 8)
                keys[at, :] = jnp.where(head_lane, cut(moved_ref, t)[:, cols], 0.0)
                vals[at, :] = jnp.where(half, cut(doubled, t)[:, h * 128 : (h + 1) * 128], 0.0)
            whole = jnp.where(head_lane, cut(moved_ref, STEPS)[:, cols], 0.0)
            high = whole.astype(BF16).astype(F32)
            decays[pl.ds(p * HEADS + h, SLOTS, stride=16), :] = high
            decays[pl.ds(8 + p * HEADS + h, SLOTS, stride=16), :] = whole - high
    ones = ((iota((16, 128), 0) // HEADS) % 2 == iota((16, 128), 1) // HEAD).astype(BF16)
    for copy in loads[2:] + [state_load]:
        copy.wait()
    place_received(meta_ref, (from_before, from_after), state)
    news = []
    for q in range(SLOTS):
        here = slice(q * STATE_ROWS, (q + 1) * STATE_ROWS)
        rows = slice(q * STEPS * 8, (q + 1) * STEPS * 8)
        fade = dot_rows(decays[q * 16 : (q + 1) * 16, :].astype(BF16), ones)
        grown = dot_rows(keys[rows, :].astype(BF16), vals[rows, :].astype(BF16))
        fresh[here, :] = fade * state_of(meta_ref, state, q) + grown
        news.append(pltpu.make_async_copy(fresh.at[here, :], new_hbm.at[here, :], new_sems.at[q]))
        news[-1].start()
    for copy in news:
        copy.wait()


def cost(flops, bytes_accessed):
    return pl.CostEstimate(flops=flops, bytes_accessed=bytes_accessed, transcendentals=0)


def tiles_view(a):
    lead, mid, width = a.shape
    return a.reshape(lead, mid, width // 128, 128).transpose(0, 2, 1, 3).reshape(lead * width // 128 * mid, 128)


def tiles_back(a, lead, mid, width):
    return a.reshape(lead, width // 128, mid, 128).transpose(0, 2, 1, 3).reshape(lead, mid, width)


def shards(
    layer_entry_vectors,
    tally_of_tokens,
    prior_slot_lookup,
    memory_matrices,
    previous_standardized_entries,
    entry_standardize_scale,
    blend_coefficients,
    acceptance_projection_matrix,
    lookup_projection_matrix,
    payload_projection_matrix,
    forget_map_left_matrix,
    forget_map_right_matrix,
    feature_forget_logloglevel,
    present_token_boost,
    team_standardize_scale,
    final_projection_matrix,
):
    rings = lax.axis_size("seq")
    teams = lax.axis_size("tensor")
    core = lax.axis_index("tensor") % 2
    x = tiles_view(layer_entry_vectors)
    mem = tiles_view(memory_matrices)
    prev = previous_standardized_entries
    lookup, tally = prior_slot_lookup, tally_of_tokens
    left_t = forget_map_left_matrix.T
    shape, scratch, dma = jax.ShapeDtypeStruct, pltpu.VMEM, pltpu.SemaphoreType.DMA
    params = lambda mib: pltpu.CompilerParams(vmem_limit_bytes=mib << 20)
    like = lambda items: [scratch(a.shape, a.dtype) for a in items]
    state_buf = scratch((SLOTS * STATE_ROWS, 128), F32)
    rows_buf = scratch((SLOTS * STEPS * 8, 128), F32)
    read_buf = scratch((SLOTS * READ_STRIDE, 128), F32)

    packed, left, meta = pl.pallas_call(
        pack_kernel,
        out_shape=[
            shape((PACK_ROWS, 128), BF16), shape((teams,) + left_t.shape, BF16), shape((META,), jnp.int32),
        ],
        in_specs=spec(pl.ANY, 5),
        out_specs=spec(pltpu.VMEM, 1) + spec(pl.ANY, 1) + spec(pltpu.SMEM, 1),
        scratch_shapes=[pltpu.SMEM(lookup.shape, jnp.int32)] * 2
        + like([prev, mem, left_t])
        + [scratch((2 * TILES, 128), F32), dma((5 + teams,))],
        compiler_params=params(PACK_MIB),
        cost_estimate=cost(0, 1 << 20),
        name="pack",
    )(lookup, tally, prev, mem, left_t)
    from_after = lax.ppermute(packed, "seq", [((i + 1) % rings, i) for i in range(rings)])
    from_before = lax.ppermute(packed, "seq", [(i, (i + 1) % rings) for i in range(rings)])
    left = lax.all_to_all(left, "tensor", 0, 0)

    gain = entry_standardize_scale.reshape(TILES, 128)
    vectors = [
        v.reshape(2, 128) for v in (feature_forget_logloglevel, present_token_boost, team_standardize_scale)
    ]
    xn, new_shifts, small = pl.pallas_call(
        norm_kernel,
        out_shape=[shape((ROWS, WIDTH), F32), shape((SLOTS, WIDTH), F32), shape((8, 128), F32)],
        in_specs=spec(pltpu.SMEM, 1) + spec(pl.ANY, 5),
        out_specs=spec(pltpu.VMEM, 3),
        scratch_shapes=like([x, gain] + vectors) + [scratch((ROWS * TILES, 128), F32), dma((5,))],
        compiler_params=params(MAIN_MIB),
        cost_estimate=cost(0, 4 << 20),
        name="norm",
    )(meta, x, gain, *vectors)

    operands = [
        xn, prev, from_after, from_before, blend_coefficients,
        acceptance_projection_matrix, lookup_projection_matrix, payload_projection_matrix,
        left, forget_map_right_matrix, small, final_projection_matrix,
    ]
    part, moved, values = pl.pallas_call(
        main_kernel,
        out_shape=[
            shape((ROWS * TILES, 128), BF16), shape((ROWS + SLOTS, LOCAL), F32), shape((ROWS, LOCAL), F32),
        ],
        in_specs=spec(pltpu.SMEM, 1) + spec(pl.ANY, 1 + len(operands)),
        out_specs=spec(pltpu.VMEM, 3),
        scratch_shapes=like(operands)
        + [scratch((SLOTS, WIDTH), F32), state_buf, read_buf, read_buf, scratch((ROWS * TILES, 128), F32)]
        + [scratch((LOCAL // 128, ROWS, 128), F32), dma((len(operands),)), dma],
        compiler_params=params(MAIN_MIB),
        cost_estimate=cost(8 * ROWS * WIDTH * LOCAL, 8 << 20),
        name="main",
    )(meta, mem, *operands)

    operands = [moved, values, from_after, from_before]
    new_states = pl.pallas_call(
        update_kernel,
        out_shape=shape((SLOTS * STATE_ROWS, 128), F32),
        in_specs=spec(pltpu.SMEM, 1) + spec(pl.ANY, 1 + len(operands)),
        out_specs=spec(pl.ANY, 1)[0],
        scratch_shapes=like(operands)
        + [state_buf, rows_buf, rows_buf, scratch((SLOTS * 16, 128), F32), state_buf]
        + [dma((len(operands),)), dma, dma((SLOTS,))],
        compiler_params=params(MAIN_MIB),
        cost_estimate=cost(1 << 24, 8 << 20),
        name="update",
    )(meta, mem, *operands)

    pairs = [[2 * i, 2 * i + 1] for i in range(teams // 2)]
    chips = [[2 * i + c for i in range(teams // 2)] for c in range(2)]
    half = ROWS * TILES // 2
    both = lax.all_gather(part, "tensor", axis_index_groups=pairs, tiled=False)
    mine = lax.dynamic_slice_in_dim(both, core * half, half, 1).astype(F32).sum(0).astype(BF16)
    spread = lax.all_to_all(
        jnp.broadcast_to(mine[None], (teams // 2,) + mine.shape), "tensor", 0, 0, axis_index_groups=chips
    )
    total = tiles_back(spread.astype(F32).sum(0).astype(BF16), SLOTS // 2, STEPS, WIDTH)
    proj = lax.all_gather(total, "tensor", axis_index_groups=pairs, tiled=True)
    valid = tally[:, None, None] > jnp.arange(STEPS, dtype=jnp.int32)[None, :, None]
    mixed = jnp.where(valid, layer_entry_vectors.astype(F32) + proj.astype(F32), 0.0).astype(BF16)
    return (
        mixed,
        tiles_back(new_states, SLOTS, HEADS, HEAD * HEAD),
        new_shifts,
    )


def solution(mesh):
    in_specs = (
        P("seq", None, None),
        P("seq"),
        P("seq"),
        P("seq", "tensor", None),
        P("seq", None),
        P(),
        P(),
        P(None, "tensor"),
        P(None, "tensor"),
        P(None, "tensor"),
        P("tensor", None),
        P(None, "tensor"),
        P("tensor"),
        P("tensor"),
        P("tensor"),
        P("tensor", None),
    )
    out_specs = (P("seq", None, None), P("seq", "tensor", None), P("seq", None))
    return jax.shard_map(shards, mesh=mesh, in_specs=in_specs, out_specs=out_specs, check_vma=False)
```

```python
import functools

import jax
import jax.numpy as jnp
from jax import lax
from jax.experimental import pallas as pl
from jax.experimental.pallas import tpu as pltpu
from jax.sharding import PartitionSpec as P

EPS = 1e-05
F32 = jnp.float32
BF16 = jnp.bfloat16
HEAD = 64
SLOTS = 16
STEPS = 4
WIDTH = 2048
HEADS = 4
LOCAL = HEADS * HEAD
TILES = WIDTH // 128
ROWS = SLOTS * STEPS
STATE_ROWS = HEADS * HEAD * HEAD // 128
PIECE = STATE_ROWS + TILES
PACK_ROWS = 2 * PIECE + 16
CAME, TALLY, META = SLOTS, SLOTS + 16, 64
READ_STRIDE = STEPS * 8 + 8
PACK_MIB, MAIN_MIB = 60, 52


def spec(space, count):
    return [pl.BlockSpec(memory_space=space)] * count


def dot(a, b):
    return jnp.dot(a, b, preferred_element_type=F32)


def dot_rows(a, b):
    return lax.dot_general(a, b, (((0,), (0,)), ((), ())), preferred_element_type=F32)


def split(a):
    hi = a.astype(BF16)
    return hi, (a - hi.astype(F32)).astype(BF16)


def dot_split(a, b):
    hi, lo = split(a)
    return dot(hi, b) + dot(lo, b)


def iota(shape, dim):
    return lax.broadcasted_iota(jnp.int32, shape, dim)


def column_of(meta_ref, shape):
    rows = iota(shape, 0)
    out = jnp.zeros(shape, jnp.int32)
    for q in range(SLOTS):
        out = jnp.where(rows == q, meta_ref[TALLY + q], out)
    return out


def row_of(ref):
    return jnp.concatenate([ref[i : i + 1, :] for i in range(ref.shape[0])], axis=1)


def start(items):
    for copy in items:
        copy.start()


def place():
    count = lax.axis_size("seq")
    me = lax.axis_index("seq")
    return me, jnp.where(me == 0, count - 1, me - 1)


def pack_kernel(
    lookup_hbm, tally_hbm, prev_hbm, mem_hbm, left_hbm, out_ref, left_out, meta_ref,
    lookup_ref, tally_ref, prev, mem, left, tile, sems,
):
    loads = copies(
        (lookup_hbm, prev_hbm, mem_hbm, left_hbm, tally_hbm), (lookup_ref, prev, mem, left, tally_ref), sems
    )
    start([loads[n] for n in (3, 0, 1, 2, 4)])
    me, behind = place()
    first = me * SLOTS
    loads[3].wait()
    sends = [pltpu.make_async_copy(left, left_out.at[n], sems.at[5 + n]) for n in range(left_out.shape[0])]
    start(sends)
    loads[0].wait()
    kept = jnp.int32(0)
    slots, wants = [jnp.int32(0)] * 2, [jnp.int32(0)] * 2
    for q in range(SLOTS):
        at = lookup_ref[q] - first
        own = (at >= 0) & (at < SLOTS)
        at = jnp.where(own, at, 0)
        kept = kept | jnp.where(own, jnp.int32(1) << at, 0)
        meta_ref[q] = at
        owner = lookup_ref[q] >> (SLOTS.bit_length() - 1)
        for n, mine in enumerate((jnp.logical_not(own) & (owner == behind), jnp.logical_not(own) & (owner != behind))):
            slots[n] = jnp.where(mine, q, slots[n])
            wants[n] = jnp.where(mine, lookup_ref[q] & (SLOTS - 1), wants[n])
    low, high = jnp.int32(0), jnp.int32(0)
    for s in range(SLOTS):
        high = jnp.where((kept >> s) & 1 == 0, s, high)
        low = jnp.where((kept >> (SLOTS - 1 - s)) & 1 == 0, SLOTS - 1 - s, low)
    for n, free in enumerate((low, high)):
        meta_ref[slots[n]] = free
        meta_ref[CAME + n] = slots[n]
        meta_ref[CAME + 2 + n] = wants[n]
        meta_ref[CAME + 4 + n] = free
    out_ref[2 * PIECE :, :] = jnp.full((16, 128), low, jnp.int32).astype(F32).astype(BF16)
    loads[1].wait()
    for n, slot in enumerate((low, high)):
        row = prev[pl.ds(slot, 1), :]
        for c in range(TILES):
            tile[n * TILES + c : n * TILES + c + 1, :] = row[:, c * 128 : (c + 1) * 128]
    loads[2].wait()
    for n, slot in enumerate((low, high)):
        begin = pl.multiple_of(slot * STATE_ROWS, STATE_ROWS)
        out_ref[n * PIECE : n * PIECE + STATE_ROWS, :] = mem[pl.ds(begin, STATE_ROWS), :].astype(BF16)
        out_ref[n * PIECE + STATE_ROWS : (n + 1) * PIECE, :] = tile[n * TILES : (n + 1) * TILES, :].astype(BF16)
    loads[4].wait()
    for q in range(SLOTS):
        meta_ref[TALLY + q] = tally_ref[q]
    for copy in sends:
        copy.wait()


def pick(recv_ref, wanted, begin, count):
    low = recv_ref[2 * PIECE :, :].astype(F32)[:1, :]
    is_low = low == wanted.astype(F32)
    rows = [recv_ref[at : at + count, :].astype(F32) for at in (begin, PIECE + begin)]
    return jnp.where(is_low, rows[0], rows[1])


def copies(sources_, targets, sems):
    return [pltpu.make_async_copy(a, b, sems.at[n]) for n, (a, b) in enumerate(zip(sources_, targets))]


def cut(a, t):
    return a[t * SLOTS : (t + 1) * SLOTS, :]


def reorder_matrix():
    row, col = iota((LOCAL, LOCAL), 0), iota((LOCAL, LOCAL), 1)
    source = (col % HEADS) * HEAD + ((col // HEADS) % (HEAD // 2)) * 2 + col // 128
    return (row == source).astype(BF16)


def place_received(meta_ref, received, state):
    for n, recv_ref in enumerate(received):
        begin = pl.multiple_of(meta_ref[CAME + 4 + n] * STATE_ROWS, STATE_ROWS)
        state[pl.ds(begin, STATE_ROWS), :] = pick(recv_ref, meta_ref[CAME + 2 + n], 0, STATE_ROWS)


def state_of(meta_ref, state, q):
    return state[pl.ds(pl.multiple_of(meta_ref[q] * STATE_ROWS, STATE_ROWS), STATE_ROWS), :]


def norm_kernel(meta_ref, x_hbm, gain_hbm, *refs):
    hbm, (xn_ref, last_ref, small_ref), (x_ref, gain_ref), bufs = refs[:3], refs[3:6], refs[6:8], refs[8:11]
    x32, sems = refs[11:]
    loads = copies((x_hbm, gain_hbm) + hbm, (x_ref, gain_ref) + bufs, sems)
    start(loads)
    loads[0].wait()
    loads[1].wait()
    x32[...] = x_ref[...].astype(F32)
    gain = row_of(gain_ref)
    normed = []
    for t in range(STEPS):
        row = jnp.concatenate([x32[pl.ds(c * STEPS + t, SLOTS, stride=STEPS * TILES), :] for c in range(TILES)], axis=1)
        center = row - jnp.mean(row, axis=-1, keepdims=True)
        spread = jnp.mean(center * center, axis=-1, keepdims=True)
        normed.append(center * lax.rsqrt(spread + EPS) * gain)
    tally = column_of(meta_ref, (SLOTS, 128))[:, :1]
    last = normed[0]
    for t in range(1, STEPS):
        last = jnp.where(tally == t + 1, normed[t], last)
    last_ref[...] = last
    for t in range(STEPS):
        xn_ref[t * SLOTS : (t + 1) * SLOTS, :] = normed[t]
    small_ref[6:8, :] = jnp.zeros((2, 128), F32)
    for n in range(3):
        loads[2 + n].wait()
        small_ref[2 * n : 2 * n + 2, :] = bufs[n][...]


def main_kernel(meta_ref, mem_hbm, *refs):
    count = 12
    hbm, (part_ref, moved_ref, vals_ref) = refs[:count], refs[count : count + 3]
    bufs = refs[count + 3 : 2 * count + 3]
    shift, state, reads, heads, part, ordered, sems, state_sem = refs[2 * count + 3 :]
    loads = copies(hbm, bufs, sems)
    start(loads[5:8] + loads[:5] + loads[8:-1])
    state_load = pltpu.make_async_copy(mem_hbm, state, state_sem)
    state_load.start()
    loads[-1].start()
    xn_ref, prev_ref, from_after, from_before, blend_ref = bufs[:5]
    left_ref, right_ref, small_ref, final_ref = bufs[8:]
    tally = column_of(meta_ref, (SLOTS, 128))[:, :1]
    for n in range(5):
        loads[n].wait()
    for q in range(SLOTS):
        shift[q : q + 1, :] = prev_ref[pl.ds(meta_ref[q], 1), :]
    slot = iota((SLOTS, 128), 0)
    moved_rows = [
        pick(recv_ref, meta_ref[CAME + 2 + n], STATE_ROWS, TILES) for n, recv_ref in enumerate((from_before, from_after))
    ]
    shift_in = []
    for c in range(TILES):
        col = shift[:, c * 128 : (c + 1) * 128]
        for n, rows in enumerate(moved_rows):
            col = jnp.where(slot == meta_ref[CAME + n], rows[c : c + 1, :], col)
        shift_in.append(col)
    xn = xn_ref[...]
    change = jnp.concatenate([jnp.concatenate(shift_in, axis=1), xn[: (STEPS - 1) * SLOTS, :]], axis=0) - xn

    def mix(which):
        return (xn + change * blend_ref[which : which + 1, :]).astype(BF16)

    mixed_rows = mix(3)
    for n in range(8, 11):
        loads[n].wait()
    pre = jnp.zeros((ROWS, left_ref.shape[1]), F32)
    chunk = left_ref.shape[2]
    for n in range(left_ref.shape[0]):
        pre = pre + lax.dot_general(
            mixed_rows[:, n * chunk : (n + 1) * chunk], left_ref[n], (((1,), (1,)), ((), ())), preferred_element_type=F32
        )
    lora = jnp.tanh(pre).astype(BF16)
    decay = jnp.exp(-jnp.exp(row_of(small_ref[0:2, :]) + dot(lora, right_ref[...])))
    row256, col256 = iota((LOCAL, LOCAL), 0), iota((LOCAL, LOCAL), 1)
    same_head = (row256 // HEAD == col256 // HEAD).astype(BF16)
    reorder = reorder_matrix()
    rkv = []
    for n in range(3):
        loads[5 + n].wait()
        rkv.append(dot(mix(n), bufs[5 + n][...]))
    r = [cut(rkv[0], t) for t in range(STEPS)]
    k = [cut(rkv[1], t) for t in range(STEPS)]
    v = [cut(rkv[2], t) for t in range(STEPS)]
    d = [jnp.where(tally > t, cut(decay, t), 1.0) for t in range(STEPS)]
    kept = [jnp.where(tally > t, k[t], 0.0) for t in range(STEPS)]
    boost = row_of(small_ref[2:4, :])

    run, reach = jnp.ones_like(r[0]), []
    for t in range(STEPS):
        reach.append(r[t] * run)
        run = run * d[t]
    tail, coefs = None, [None] * STEPS
    for t in reversed(range(STEPS)):
        coefs[t] = kept[t] if tail is None else kept[t] * tail
        tail = d[t] if tail is None else tail * d[t]
    pairs, terms = [], []
    for t in range(STEPS):
        pairs.append((t, t))
        terms.append(r[t] * boost * k[t])
        weight = r[t]
        for s in reversed(range(t)):
            pairs.append((t, s))
            terms.append(weight * kept[s])
            weight = weight * d[s]
    sums = dot_split(jnp.concatenate(terms, axis=0), same_head)
    within = [None] * STEPS
    for n, (t, s) in enumerate(pairs):
        term = cut(sums, n) * v[s]
        within[t] = term if within[t] is None else within[t] + term

    moved = dot(jnp.concatenate(reach, axis=0).astype(BF16), reorder)
    moved_ref[...] = jnp.concatenate(coefs + [run], axis=0)
    vals_ref[...] = rkv[2]

    lane = iota((SLOTS, 128), 1)
    for h in range(HEADS):
        head_lane = lane % HEADS == h
        for p in range(2):
            for t in range(STEPS):
                at = pl.ds(t * 8 + p * HEADS + h, SLOTS, stride=READ_STRIDE)
                reads[at, :] = jnp.where(head_lane, cut(moved, t)[:, p * 128 : (p + 1) * 128], 0.0)
    state_load.wait()
    place_received(meta_ref, (from_before, from_after), state)
    for q in range(SLOTS):
        rows = slice(q * READ_STRIDE, q * READ_STRIDE + STEPS * 8)
        now = state_of(meta_ref, state, q)
        heads[rows, :] = dot(reads[rows, :].astype(BF16), now.astype(BF16))

    outs = []
    left_half = lane < HEAD
    for t in range(STEPS):
        def read(p, h):
            return heads[pl.ds(t * 8 + p * HEADS + h, SLOTS, stride=READ_STRIDE), :]

        cols = []
        for h in range(0, HEADS, 2):
            a, b, c, e = read(0, h), read(1, h), read(0, h + 1), read(1, h + 1)
            cols.append(jnp.where(left_half, a, e) + pltpu.roll(jnp.where(left_half, c, b), HEAD, 1))
        outs.append(jnp.concatenate(cols, axis=1) + within[t])
    y = jnp.concatenate(outs, axis=0)
    center = y - dot_split(y, same_head) * (1.0 / HEAD)
    spread = dot_split(center * center, same_head) * (1.0 / HEAD)
    g = center * lax.rsqrt(spread + EPS) * row_of(small_ref[4:6, :])
    for t in range(STEPS):
        for c in range(LOCAL // 128):
            ordered[c, pl.ds(t, SLOTS, stride=STEPS), :] = cut(g, t)[:, c * 128 : (c + 1) * 128]
    g = jnp.concatenate([ordered[c] for c in range(LOCAL // 128)], axis=1).astype(BF16)
    loads[11].wait()
    proj = dot(g, final_ref[...])
    for q in range(SLOTS):
        rows = proj[q * STEPS : (q + 1) * STEPS, :]
        for c in range(0, TILES, 2):
            at = (q * TILES + c) * STEPS
            part[at : at + 2 * STEPS, :] = jnp.concatenate(
                [rows[:, c * 128 : (c + 1) * 128], rows[:, (c + 1) * 128 : (c + 2) * 128]], axis=0
            )
    part_ref[...] = part[...].astype(BF16)


def update_kernel(meta_ref, mem_hbm, *refs):
    count = 4
    hbm, new_hbm, bufs = refs[:count], refs[count], refs[count + 1 : 2 * count + 1]
    state, keys, vals, decays, fresh, sems, state_sem, new_sems = refs[2 * count + 1 :]
    loads = copies(hbm, bufs, sems)
    start(loads)
    state_load = pltpu.make_async_copy(mem_hbm, state, state_sem)
    state_load.start()
    moved_ref, vals_ref, from_after, from_before = bufs
    loads[0].wait()
    loads[1].wait()
    moved = dot_split(moved_ref[...], reorder_matrix())
    rowd, cold = iota((LOCAL, HEADS * 128), 0), iota((LOCAL, HEADS * 128), 1)
    double = (rowd == (cold // 128) * HEAD + cold % HEAD).astype(BF16)
    doubled = dot(vals_ref[...].astype(BF16), double)
    lane = iota((SLOTS, 128), 1)
    for h in range(HEADS):
        head_lane = lane % HEADS == h
        for p in range(2):
            half = lane // HEAD == p
            cols = slice(p * 128, (p + 1) * 128)
            for t in range(STEPS):
                at = pl.ds(t * 8 + p * HEADS + h, SLOTS, stride=STEPS * 8)
                keys[at, :] = jnp.where(head_lane, cut(moved, t)[:, cols], 0.0)
                vals[at, :] = jnp.where(half, cut(doubled, t)[:, h * 128 : (h + 1) * 128], 0.0)
            whole = jnp.where(head_lane, cut(moved, STEPS)[:, cols], 0.0)
            high = whole.astype(BF16).astype(F32)
            decays[pl.ds(p * HEADS + h, SLOTS, stride=16), :] = high
            decays[pl.ds(8 + p * HEADS + h, SLOTS, stride=16), :] = whole - high
    ones = ((iota((16, 128), 0) // HEADS) % 2 == iota((16, 128), 1) // HEAD).astype(BF16)
    for copy in loads[2:] + [state_load]:
        copy.wait()
    place_received(meta_ref, (from_before, from_after), state)
    news = []
    for q in range(SLOTS):
        here = slice(q * STATE_ROWS, (q + 1) * STATE_ROWS)
        rows = slice(q * STEPS * 8, (q + 1) * STEPS * 8)
        fade = dot_rows(decays[q * 16 : (q + 1) * 16, :].astype(BF16), ones)
        grown = dot_rows(keys[rows, :].astype(BF16), vals[rows, :].astype(BF16))
        fresh[here, :] = fade * state_of(meta_ref, state, q) + grown
        news.append(pltpu.make_async_copy(fresh.at[here, :], new_hbm.at[here, :], new_sems.at[q]))
        news[-1].start()
    for copy in news:
        copy.wait()


def cost(flops, bytes_accessed):
    return pl.CostEstimate(flops=flops, bytes_accessed=bytes_accessed, transcendentals=0)


def tiles_view(a):
    lead, mid, width = a.shape
    return a.reshape(lead, mid, width // 128, 128).transpose(0, 2, 1, 3).reshape(lead * width // 128 * mid, 128)


def tiles_back(a, lead, mid, width):
    return a.reshape(lead, width // 128, mid, 128).transpose(0, 2, 1, 3).reshape(lead, mid, width)


def shards(
    layer_entry_vectors,
    tally_of_tokens,
    prior_slot_lookup,
    memory_matrices,
    previous_standardized_entries,
    entry_standardize_scale,
    blend_coefficients,
    acceptance_projection_matrix,
    lookup_projection_matrix,
    payload_projection_matrix,
    forget_map_left_matrix,
    forget_map_right_matrix,
    feature_forget_logloglevel,
    present_token_boost,
    team_standardize_scale,
    final_projection_matrix,
):
    rings = lax.axis_size("seq")
    teams = lax.axis_size("tensor")
    core = lax.axis_index("tensor") % 2
    x = tiles_view(layer_entry_vectors)
    mem = tiles_view(memory_matrices)
    prev = previous_standardized_entries
    lookup, tally = prior_slot_lookup, tally_of_tokens
    left_t = forget_map_left_matrix.T
    shape, scratch, dma = jax.ShapeDtypeStruct, pltpu.VMEM, pltpu.SemaphoreType.DMA
    params = lambda mib: pltpu.CompilerParams(vmem_limit_bytes=mib << 20)
    like = lambda items: [scratch(a.shape, a.dtype) for a in items]
    state_buf = scratch((SLOTS * STATE_ROWS, 128), F32)
    rows_buf = scratch((SLOTS * STEPS * 8, 128), F32)
    read_buf = scratch((SLOTS * READ_STRIDE, 128), F32)

    packed, left, meta = pl.pallas_call(
        pack_kernel,
        out_shape=[
            shape((PACK_ROWS, 128), BF16), shape((teams,) + left_t.shape, BF16), shape((META,), jnp.int32),
        ],
        in_specs=spec(pl.ANY, 5),
        out_specs=spec(pltpu.VMEM, 1) + spec(pl.ANY, 1) + spec(pltpu.SMEM, 1),
        scratch_shapes=[pltpu.SMEM(lookup.shape, jnp.int32)] * 2
        + like([prev, mem, left_t])
        + [scratch((2 * TILES, 128), F32), dma((5 + teams,))],
        compiler_params=params(PACK_MIB),
        cost_estimate=cost(0, 1 << 20),
        name="pack",
    )(lookup, tally, prev, mem, left_t)
    from_after = lax.ppermute(packed, "seq", [((i + 1) % rings, i) for i in range(rings)])
    from_before = lax.ppermute(packed, "seq", [(i, (i + 1) % rings) for i in range(rings)])
    left = lax.all_to_all(left, "tensor", 0, 0)

    gain = entry_standardize_scale.reshape(TILES, 128)
    vectors = [
        v.reshape(2, 128) for v in (feature_forget_logloglevel, present_token_boost, team_standardize_scale)
    ]
    xn, new_shifts, small = pl.pallas_call(
        norm_kernel,
        out_shape=[shape((ROWS, WIDTH), F32), shape((SLOTS, WIDTH), F32), shape((8, 128), F32)],
        in_specs=spec(pltpu.SMEM, 1) + spec(pl.ANY, 5),
        out_specs=spec(pltpu.VMEM, 3),
        scratch_shapes=like([x, gain] + vectors) + [scratch((ROWS * TILES, 128), F32), dma((5,))],
        compiler_params=params(MAIN_MIB),
        cost_estimate=cost(0, 4 << 20),
        name="norm",
    )(meta, x, gain, *vectors)

    operands = [
        xn, prev, from_after, from_before, blend_coefficients,
        acceptance_projection_matrix, lookup_projection_matrix, payload_projection_matrix,
        left, forget_map_right_matrix, small, final_projection_matrix,
    ]
    part, moved, values = pl.pallas_call(
        main_kernel,
        out_shape=[
            shape((ROWS * TILES, 128), BF16), shape((ROWS + SLOTS, LOCAL), F32), shape((ROWS, LOCAL), F32),
        ],
        in_specs=spec(pltpu.SMEM, 1) + spec(pl.ANY, 1 + len(operands)),
        out_specs=spec(pltpu.VMEM, 3),
        scratch_shapes=like(operands)
        + [scratch((SLOTS, WIDTH), F32), state_buf, read_buf, read_buf, scratch((ROWS * TILES, 128), F32)]
        + [scratch((LOCAL // 128, ROWS, 128), F32), dma((len(operands),)), dma],
        compiler_params=params(MAIN_MIB),
        cost_estimate=cost(8 * ROWS * WIDTH * LOCAL, 8 << 20),
        name="main",
    )(meta, mem, *operands)

    operands = [moved, values, from_after, from_before]
    new_states = pl.pallas_call(
        update_kernel,
        out_shape=shape((SLOTS * STATE_ROWS, 128), F32),
        in_specs=spec(pltpu.SMEM, 1) + spec(pl.ANY, 1 + len(operands)),
        out_specs=spec(pl.ANY, 1)[0],
        scratch_shapes=like(operands)
        + [state_buf, rows_buf, rows_buf, scratch((SLOTS * 16, 128), F32), state_buf]
        + [dma((len(operands),)), dma, dma((SLOTS,))],
        compiler_params=params(MAIN_MIB),
        cost_estimate=cost(1 << 24, 8 << 20),
        name="update",
    )(meta, mem, *operands)

    pairs = [[2 * i, 2 * i + 1] for i in range(teams // 2)]
    chips = [[2 * i + c for i in range(teams // 2)] for c in range(2)]
    half = ROWS * TILES // 2
    both = lax.all_gather(part, "tensor", axis_index_groups=pairs, tiled=False)
    mine = lax.dynamic_slice_in_dim(both, core * half, half, 1).astype(F32).sum(0).astype(BF16)
    spread = lax.all_to_all(
        jnp.broadcast_to(mine[None], (teams // 2,) + mine.shape), "tensor", 0, 0, axis_index_groups=chips
    )
    total = tiles_back(spread.astype(F32).sum(0).astype(BF16), SLOTS // 2, STEPS, WIDTH)
    proj = lax.all_gather(total, "tensor", axis_index_groups=pairs, tiled=True)
    valid = tally[:, None, None] > jnp.arange(STEPS, dtype=jnp.int32)[None, :, None]
    mixed = jnp.where(valid, layer_entry_vectors.astype(F32) + proj.astype(F32), 0.0).astype(BF16)
    return (
        mixed,
        tiles_back(new_states, SLOTS, HEADS, HEAD * HEAD),
        new_shifts,
    )


def solution(mesh):
    in_specs = (
        P("seq", None, None),
        P("seq"),
        P("seq"),
        P("seq", "tensor", None),
        P("seq", None),
        P(),
        P(),
        P(None, "tensor"),
        P(None, "tensor"),
        P(None, "tensor"),
        P("tensor", None),
        P(None, "tensor"),
        P("tensor"),
        P("tensor"),
        P("tensor"),
        P("tensor", None),
    )
    out_specs = (P("seq", None, None), P("seq", "tensor", None), P("seq", None))
    return jax.shard_map(shards, mesh=mesh, in_specs=in_specs, out_specs=out_specs, check_vma=False)
```

```python
import functools

import jax
import jax.numpy as jnp
from jax import lax
from jax.experimental import pallas as pl
from jax.experimental.pallas import tpu as pltpu
from jax.sharding import PartitionSpec as P

EPS = 1e-05
F32 = jnp.float32
BF16 = jnp.bfloat16
HEAD = 64
SLOTS = 16
STEPS = 4
WIDTH = 2048
HEADS = 4
LOCAL = HEADS * HEAD
TILES = WIDTH // 128
ROWS = SLOTS * STEPS
STATE_ROWS = HEADS * HEAD * HEAD // 128
PIECE = STATE_ROWS + TILES
PACK_ROWS = 2 * PIECE + 16
CAME, TALLY, META = SLOTS, SLOTS + 16, 64
READ_STRIDE = STEPS * 8 + 8
PACK_MIB, MAIN_MIB = 60, 52


def spec(space, count):
    return [pl.BlockSpec(memory_space=space)] * count


def dot(a, b):
    return jnp.dot(a, b, preferred_element_type=F32)


def dot_rows(a, b):
    return lax.dot_general(a, b, (((0,), (0,)), ((), ())), preferred_element_type=F32)


def split(a):
    hi = a.astype(BF16)
    return hi, (a - hi.astype(F32)).astype(BF16)


def dot_split(a, b):
    hi, lo = split(a)
    return dot(hi, b) + dot(lo, b)


def iota(shape, dim):
    return lax.broadcasted_iota(jnp.int32, shape, dim)


def column_of(meta_ref, shape):
    rows = iota(shape, 0)
    out = jnp.zeros(shape, jnp.int32)
    for q in range(SLOTS):
        out = jnp.where(rows == q, meta_ref[TALLY + q], out)
    return out


def row_of(ref):
    return jnp.concatenate([ref[i : i + 1, :] for i in range(ref.shape[0])], axis=1)


def start(items):
    for copy in items:
        copy.start()


def place():
    count = lax.axis_size("seq")
    me = lax.axis_index("seq")
    return me, jnp.where(me == 0, count - 1, me - 1)


def pack_kernel(
    lookup_hbm, tally_hbm, prev_hbm, mem_hbm, left_hbm, out_ref, left_out, meta_ref,
    lookup_ref, tally_ref, prev, mem, left, tile, sems,
):
    loads = copies(
        (lookup_hbm, prev_hbm, mem_hbm, left_hbm, tally_hbm), (lookup_ref, prev, mem, left, tally_ref), sems
    )
    start([loads[n] for n in (3, 0, 1, 2, 4)])
    me, behind = place()
    first = me * SLOTS
    loads[3].wait()
    sends = [pltpu.make_async_copy(left, left_out.at[n], sems.at[5 + n]) for n in range(left_out.shape[0])]
    start(sends)
    loads[0].wait()
    kept = jnp.int32(0)
    slots, wants = [jnp.int32(0)] * 2, [jnp.int32(0)] * 2
    for q in range(SLOTS):
        at = lookup_ref[q] - first
        own = (at >= 0) & (at < SLOTS)
        at = jnp.where(own, at, 0)
        kept = kept | jnp.where(own, jnp.int32(1) << at, 0)
        meta_ref[q] = at
        owner = lookup_ref[q] >> (SLOTS.bit_length() - 1)
        for n, mine in enumerate((jnp.logical_not(own) & (owner == behind), jnp.logical_not(own) & (owner != behind))):
            slots[n] = jnp.where(mine, q, slots[n])
            wants[n] = jnp.where(mine, lookup_ref[q] & (SLOTS - 1), wants[n])
    low, high = jnp.int32(0), jnp.int32(0)
    for s in range(SLOTS):
        high = jnp.where((kept >> s) & 1 == 0, s, high)
        low = jnp.where((kept >> (SLOTS - 1 - s)) & 1 == 0, SLOTS - 1 - s, low)
    for n, free in enumerate((low, high)):
        meta_ref[slots[n]] = free
        meta_ref[CAME + n] = slots[n]
        meta_ref[CAME + 2 + n] = wants[n]
        meta_ref[CAME + 4 + n] = free
    out_ref[2 * PIECE :, :] = jnp.full((16, 128), low, jnp.int32).astype(F32).astype(BF16)
    loads[1].wait()
    for n, slot in enumerate((low, high)):
        row = prev[pl.ds(slot, 1), :]
        for c in range(TILES):
            tile[n * TILES + c : n * TILES + c + 1, :] = row[:, c * 128 : (c + 1) * 128]
    loads[2].wait()
    for n, slot in enumerate((low, high)):
        begin = pl.multiple_of(slot * STATE_ROWS, STATE_ROWS)
        out_ref[n * PIECE : n * PIECE + STATE_ROWS, :] = mem[pl.ds(begin, STATE_ROWS), :].astype(BF16)
        out_ref[n * PIECE + STATE_ROWS : (n + 1) * PIECE, :] = tile[n * TILES : (n + 1) * TILES, :].astype(BF16)
    loads[4].wait()
    for q in range(SLOTS):
        meta_ref[TALLY + q] = tally_ref[q]
    for copy in sends:
        copy.wait()


def pick(recv_ref, wanted, begin, count):
    low = recv_ref[2 * PIECE :, :].astype(F32)[:1, :]
    is_low = low == wanted.astype(F32)
    rows = [recv_ref[at : at + count, :].astype(F32) for at in (begin, PIECE + begin)]
    return jnp.where(is_low, rows[0], rows[1])


def copies(sources_, targets, sems):
    return [pltpu.make_async_copy(a, b, sems.at[n]) for n, (a, b) in enumerate(zip(sources_, targets))]


def cut(a, t):
    return a[t * SLOTS : (t + 1) * SLOTS, :]


def reorder_matrix():
    row, col = iota((LOCAL, LOCAL), 0), iota((LOCAL, LOCAL), 1)
    source = (col % HEADS) * HEAD + ((col // HEADS) % (HEAD // 2)) * 2 + col // 128
    return (row == source).astype(BF16)


def place_received(meta_ref, received, state):
    for n, recv_ref in enumerate(received):
        begin = pl.multiple_of(meta_ref[CAME + 4 + n] * STATE_ROWS, STATE_ROWS)
        state[pl.ds(begin, STATE_ROWS), :] = pick(recv_ref, meta_ref[CAME + 2 + n], 0, STATE_ROWS)


def state_of(meta_ref, state, q):
    return state[pl.ds(pl.multiple_of(meta_ref[q] * STATE_ROWS, STATE_ROWS), STATE_ROWS), :]


def norm_kernel(meta_ref, x_hbm, gain_hbm, *refs):
    hbm, (xn_ref, last_ref, small_ref), (x_ref, gain_ref), bufs = refs[:3], refs[3:6], refs[6:8], refs[8:11]
    x32, sems = refs[11:]
    loads = copies((x_hbm, gain_hbm) + hbm, (x_ref, gain_ref) + bufs, sems)
    start(loads)
    loads[0].wait()
    loads[1].wait()
    x32[...] = x_ref[...].astype(F32)
    gain = row_of(gain_ref)
    normed = []
    for t in range(STEPS):
        row = jnp.concatenate([x32[pl.ds(c * STEPS + t, SLOTS, stride=STEPS * TILES), :] for c in range(TILES)], axis=1)
        center = row - jnp.mean(row, axis=-1, keepdims=True)
        spread = jnp.mean(center * center, axis=-1, keepdims=True)
        normed.append(center * lax.rsqrt(spread + EPS) * gain)
    tally = column_of(meta_ref, (SLOTS, 128))[:, :1]
    last = normed[0]
    for t in range(1, STEPS):
        last = jnp.where(tally == t + 1, normed[t], last)
    last_ref[...] = last
    for t in range(STEPS):
        xn_ref[t * SLOTS : (t + 1) * SLOTS, :] = normed[t]
    small_ref[6:8, :] = jnp.zeros((2, 128), F32)
    for n in range(3):
        loads[2 + n].wait()
        small_ref[2 * n : 2 * n + 2, :] = bufs[n][...]


def main_kernel(meta_ref, mem_hbm, *refs):
    count = 12
    hbm, (part_ref, moved_ref, vals_ref) = refs[:count], refs[count : count + 3]
    bufs = refs[count + 3 : 2 * count + 3]
    shift, state, reads, heads, part, ordered, sems, state_sem = refs[2 * count + 3 :]
    loads = copies(hbm, bufs, sems)
    start(loads[5:8] + loads[:5] + loads[8:-1])
    state_load = pltpu.make_async_copy(mem_hbm, state, state_sem)
    state_load.start()
    loads[-1].start()
    xn_ref, prev_ref, from_after, from_before, blend_ref = bufs[:5]
    left_ref, right_ref, small_ref, final_ref = bufs[8:]
    tally = column_of(meta_ref, (SLOTS, 128))[:, :1]
    for n in range(5):
        loads[n].wait()
    for q in range(SLOTS):
        shift[q : q + 1, :] = prev_ref[pl.ds(meta_ref[q], 1), :]
    slot = iota((SLOTS, 128), 0)
    moved_rows = [
        pick(recv_ref, meta_ref[CAME + 2 + n], STATE_ROWS, TILES) for n, recv_ref in enumerate((from_before, from_after))
    ]
    shift_in = []
    for c in range(TILES):
        col = shift[:, c * 128 : (c + 1) * 128]
        for n, rows in enumerate(moved_rows):
            col = jnp.where(slot == meta_ref[CAME + n], rows[c : c + 1, :], col)
        shift_in.append(col)
    xn = xn_ref[...]
    change = jnp.concatenate([jnp.concatenate(shift_in, axis=1), xn[: (STEPS - 1) * SLOTS, :]], axis=0) - xn

    def mix(which):
        return (xn + change * blend_ref[which : which + 1, :]).astype(BF16)

    mixed_rows = mix(3)
    for n in range(8, 11):
        loads[n].wait()
    pre = jnp.zeros((ROWS, left_ref.shape[1]), F32)
    chunk = left_ref.shape[2]
    for n in range(left_ref.shape[0]):
        pre = pre + lax.dot_general(
            mixed_rows[:, n * chunk : (n + 1) * chunk], left_ref[n], (((1,), (1,)), ((), ())), preferred_element_type=F32
        )
    lora = jnp.tanh(pre).astype(BF16)
    decay = jnp.exp(-jnp.exp(row_of(small_ref[0:2, :]) + dot(lora, right_ref[...])))
    row256, col256 = iota((LOCAL, LOCAL), 0), iota((LOCAL, LOCAL), 1)
    same_head = (row256 // HEAD == col256 // HEAD).astype(BF16)
    reorder = reorder_matrix()
    rkv = []
    for n in range(3):
        loads[5 + n].wait()
        rkv.append(dot(mix(n), bufs[5 + n][...]))
    r = [cut(rkv[0], t) for t in range(STEPS)]
    k = [cut(rkv[1], t) for t in range(STEPS)]
    v = [cut(rkv[2], t) for t in range(STEPS)]
    d = [jnp.where(tally > t, cut(decay, t), 1.0) for t in range(STEPS)]
    kept = [jnp.where(tally > t, k[t], 0.0) for t in range(STEPS)]
    boost = row_of(small_ref[2:4, :])

    run, reach = jnp.ones_like(r[0]), []
    for t in range(STEPS):
        reach.append(r[t] * run)
        run = run * d[t]
    tail, coefs = None, [None] * STEPS
    for t in reversed(range(STEPS)):
        coefs[t] = kept[t] if tail is None else kept[t] * tail
        tail = d[t] if tail is None else tail * d[t]
    pairs, terms = [], []
    for t in range(STEPS):
        pairs.append((t, t))
        terms.append(r[t] * boost * k[t])
        weight = r[t]
        for s in reversed(range(t)):
            pairs.append((t, s))
            terms.append(weight * kept[s])
            weight = weight * d[s]
    sums = dot_split(jnp.concatenate(terms, axis=0), same_head)
    within = [None] * STEPS
    for n, (t, s) in enumerate(pairs):
        term = cut(sums, n) * v[s]
        within[t] = term if within[t] is None else within[t] + term

    moved = dot(jnp.concatenate(reach, axis=0).astype(BF16), reorder)
    moved_ref[...] = jnp.concatenate(coefs + [run], axis=0)
    vals_ref[...] = rkv[2]

    lane = iota((SLOTS, 128), 1)
    for h in range(HEADS):
        head_lane = lane % HEADS == h
        for p in range(2):
            for t in range(STEPS):
                at = pl.ds(t * 8 + p * HEADS + h, SLOTS, stride=READ_STRIDE)
                reads[at, :] = jnp.where(head_lane, cut(moved, t)[:, p * 128 : (p + 1) * 128], 0.0)
    state_load.wait()
    place_received(meta_ref, (from_before, from_after), state)
    for q in range(SLOTS):
        rows = slice(q * READ_STRIDE, q * READ_STRIDE + STEPS * 8)
        now = state_of(meta_ref, state, q)
        heads[rows, :] = dot(reads[rows, :].astype(BF16), now.astype(BF16))

    outs = []
    left_half = lane < HEAD
    for t in range(STEPS):
        def read(p, h):
            return heads[pl.ds(t * 8 + p * HEADS + h, SLOTS, stride=READ_STRIDE), :]

        cols = []
        for h in range(0, HEADS, 2):
            a, b, c, e = read(0, h), read(1, h), read(0, h + 1), read(1, h + 1)
            cols.append(jnp.where(left_half, a, e) + pltpu.roll(jnp.where(left_half, c, b), HEAD, 1))
        outs.append(jnp.concatenate(cols, axis=1) + within[t])
    y = jnp.concatenate(outs, axis=0)
    center = y - dot_split(y, same_head) * (1.0 / HEAD)
    spread = dot_split(center * center, same_head) * (1.0 / HEAD)
    g = center * lax.rsqrt(spread + EPS) * row_of(small_ref[4:6, :])
    for t in range(STEPS):
        for c in range(LOCAL // 128):
            ordered[c, pl.ds(t, SLOTS, stride=STEPS), :] = cut(g, t)[:, c * 128 : (c + 1) * 128]
    g = jnp.concatenate([ordered[c] for c in range(LOCAL // 128)], axis=1).astype(BF16)
    loads[11].wait()
    proj = dot(g, final_ref[...])
    for q in range(SLOTS):
        rows = proj[q * STEPS : (q + 1) * STEPS, :]
        for c in range(0, TILES, 2):
            at = (q * TILES + c) * STEPS
            part[at : at + 2 * STEPS, :] = jnp.concatenate(
                [rows[:, c * 128 : (c + 1) * 128], rows[:, (c + 1) * 128 : (c + 2) * 128]], axis=0
            )
    part_ref[...] = part[...].astype(BF16)


def update_kernel(meta_ref, mem_hbm, *refs):
    count = 4
    hbm, new_hbm, bufs = refs[:count], refs[count], refs[count + 1 : 2 * count + 1]
    state, keys, vals, decays, fresh, sems, state_sem, new_sems = refs[2 * count + 1 :]
    loads = copies(hbm, bufs, sems)
    start(loads)
    state_load = pltpu.make_async_copy(mem_hbm, state, state_sem)
    state_load.start()
    moved_ref, vals_ref, from_after, from_before = bufs
    loads[0].wait()
    loads[1].wait()
    moved = dot_split(moved_ref[...], reorder_matrix())
    rowd, cold = iota((LOCAL, HEADS * 128), 0), iota((LOCAL, HEADS * 128), 1)
    double = (rowd == (cold // 128) * HEAD + cold % HEAD).astype(BF16)
    doubled = dot(vals_ref[...].astype(BF16), double)
    lane = iota((SLOTS, 128), 1)
    for h in range(HEADS):
        head_lane = lane % HEADS == h
        for p in range(2):
            half = lane // HEAD == p
            cols = slice(p * 128, (p + 1) * 128)
            for t in range(STEPS):
                at = pl.ds(t * 8 + p * HEADS + h, SLOTS, stride=STEPS * 8)
                keys[at, :] = jnp.where(head_lane, cut(moved, t)[:, cols], 0.0)
                vals[at, :] = jnp.where(half, cut(doubled, t)[:, h * 128 : (h + 1) * 128], 0.0)
            whole = jnp.where(head_lane, cut(moved, STEPS)[:, cols], 0.0)
            high = whole.astype(BF16).astype(F32)
            decays[pl.ds(p * HEADS + h, SLOTS, stride=16), :] = high
            decays[pl.ds(8 + p * HEADS + h, SLOTS, stride=16), :] = whole - high
    ones = ((iota((16, 128), 0) // HEADS) % 2 == iota((16, 128), 1) // HEAD).astype(BF16)
    for copy in loads[2:] + [state_load]:
        copy.wait()
    place_received(meta_ref, (from_before, from_after), state)
    news = []
    for q in range(SLOTS):
        here = slice(q * STATE_ROWS, (q + 1) * STATE_ROWS)
        rows = slice(q * STEPS * 8, (q + 1) * STEPS * 8)
        fade = dot_rows(decays[q * 16 : (q + 1) * 16, :].astype(BF16), ones)
        grown = dot_rows(keys[rows, :].astype(BF16), vals[rows, :].astype(BF16))
        fresh[here, :] = fade * state_of(meta_ref, state, q) + grown
        news.append(pltpu.make_async_copy(fresh.at[here, :], new_hbm.at[here, :], new_sems.at[q]))
        news[-1].start()
    for copy in news:
        copy.wait()


def cost(flops, bytes_accessed):
    return pl.CostEstimate(flops=flops, bytes_accessed=bytes_accessed, transcendentals=0)


def tiles_view(a):
    lead, mid, width = a.shape
    return a.reshape(lead, mid, width // 128, 128).transpose(0, 2, 1, 3).reshape(lead * width // 128 * mid, 128)


def tiles_back(a, lead, mid, width):
    return a.reshape(lead, width // 128, mid, 128).transpose(0, 2, 1, 3).reshape(lead, mid, width)


def shards(
    layer_entry_vectors,
    tally_of_tokens,
    prior_slot_lookup,
    memory_matrices,
    previous_standardized_entries,
    entry_standardize_scale,
    blend_coefficients,
    acceptance_projection_matrix,
    lookup_projection_matrix,
    payload_projection_matrix,
    forget_map_left_matrix,
    forget_map_right_matrix,
    feature_forget_logloglevel,
    present_token_boost,
    team_standardize_scale,
    final_projection_matrix,
):
    rings = lax.axis_size("seq")
    teams = lax.axis_size("tensor")
    core = lax.axis_index("tensor") % 2
    x = tiles_view(layer_entry_vectors)
    mem = tiles_view(memory_matrices)
    prev = previous_standardized_entries
    lookup, tally = prior_slot_lookup, tally_of_tokens
    left_t = forget_map_left_matrix.T
    shape, scratch, dma = jax.ShapeDtypeStruct, pltpu.VMEM, pltpu.SemaphoreType.DMA
    params = lambda mib: pltpu.CompilerParams(vmem_limit_bytes=mib << 20)
    like = lambda items: [scratch(a.shape, a.dtype) for a in items]
    state_buf = scratch((SLOTS * STATE_ROWS, 128), F32)
    rows_buf = scratch((SLOTS * STEPS * 8, 128), F32)
    read_buf = scratch((SLOTS * READ_STRIDE, 128), F32)

    packed, left, meta = pl.pallas_call(
        pack_kernel,
        out_shape=[
            shape((PACK_ROWS, 128), BF16), shape((teams,) + left_t.shape, BF16), shape((META,), jnp.int32),
        ],
        in_specs=spec(pl.ANY, 5),
        out_specs=spec(pltpu.VMEM, 1) + spec(pl.ANY, 1) + spec(pltpu.SMEM, 1),
        scratch_shapes=[pltpu.SMEM(lookup.shape, jnp.int32)] * 2
        + like([prev, mem, left_t])
        + [scratch((2 * TILES, 128), F32), dma((5 + teams,))],
        compiler_params=params(PACK_MIB),
        cost_estimate=cost(0, 1 << 20),
        name="pack",
    )(lookup, tally, prev, mem, left_t)
    from_after = lax.ppermute(packed, "seq", [((i + 1) % rings, i) for i in range(rings)])
    from_before = lax.ppermute(packed, "seq", [(i, (i + 1) % rings) for i in range(rings)])
    left = lax.all_to_all(left, "tensor", 0, 0)

    gain = entry_standardize_scale.reshape(TILES, 128)
    vectors = [
        v.reshape(2, 128) for v in (feature_forget_logloglevel, present_token_boost, team_standardize_scale)
    ]
    xn, new_shifts, small = pl.pallas_call(
        norm_kernel,
        out_shape=[shape((ROWS, WIDTH), F32), shape((SLOTS, WIDTH), F32), shape((8, 128), F32)],
        in_specs=spec(pltpu.SMEM, 1) + spec(pl.ANY, 5),
        out_specs=spec(pltpu.VMEM, 3),
        scratch_shapes=like([x, gain] + vectors) + [scratch((ROWS * TILES, 128), F32), dma((5,))],
        compiler_params=params(MAIN_MIB),
        cost_estimate=cost(0, 4 << 20),
        name="norm",
    )(meta, x, gain, *vectors)

    operands = [
        xn, prev, from_after, from_before, blend_coefficients,
        acceptance_projection_matrix, lookup_projection_matrix, payload_projection_matrix,
        left, forget_map_right_matrix, small, final_projection_matrix,
    ]
    part, moved, values = pl.pallas_call(
        main_kernel,
        out_shape=[
            shape((ROWS * TILES, 128), BF16), shape((ROWS + SLOTS, LOCAL), F32), shape((ROWS, LOCAL), F32),
        ],
        in_specs=spec(pltpu.SMEM, 1) + spec(pl.ANY, 1 + len(operands)),
        out_specs=spec(pltpu.VMEM, 3),
        scratch_shapes=like(operands)
        + [scratch((SLOTS, WIDTH), F32), state_buf, read_buf, read_buf, scratch((ROWS * TILES, 128), F32)]
        + [scratch((LOCAL // 128, ROWS, 128), F32), dma((len(operands),)), dma],
        compiler_params=params(MAIN_MIB),
        cost_estimate=cost(8 * ROWS * WIDTH * LOCAL, 8 << 20),
        name="main",
    )(meta, mem, *operands)

    operands = [moved, values, from_after, from_before]
    new_states = pl.pallas_call(
        update_kernel,
        out_shape=shape((SLOTS * STATE_ROWS, 128), F32),
        in_specs=spec(pltpu.SMEM, 1) + spec(pl.ANY, 1 + len(operands)),
        out_specs=spec(pl.ANY, 1)[0],
        scratch_shapes=like(operands)
        + [state_buf, rows_buf, rows_buf, scratch((SLOTS * 16, 128), F32), state_buf]
        + [dma((len(operands),)), dma, dma((SLOTS,))],
        compiler_params=params(MAIN_MIB),
        cost_estimate=cost(1 << 24, 8 << 20),
        name="update",
    )(meta, mem, *operands)

    pairs = [[2 * i, 2 * i + 1] for i in range(teams // 2)]
    chips = [[2 * i + c for i in range(teams // 2)] for c in range(2)]
    half = ROWS * TILES // 2
    both = lax.all_gather(part, "tensor", axis_index_groups=pairs, tiled=False)
    mine = lax.dynamic_slice_in_dim(both, core * half, half, 1).astype(F32).sum(0).astype(BF16)
    spread = lax.all_to_all(
        jnp.broadcast_to(mine[None], (teams // 2,) + mine.shape), "tensor", 0, 0, axis_index_groups=chips
    )
    mine_rows = SLOTS // 2
    residual = lax.dynamic_slice_in_dim(layer_entry_vectors, core * mine_rows, mine_rows, 0).astype(F32)
    counts = lax.dynamic_slice_in_dim(tally, core * mine_rows, mine_rows, 0)
    valid = counts[:, None, None] > jnp.arange(STEPS, dtype=jnp.int32)[None, :, None]
    total = residual + tiles_back(spread.astype(F32).sum(0), mine_rows, STEPS, WIDTH)
    mixed = jnp.where(valid, total, 0.0).astype(BF16)
    mixed = lax.all_gather(mixed, "tensor", axis_index_groups=pairs, tiled=True)
    return (
        mixed,
        tiles_back(new_states, SLOTS, HEADS, HEAD * HEAD),
        new_shifts,
    )


def solution(mesh):
    in_specs = (
        P("seq", None, None),
        P("seq"),
        P("seq"),
        P("seq", "tensor", None),
        P("seq", None),
        P(),
        P(),
        P(None, "tensor"),
        P(None, "tensor"),
        P(None, "tensor"),
        P("tensor", None),
        P(None, "tensor"),
        P("tensor"),
        P("tensor"),
        P("tensor"),
        P("tensor", None),
    )
    out_specs = (P("seq", None, None), P("seq", "tensor", None), P("seq", None))
    return jax.shard_map(shards, mesh=mesh, in_specs=in_specs, out_specs=out_specs, check_vma=False)
```

```python
import functools

import jax
import jax.numpy as jnp
from jax import lax
from jax.experimental import pallas as pl
from jax.experimental.pallas import tpu as pltpu
from jax.sharding import PartitionSpec as P

EPS = 1e-05
F32 = jnp.float32
BF16 = jnp.bfloat16
HEAD = 64
SLOTS = 16
STEPS = 4
WIDTH = 2048
HEADS = 4
LOCAL = HEADS * HEAD
TILES = WIDTH // 128
ROWS = SLOTS * STEPS
STATE_ROWS = HEADS * HEAD * HEAD // 128
PIECE = STATE_ROWS + TILES
PACK_ROWS = 2 * PIECE + 16
CAME, TALLY, META = SLOTS, SLOTS + 16, 64
READ_STRIDE = STEPS * 8 + 8
PACK_MIB, MAIN_MIB = 60, 52


def spec(space, count):
    return [pl.BlockSpec(memory_space=space)] * count


def dot(a, b):
    return jnp.dot(a, b, preferred_element_type=F32)


def dot_rows(a, b):
    return lax.dot_general(a, b, (((0,), (0,)), ((), ())), preferred_element_type=F32)


def split(a):
    hi = a.astype(BF16)
    return hi, (a - hi.astype(F32)).astype(BF16)


def dot_split(a, b):
    hi, lo = split(a)
    return dot(hi, b) + dot(lo, b)


def iota(shape, dim):
    return lax.broadcasted_iota(jnp.int32, shape, dim)


def column_of(meta_ref, shape):
    rows = iota(shape, 0)
    out = jnp.zeros(shape, jnp.int32)
    for q in range(SLOTS):
        out = jnp.where(rows == q, meta_ref[TALLY + q], out)
    return out


def row_of(ref):
    return jnp.concatenate([ref[i : i + 1, :] for i in range(ref.shape[0])], axis=1)


def start(items):
    for copy in items:
        copy.start()


def place():
    count = lax.axis_size("seq")
    me = lax.axis_index("seq")
    return me, jnp.where(me == 0, count - 1, me - 1)


def pack_kernel(
    lookup_hbm, tally_hbm, prev_hbm, mem_hbm, left_hbm, out_ref, left_out, meta_ref,
    lookup_ref, tally_ref, prev, mem, left, tile, sems,
):
    loads = copies(
        (lookup_hbm, prev_hbm, mem_hbm, left_hbm, tally_hbm), (lookup_ref, prev, mem, left, tally_ref), sems
    )
    start([loads[n] for n in (3, 0, 2, 1, 4)])
    me, behind = place()
    first = me * SLOTS
    loads[3].wait()
    sends = [pltpu.make_async_copy(left, left_out.at[n], sems.at[5 + n]) for n in range(left_out.shape[0])]
    start(sends)
    loads[0].wait()
    kept = jnp.int32(0)
    slots, wants = [jnp.int32(0)] * 2, [jnp.int32(0)] * 2
    for q in range(SLOTS):
        at = lookup_ref[q] - first
        own = (at >= 0) & (at < SLOTS)
        at = jnp.where(own, at, 0)
        kept = kept | jnp.where(own, jnp.int32(1) << at, 0)
        meta_ref[q] = at
        owner = lookup_ref[q] >> (SLOTS.bit_length() - 1)
        for n, mine in enumerate((jnp.logical_not(own) & (owner == behind), jnp.logical_not(own) & (owner != behind))):
            slots[n] = jnp.where(mine, q, slots[n])
            wants[n] = jnp.where(mine, lookup_ref[q] & (SLOTS - 1), wants[n])
    low, high = jnp.int32(0), jnp.int32(0)
    for s in range(SLOTS):
        high = jnp.where((kept >> s) & 1 == 0, s, high)
        low = jnp.where((kept >> (SLOTS - 1 - s)) & 1 == 0, SLOTS - 1 - s, low)
    for n, free in enumerate((low, high)):
        meta_ref[slots[n]] = free
        meta_ref[CAME + n] = slots[n]
        meta_ref[CAME + 2 + n] = wants[n]
        meta_ref[CAME + 4 + n] = free
    out_ref[2 * PIECE :, :] = jnp.full((16, 128), low, jnp.int32).astype(F32).astype(BF16)
    loads[1].wait()
    for n, slot in enumerate((low, high)):
        row = prev[pl.ds(slot, 1), :]
        for c in range(TILES):
            tile[n * TILES + c : n * TILES + c + 1, :] = row[:, c * 128 : (c + 1) * 128]
    loads[2].wait()
    for n, slot in enumerate((low, high)):
        begin = pl.multiple_of(slot * STATE_ROWS, STATE_ROWS)
        out_ref[n * PIECE : n * PIECE + STATE_ROWS, :] = mem[pl.ds(begin, STATE_ROWS), :].astype(BF16)
        out_ref[n * PIECE + STATE_ROWS : (n + 1) * PIECE, :] = tile[n * TILES : (n + 1) * TILES, :].astype(BF16)
    loads[4].wait()
    for q in range(SLOTS):
        meta_ref[TALLY + q] = tally_ref[q]
    for copy in sends:
        copy.wait()


def pick(recv_ref, wanted, begin, count):
    low = recv_ref[2 * PIECE :, :].astype(F32)[:1, :]
    is_low = low == wanted.astype(F32)
    rows = [recv_ref[at : at + count, :].astype(F32) for at in (begin, PIECE + begin)]
    return jnp.where(is_low, rows[0], rows[1])


def copies(sources_, targets, sems):
    return [pltpu.make_async_copy(a, b, sems.at[n]) for n, (a, b) in enumerate(zip(sources_, targets))]


def cut(a, t):
    return a[t * SLOTS : (t + 1) * SLOTS, :]


def reorder_matrix():
    row, col = iota((LOCAL, LOCAL), 0), iota((LOCAL, LOCAL), 1)
    source = (col % HEADS) * HEAD + ((col // HEADS) % (HEAD // 2)) * 2 + col // 128
    return (row == source).astype(BF16)


def place_received(meta_ref, received, state):
    for n, recv_ref in enumerate(received):
        begin = pl.multiple_of(meta_ref[CAME + 4 + n] * STATE_ROWS, STATE_ROWS)
        state[pl.ds(begin, STATE_ROWS), :] = pick(recv_ref, meta_ref[CAME + 2 + n], 0, STATE_ROWS)


def state_of(meta_ref, state, q):
    return state[pl.ds(pl.multiple_of(meta_ref[q] * STATE_ROWS, STATE_ROWS), STATE_ROWS), :]


def norm_kernel(meta_ref, x_hbm, gain_hbm, *refs):
    hbm, (xn_ref, last_ref, small_ref), (x_ref, gain_ref), bufs = refs[:3], refs[3:6], refs[6:8], refs[8:11]
    x32, sems = refs[11:]
    loads = copies((x_hbm, gain_hbm) + hbm, (x_ref, gain_ref) + bufs, sems)
    start(loads)
    loads[0].wait()
    loads[1].wait()
    x32[...] = x_ref[...].astype(F32)
    gain = row_of(gain_ref)
    normed = []
    for t in range(STEPS):
        row = jnp.concatenate([x32[pl.ds(c * STEPS + t, SLOTS, stride=STEPS * TILES), :] for c in range(TILES)], axis=1)
        center = row - jnp.mean(row, axis=-1, keepdims=True)
        spread = jnp.mean(center * center, axis=-1, keepdims=True)
        normed.append(center * lax.rsqrt(spread + EPS) * gain)
    tally = column_of(meta_ref, (SLOTS, 128))[:, :1]
    last = normed[0]
    for t in range(1, STEPS):
        last = jnp.where(tally == t + 1, normed[t], last)
    last_ref[...] = last
    for t in range(STEPS):
        xn_ref[t * SLOTS : (t + 1) * SLOTS, :] = normed[t]
    small_ref[6:8, :] = jnp.zeros((2, 128), F32)
    for n in range(3):
        loads[2 + n].wait()
        small_ref[2 * n : 2 * n + 2, :] = bufs[n][...]


def main_kernel(meta_ref, mem_hbm, *refs):
    count = 12
    hbm, (part_ref, moved_ref, vals_ref) = refs[:count], refs[count : count + 3]
    bufs = refs[count + 3 : 2 * count + 3]
    shift, state, reads, heads, part, ordered, sems, state_sem = refs[2 * count + 3 :]
    loads = copies(hbm, bufs, sems)
    start(loads[5:8] + loads[:5] + loads[8:-1])
    state_load = pltpu.make_async_copy(mem_hbm, state, state_sem)
    state_load.start()
    loads[-1].start()
    xn_ref, prev_ref, from_after, from_before, blend_ref = bufs[:5]
    left_ref, right_ref, small_ref, final_ref = bufs[8:]
    tally = column_of(meta_ref, (SLOTS, 128))[:, :1]
    for n in range(5):
        loads[n].wait()
    for q in range(SLOTS):
        shift[q : q + 1, :] = prev_ref[pl.ds(meta_ref[q], 1), :]
    slot = iota((SLOTS, 128), 0)
    moved_rows = [
        pick(recv_ref, meta_ref[CAME + 2 + n], STATE_ROWS, TILES) for n, recv_ref in enumerate((from_before, from_after))
    ]
    shift_in = []
    for c in range(TILES):
        col = shift[:, c * 128 : (c + 1) * 128]
        for n, rows in enumerate(moved_rows):
            col = jnp.where(slot == meta_ref[CAME + n], rows[c : c + 1, :], col)
        shift_in.append(col)
    xn = xn_ref[...]
    change = jnp.concatenate([jnp.concatenate(shift_in, axis=1), xn[: (STEPS - 1) * SLOTS, :]], axis=0) - xn

    def mix(which):
        return (xn + change * blend_ref[which : which + 1, :]).astype(BF16)

    mixed_rows = mix(3)
    for n in range(8, 11):
        loads[n].wait()
    pre = jnp.zeros((ROWS, left_ref.shape[1]), F32)
    chunk = left_ref.shape[2]
    for n in range(left_ref.shape[0]):
        pre = pre + lax.dot_general(
            mixed_rows[:, n * chunk : (n + 1) * chunk], left_ref[n], (((1,), (1,)), ((), ())), preferred_element_type=F32
        )
    lora = jnp.tanh(pre).astype(BF16)
    decay = jnp.exp(-jnp.exp(row_of(small_ref[0:2, :]) + dot(lora, right_ref[...])))
    row256, col256 = iota((LOCAL, LOCAL), 0), iota((LOCAL, LOCAL), 1)
    same_head = (row256 // HEAD == col256 // HEAD).astype(BF16)
    reorder = reorder_matrix()
    rkv = []
    for n in range(3):
        loads[5 + n].wait()
        rkv.append(dot(mix(n), bufs[5 + n][...]))
    r = [cut(rkv[0], t) for t in range(STEPS)]
    k = [cut(rkv[1], t) for t in range(STEPS)]
    v = [cut(rkv[2], t) for t in range(STEPS)]
    d = [jnp.where(tally > t, cut(decay, t), 1.0) for t in range(STEPS)]
    kept = [jnp.where(tally > t, k[t], 0.0) for t in range(STEPS)]
    boost = row_of(small_ref[2:4, :])

    run, reach = jnp.ones_like(r[0]), []
    for t in range(STEPS):
        reach.append(r[t] * run)
        run = run * d[t]
    tail, coefs = None, [None] * STEPS
    for t in reversed(range(STEPS)):
        coefs[t] = kept[t] if tail is None else kept[t] * tail
        tail = d[t] if tail is None else tail * d[t]
    pairs, terms = [], []
    for t in range(STEPS):
        pairs.append((t, t))
        terms.append(r[t] * boost * k[t])
        weight = r[t]
        for s in reversed(range(t)):
            pairs.append((t, s))
            terms.append(weight * kept[s])
            weight = weight * d[s]
    sums = dot_split(jnp.concatenate(terms, axis=0), same_head)
    within = [None] * STEPS
    for n, (t, s) in enumerate(pairs):
        term = cut(sums, n) * v[s]
        within[t] = term if within[t] is None else within[t] + term

    moved = dot(jnp.concatenate(reach, axis=0).astype(BF16), reorder)
    moved_ref[...] = jnp.concatenate(coefs + [run], axis=0)
    vals_ref[...] = rkv[2]

    lane = iota((SLOTS, 128), 1)
    for h in range(HEADS):
        head_lane = lane % HEADS == h
        for p in range(2):
            for t in range(STEPS):
                at = pl.ds(t * 8 + p * HEADS + h, SLOTS, stride=READ_STRIDE)
                reads[at, :] = jnp.where(head_lane, cut(moved, t)[:, p * 128 : (p + 1) * 128], 0.0)
    state_load.wait()
    place_received(meta_ref, (from_before, from_after), state)
    for q in range(SLOTS):
        rows = slice(q * READ_STRIDE, q * READ_STRIDE + STEPS * 8)
        now = state_of(meta_ref, state, q)
        heads[rows, :] = dot(reads[rows, :].astype(BF16), now.astype(BF16))

    outs = []
    left_half = lane < HEAD
    for t in range(STEPS):
        def read(p, h):
            return heads[pl.ds(t * 8 + p * HEADS + h, SLOTS, stride=READ_STRIDE), :]

        cols = []
        for h in range(0, HEADS, 2):
            a, b, c, e = read(0, h), read(1, h), read(0, h + 1), read(1, h + 1)
            cols.append(jnp.where(left_half, a, e) + pltpu.roll(jnp.where(left_half, c, b), HEAD, 1))
        outs.append(jnp.concatenate(cols, axis=1) + within[t])
    y = jnp.concatenate(outs, axis=0)
    center = y - dot_split(y, same_head) * (1.0 / HEAD)
    spread = dot_split(center * center, same_head) * (1.0 / HEAD)
    g = center * lax.rsqrt(spread + EPS) * row_of(small_ref[4:6, :])
    for t in range(STEPS):
        for c in range(LOCAL // 128):
            ordered[c, pl.ds(t, SLOTS, stride=STEPS), :] = cut(g, t)[:, c * 128 : (c + 1) * 128]
    g = jnp.concatenate([ordered[c] for c in range(LOCAL // 128)], axis=1).astype(BF16)
    loads[11].wait()
    proj = dot(g, final_ref[...])
    for q in range(SLOTS):
        rows = proj[q * STEPS : (q + 1) * STEPS, :]
        for c in range(0, TILES, 2):
            at = (q * TILES + c) * STEPS
            part[at : at + 2 * STEPS, :] = jnp.concatenate(
                [rows[:, c * 128 : (c + 1) * 128], rows[:, (c + 1) * 128 : (c + 2) * 128]], axis=0
            )
    part_ref[...] = part[...].astype(BF16)


def update_kernel(meta_ref, mem_hbm, *refs):
    count = 4
    hbm, new_hbm, bufs = refs[:count], refs[count], refs[count + 1 : 2 * count + 1]
    state, keys, vals, decays, fresh, sems, state_sem, new_sems = refs[2 * count + 1 :]
    loads = copies(hbm, bufs, sems)
    start(loads)
    state_load = pltpu.make_async_copy(mem_hbm, state, state_sem)
    state_load.start()
    moved_ref, vals_ref, from_after, from_before = bufs
    loads[0].wait()
    loads[1].wait()
    moved = dot_split(moved_ref[...], reorder_matrix())
    rowd, cold = iota((LOCAL, HEADS * 128), 0), iota((LOCAL, HEADS * 128), 1)
    double = (rowd == (cold // 128) * HEAD + cold % HEAD).astype(BF16)
    doubled = dot(vals_ref[...].astype(BF16), double)
    lane = iota((SLOTS, 128), 1)
    for h in range(HEADS):
        head_lane = lane % HEADS == h
        for p in range(2):
            half = lane // HEAD == p
            cols = slice(p * 128, (p + 1) * 128)
            for t in range(STEPS):
                at = pl.ds(t * 8 + p * HEADS + h, SLOTS, stride=STEPS * 8)
                keys[at, :] = jnp.where(head_lane, cut(moved, t)[:, cols], 0.0)
                vals[at, :] = jnp.where(half, cut(doubled, t)[:, h * 128 : (h + 1) * 128], 0.0)
            whole = jnp.where(head_lane, cut(moved, STEPS)[:, cols], 0.0)
            high = whole.astype(BF16).astype(F32)
            decays[pl.ds(p * HEADS + h, SLOTS, stride=16), :] = high
            decays[pl.ds(8 + p * HEADS + h, SLOTS, stride=16), :] = whole - high
    ones = ((iota((16, 128), 0) // HEADS) % 2 == iota((16, 128), 1) // HEAD).astype(BF16)
    for copy in loads[2:] + [state_load]:
        copy.wait()
    place_received(meta_ref, (from_before, from_after), state)
    news = []
    for q in range(SLOTS):
        here = slice(q * STATE_ROWS, (q + 1) * STATE_ROWS)
        rows = slice(q * STEPS * 8, (q + 1) * STEPS * 8)
        fade = dot_rows(decays[q * 16 : (q + 1) * 16, :].astype(BF16), ones)
        grown = dot_rows(keys[rows, :].astype(BF16), vals[rows, :].astype(BF16))
        fresh[here, :] = fade * state_of(meta_ref, state, q) + grown
        news.append(pltpu.make_async_copy(fresh.at[here, :], new_hbm.at[here, :], new_sems.at[q]))
        news[-1].start()
    for copy in news:
        copy.wait()


def cost(flops, bytes_accessed):
    return pl.CostEstimate(flops=flops, bytes_accessed=bytes_accessed, transcendentals=0)


def tiles_view(a):
    lead, mid, width = a.shape
    return a.reshape(lead, mid, width // 128, 128).transpose(0, 2, 1, 3).reshape(lead * width // 128 * mid, 128)


def tiles_back(a, lead, mid, width):
    return a.reshape(lead, width // 128, mid, 128).transpose(0, 2, 1, 3).reshape(lead, mid, width)


def shards(
    layer_entry_vectors,
    tally_of_tokens,
    prior_slot_lookup,
    memory_matrices,
    previous_standardized_entries,
    entry_standardize_scale,
    blend_coefficients,
    acceptance_projection_matrix,
    lookup_projection_matrix,
    payload_projection_matrix,
    forget_map_left_matrix,
    forget_map_right_matrix,
    feature_forget_logloglevel,
    present_token_boost,
    team_standardize_scale,
    final_projection_matrix,
):
    rings = lax.axis_size("seq")
    teams = lax.axis_size("tensor")
    core = lax.axis_index("tensor") % 2
    x = tiles_view(layer_entry_vectors)
    mem = tiles_view(memory_matrices)
    prev = previous_standardized_entries
    lookup, tally = prior_slot_lookup, tally_of_tokens
    left_t = forget_map_left_matrix.T
    shape, scratch, dma = jax.ShapeDtypeStruct, pltpu.VMEM, pltpu.SemaphoreType.DMA
    params = lambda mib: pltpu.CompilerParams(vmem_limit_bytes=mib << 20)
    like = lambda items: [scratch(a.shape, a.dtype) for a in items]
    state_buf = scratch((SLOTS * STATE_ROWS, 128), F32)
    rows_buf = scratch((SLOTS * STEPS * 8, 128), F32)
    read_buf = scratch((SLOTS * READ_STRIDE, 128), F32)

    packed, left, meta = pl.pallas_call(
        pack_kernel,
        out_shape=[
            shape((PACK_ROWS, 128), BF16), shape((teams,) + left_t.shape, BF16), shape((META,), jnp.int32),
        ],
        in_specs=spec(pl.ANY, 5),
        out_specs=spec(pltpu.VMEM, 1) + spec(pl.ANY, 1) + spec(pltpu.SMEM, 1),
        scratch_shapes=[pltpu.SMEM(lookup.shape, jnp.int32)] * 2
        + like([prev, mem, left_t])
        + [scratch((2 * TILES, 128), F32), dma((5 + teams,))],
        compiler_params=params(PACK_MIB),
        cost_estimate=cost(0, 1 << 20),
        name="pack",
    )(lookup, tally, prev, mem, left_t)
    from_after = lax.ppermute(packed, "seq", [((i + 1) % rings, i) for i in range(rings)])
    from_before = lax.ppermute(packed, "seq", [(i, (i + 1) % rings) for i in range(rings)])
    left = lax.all_to_all(left, "tensor", 0, 0)

    gain = entry_standardize_scale.reshape(TILES, 128)
    vectors = [
        v.reshape(2, 128) for v in (feature_forget_logloglevel, present_token_boost, team_standardize_scale)
    ]
    xn, new_shifts, small = pl.pallas_call(
        norm_kernel,
        out_shape=[shape((ROWS, WIDTH), F32), shape((SLOTS, WIDTH), F32), shape((8, 128), F32)],
        in_specs=spec(pltpu.SMEM, 1) + spec(pl.ANY, 5),
        out_specs=spec(pltpu.VMEM, 3),
        scratch_shapes=like([x, gain] + vectors) + [scratch((ROWS * TILES, 128), F32), dma((5,))],
        compiler_params=params(MAIN_MIB),
        cost_estimate=cost(0, 4 << 20),
        name="norm",
    )(meta, x, gain, *vectors)

    operands = [
        xn, prev, from_after, from_before, blend_coefficients,
        acceptance_projection_matrix, lookup_projection_matrix, payload_projection_matrix,
        left, forget_map_right_matrix, small, final_projection_matrix,
    ]
    part, moved, values = pl.pallas_call(
        main_kernel,
        out_shape=[
            shape((ROWS * TILES, 128), BF16), shape((ROWS + SLOTS, LOCAL), F32), shape((ROWS, LOCAL), F32),
        ],
        in_specs=spec(pltpu.SMEM, 1) + spec(pl.ANY, 1 + len(operands)),
        out_specs=spec(pltpu.VMEM, 3),
        scratch_shapes=like(operands)
        + [scratch((SLOTS, WIDTH), F32), state_buf, read_buf, read_buf, scratch((ROWS * TILES, 128), F32)]
        + [scratch((LOCAL // 128, ROWS, 128), F32), dma((len(operands),)), dma],
        compiler_params=params(MAIN_MIB),
        cost_estimate=cost(8 * ROWS * WIDTH * LOCAL, 8 << 20),
        name="main",
    )(meta, mem, *operands)

    operands = [moved, values, from_after, from_before]
    new_states = pl.pallas_call(
        update_kernel,
        out_shape=shape((SLOTS * STATE_ROWS, 128), F32),
        in_specs=spec(pltpu.SMEM, 1) + spec(pl.ANY, 1 + len(operands)),
        out_specs=spec(pl.ANY, 1)[0],
        scratch_shapes=like(operands)
        + [state_buf, rows_buf, rows_buf, scratch((SLOTS * 16, 128), F32), state_buf]
        + [dma((len(operands),)), dma, dma((SLOTS,))],
        compiler_params=params(MAIN_MIB),
        cost_estimate=cost(1 << 24, 8 << 20),
        name="update",
    )(meta, mem, *operands)

    pairs = [[2 * i, 2 * i + 1] for i in range(teams // 2)]
    chips = [[2 * i + c for i in range(teams // 2)] for c in range(2)]
    half = ROWS * TILES // 2
    both = lax.all_gather(part, "tensor", axis_index_groups=pairs, tiled=False)
    mine = lax.dynamic_slice_in_dim(both, core * half, half, 1).astype(F32).sum(0).astype(BF16)
    spread = lax.all_to_all(
        jnp.broadcast_to(mine[None], (teams // 2,) + mine.shape), "tensor", 0, 0, axis_index_groups=chips
    )
    mine_rows = SLOTS // 2
    residual = lax.dynamic_slice_in_dim(layer_entry_vectors, core * mine_rows, mine_rows, 0).astype(F32)
    counts = lax.dynamic_slice_in_dim(tally, core * mine_rows, mine_rows, 0)
    valid = counts[:, None, None] > jnp.arange(STEPS, dtype=jnp.int32)[None, :, None]
    total = residual + tiles_back(spread.astype(F32).sum(0), mine_rows, STEPS, WIDTH)
    mixed = jnp.where(valid, total, 0.0).astype(BF16)
    mixed = lax.all_gather(mixed, "tensor", axis_index_groups=pairs, tiled=True)
    return (
        mixed,
        tiles_back(new_states, SLOTS, HEADS, HEAD * HEAD),
        new_shifts,
    )


def solution(mesh):
    in_specs = (
        P("seq", None, None),
        P("seq"),
        P("seq"),
        P("seq", "tensor", None),
        P("seq", None),
        P(),
        P(),
        P(None, "tensor"),
        P(None, "tensor"),
        P(None, "tensor"),
        P("tensor", None),
        P(None, "tensor"),
        P("tensor"),
        P("tensor"),
        P("tensor"),
        P("tensor", None),
    )
    out_specs = (P("seq", None, None), P("seq", "tensor", None), P("seq", None))
    return jax.shard_map(shards, mesh=mesh, in_specs=in_specs, out_specs=out_specs, check_vma=False)
```
